32 devices in a mesh: dp: 8 (over z, x), mp: 4 (over y, core).
Axes of the slice: x: 2, y: 2, z: 4, core: 2. Of those that a mesh axis runs over, the one named last changes fastest.
Arguments:
- tokens: bfloat16 [32, 512, 768], P('dp', 'mp'), may hold values from -6 to 6
- coeffs: bfloat16 [32, 256, 768], P('dp', 'mp'), may hold values from -6 to 6
- present_flag: int32 [32], P('dp'), may hold values 0 or 1
- sticky_pos: int32 [32, 256], P('dp'), may hold values from 0 to 511
- gain_one: bfloat16 [768], replicated, may hold values from 0.5 to 1.5
- w_query: bfloat16 [768, 768], P('dp', 'mp'), may hold values from -0.21875 to 0.21875
- w_key: bfloat16 [768, 768], P('dp', 'mp'), may hold values from -0.21875 to 0.21875
- w_value: bfloat16 [768, 768], P('dp', 'mp'), may hold values from -0.21875 to 0.21875
- w_out: bfloat16 [768, 768], P('mp', 'dp'), may hold values from -0.875 to 0.875
- mu_weight: bfloat16 [12, 256], P('mp'), may hold values from -0.375 to 0.375
- sigma_weight: bfloat16 [12, 256], P('mp'), may hold values from -0.375 to 0.375
- gain_two: bfloat16 [768], replicated, may hold values from 0.5 to 1.5
- w_up: bfloat16 [768, 3072], P('dp', 'mp'), may hold values from -0.21875 to 0.21875
- w_down: bfloat16 [3072, 768], P('mp', 'dp'), may hold values from -0.109375 to 0.109375
- cotangent: bfloat16 [32, 256, 768], P('dp', 'mp'), may hold values from -6 to 6
Outputs:
- output: bfloat16 [32, 256, 768], P('dp', 'mp')
- token_grad: float32 [32, 512, 768], P('dp', 'mp')
- coeff_grad: float32 [32, 256, 768], P('dp', 'mp')
- gain_one_grad: float32 [768], replicated
- w_query_grad: float32 [768, 768], P('dp', 'mp')
- w_key_grad: float32 [768, 768], P('dp', 'mp')
- w_value_grad: float32 [768, 768], P('dp', 'mp')
- w_out_grad: float32 [768, 768], P('mp', 'dp')
- mu_weight_grad: float32 [12, 256], P('mp')
- sigma_weight_grad: float32 [12, 256], P('mp')
- gain_two_grad: float32 [768], replicated
- w_up_grad: float32 [768, 3072], P('dp', 'mp')
- w_down_grad: float32 [3072, 768], P('mp', 'dp')
The draws below stay inside these ranges and needn't reach their ends.
All inputs are finite; a program needn't handle non-finite values. No bound on the sum of `present_flag` on one device may be relied on, other than what follows from the above.
Results may differ from the reference program's by a relative error of at most 0.019.
The reference program's roundings to bfloat16 on the way count: a program that leaves them out, or rounds other values in their place, can miss the bound.
Values may be sent and summed in bfloat16 or wider, within the bound.
A program may use at most 192 MiB of HBM per device.

```python
import math
import jax
import jax.numpy as jnp
from jax import lax

D = 768
H = 12
HD = 64
FF = 3072
NB = 256
SEGMENT_TOKENS = 256
LEN = 512
SEQS = 32


def set_ends(drawn, key, smallest, largest):
    longest = drawn.shape.index(max(drawn.shape))
    spots = []
    for shift in (0, 1):
        where = [jax.random.randint(jax.random.fold_in(key, axis), (), 0, length) for axis, length in enumerate(drawn.shape)]
        where[longest] = (where[longest] + shift) % drawn.shape[longest]
        spots.append(tuple(where))
    return drawn.at[spots[0]].set(smallest).at[spots[1]].set(largest)


def block_scale(own_key, shape, shards, low, high):
    def one(position, blocks):
        heights = jax.random.uniform(jax.random.fold_in(jax.random.fold_in(own_key, 6), position), (blocks,), jnp.float32, low / len(shards), high / len(shards))
        return jnp.repeat(jnp.exp(heights), shape[position] // blocks).reshape((-1,) + (1,) * (len(shape) - position - 1))

    loudness = one(*shards[0])
    for cut in shards[1:]:
        loudness = loudness * one(*cut)
    return loudness


def centred(key, dims, scale, bound, shards=(), kind=jnp.bfloat16):
    values = jax.random.normal(key, dims, jnp.float32) * scale
    if len(shards) > 0:
        values = block_scale(key, dims, shards, -0.22, 0.18) * values
    return jnp.clip(values, min=-bound, max=bound).astype(kind)


def setup_inputs(seed: int = 0) -> dict:
    seeds = jax.random.split(jax.random.key(seed), 16)
    tokens = centred(seeds[0], (SEQS, LEN, D), 1.0, 6.0, ((0, 8), (1, 4)))
    coeffs = centred(seeds[1], (SEQS, NB, D), 1.0, 6.0, ((0, 8), (1, 4)))
    present_flag = set_ends((jax.random.randint(seeds[2], (SEQS,), 0, 2) < 1).astype(jnp.int32), jax.random.fold_in(seeds[2], 1), 0, 1)
    sticky_pos = set_ends(jax.random.randint(seeds[3], (SEQS, SEGMENT_TOKENS), 0, 2 * SEGMENT_TOKENS), jax.random.fold_in(seeds[3], 1), 0, (2 * SEGMENT_TOKENS) - 1).astype(jnp.int32)
    gain_one = jnp.clip(1.0 + 0.1 * jax.random.normal(seeds[4], (D,), jnp.float32), 0.5, 1.5).astype(jnp.bfloat16)
    w_query = centred(seeds[5], (D, D), D ** -0.5, 0.21875, ((0, 8), (1, 4)))
    w_key = centred(seeds[6], (D, D), D ** -0.5, 0.21875, ((0, 8), (1, 4)))
    w_value = centred(seeds[7], (D, D), D ** -0.5, 0.21875, ((0, 8), (1, 4)))
    w_out = centred(seeds[8], (D, D), (D // 16) ** -0.5, 0.875, ((0, 4), (1, 8)))
    mu_weight = centred(seeds[9], (H, NB), NB ** -0.5, 0.375, ((0, 4),))
    sigma_weight = centred(seeds[10], (H, NB), NB ** -0.5, 0.375, ((0, 4),))
    gain_two = jnp.clip(1.0 + 0.1 * jax.random.normal(seeds[11], (D,), jnp.float32), 0.5, 1.5).astype(jnp.bfloat16)
    w_up = centred(seeds[12], (D, FF), D ** -0.5, 0.21875, ((0, 8), (1, 4)))
    w_down = centred(seeds[13], (FF, D), FF ** -0.5, 0.109375, ((0, 4), (1, 8)))
    cotangent = centred(seeds[14], (SEQS, SEGMENT_TOKENS, D), 1.0, 6.0, ((0, 8), (1, 4)))
    return {"tokens": tokens, "coeffs": coeffs, "present_flag": present_flag, "sticky_pos": sticky_pos, "gain_one": gain_one, "w_query": w_query, "w_key": w_key, "w_value": w_value, "w_out": w_out, "mu_weight": mu_weight, "sigma_weight": sigma_weight, "gain_two": gain_two, "w_up": w_up, "w_down": w_down, "cotangent": cotangent}


highest = lax.Precision.HIGHEST
epsilon = 1e-05
ridge = 0.5
spread_scale = 1.0 / 64.0
gelu_coef = 0.7978845608028654

@jax.custom_vjp
def low(v):
    return lax.optimization_barrier(v.astype(jnp.bfloat16)).astype(jnp.float32)

@jax.custom_vjp
def low_back(v):
    return v

def low_keep(v):
    return (low(v), None)

def low_pass(kept, grad):
    return (grad,)

def back_keep(v):
    return (v, None)

def back_low(kept, grad):
    return (low(grad),)
low.defvjp(low_keep, low_pass)
low_back.defvjp(back_keep, back_low)

def basis_tables(basis_count, seg_len):
    centers = (jnp.arange(basis_count, dtype=jnp.float32) + 0.5) / basis_count
    rbf_width = 1.0 / basis_count
    sample_times = (jnp.arange(2 * seg_len, dtype=jnp.float32) + 0.5) / (2 * seg_len)
    design = jnp.exp(-(sample_times[:, None] - centers[None, :]) ** 2 / (2.0 * rbf_width * rbf_width))
    normal = jnp.dot(design.T, design, precision=highest) + ridge * jnp.eye(basis_count, dtype=jnp.float32)
    factor = jnp.linalg.cholesky(normal)
    fitting = jax.scipy.linalg.cho_solve((factor, True), design.T)
    return (centers, fitting)

def sticky_map(positions, centers, fitting):
    rbf_width = 1.0 / NB
    old_spots = (positions.astype(jnp.float32) + 0.5) / (2 * SEGMENT_TOKENS)
    samples = jnp.exp(-(old_spots[:, None] - centers[None, :]) ** 2 / (2.0 * rbf_width * rbf_width))
    return jnp.dot(fitting[:, :SEGMENT_TOKENS], samples, precision=highest)

def layer_norm(values, gain_vec):
    centered = values - lax.optimization_barrier(jnp.mean(values, axis=-1, keepdims=True))
    inverse = lax.rsqrt(lax.optimization_barrier(jnp.mean(centered * centered, axis=-1, keepdims=True)) + epsilon)
    return centered * inverse * gain_vec

def gelu_tanh(values):
    return 0.5 * values * (1.0 + jnp.tanh(gelu_coef * (values + 0.044715 * values * values * values)))

def memory_reach(mem_scores, mu_in, sigma_in, centers):
    rbf_width = 1.0 / centers.shape[0]
    mu_logit = jnp.einsum('...hn,hn->...h', mem_scores, mu_in, precision=highest)
    sigma_logit = jnp.einsum('...hn,hn->...h', mem_scores, sigma_in, precision=highest)
    mean_pos = jax.nn.sigmoid(mu_logit)
    spread = jax.nn.softplus(sigma_logit) * spread_scale + rbf_width * rbf_width
    distance = mean_pos[..., None] - centers
    return rbf_width * lax.rsqrt(spread)[..., None] * jnp.exp(-distance * distance / (2.0 * spread[..., None]))

def matmul_high(left_in, right_in):
    return jnp.dot(left_in, right_in, precision=highest)

def forward(token_rows, coef_rows, params, present, sticky_fit, past_fit, centers):
    gain_one, w_query, w_key, w_value, w_out, mu_weight, sigma_weight, gain_two, w_up, w_down = params
    head_root = math.sqrt(HD)
    normed = low(layer_norm(token_rows, gain_one))
    query_rows = low(low_back(matmul_high(normed[SEGMENT_TOKENS:], w_query)))
    key_rows = low(low_back(matmul_high(normed, w_key)))
    value_rows = low(low_back(matmul_high(normed, w_value)))
    coef_key = low(low_back(present * matmul_high(coef_rows, w_key)))
    coef_value = low(low_back(present * matmul_high(coef_rows, w_value)))
    mem_key = low(low_back(matmul_high(sticky_fit, coef_key) + matmul_high(past_fit, key_rows[:SEGMENT_TOKENS])))
    mem_value = low(low_back(matmul_high(sticky_fit, coef_value) + matmul_high(past_fit, value_rows[:SEGMENT_TOKENS])))
    query_heads = query_rows.reshape(SEGMENT_TOKENS, H, HD)
    key_heads = key_rows.reshape(2 * SEGMENT_TOKENS, H, HD)
    value_heads = value_rows.reshape(2 * SEGMENT_TOKENS, H, HD)
    mem_key_heads = mem_key.reshape(NB, H, HD)
    mem_value_heads = mem_value.reshape(NB, H, HD)
    raw_scores = low_back(jnp.einsum('qhd,khd->hqk', query_heads, key_heads, precision=highest) / head_root)
    causal = jnp.arange(2 * SEGMENT_TOKENS)[None, :] <= (SEGMENT_TOKENS + jnp.arange(SEGMENT_TOKENS))[:, None]
    attn_probs = jax.nn.softmax(jnp.where(causal, raw_scores, -1e+30), axis=-1)
    short = jnp.einsum('hqk,khd->qhd', low(attn_probs), value_heads, precision=highest)
    mem_scores = low_back(jnp.einsum('qhd,nhd->qhn', query_heads, mem_key_heads, precision=highest) / head_root)
    reach_rows = memory_reach(mem_scores, mu_weight, sigma_weight, centers)
    long_part = jnp.einsum('qhn,nhd->qhd', low(reach_rows), mem_value_heads, precision=highest)
    context_vectors = low(low_back((short + long_part).reshape(SEGMENT_TOKENS, D)))
    hidden = token_rows[SEGMENT_TOKENS:] + low_back(matmul_high(context_vectors, w_out))
    second_normed = low(layer_norm(hidden, gain_two))
    up_preactivation = low_back(matmul_high(second_normed, w_up))
    active_values = low(gelu_tanh(up_preactivation))
    return hidden + matmul_high(active_values, w_down)

def reference(tokens, coeffs, present_flag, sticky_pos, gain_one, w_query, w_key, w_value, w_out, mu_weight, sigma_weight, gain_two, w_up, w_down, cotangent):
    centers, fitting = basis_tables(NB, SEGMENT_TOKENS)
    past_fit = low(fitting[:, SEGMENT_TOKENS:])
    weights = tuple((array_in.astype(jnp.float32) for array_in in (gain_one, w_query, w_key, w_value, w_out, mu_weight, sigma_weight, gain_two, w_up, w_down)))

    def sequence_step(totals, seq_batch):
        seq_tokens, seq_coeffs, seq_flag, seq_pos, seq_cot = seq_batch
        sticky_fit = low(sticky_map(seq_pos, centers, fitting))
        present = seq_flag.astype(jnp.float32)

        def run_layer(tok_rows, coef_rows, params):
            return forward(tok_rows, coef_rows, params, present, sticky_fit, past_fit, centers)
        result, pullback = jax.vjp(run_layer, seq_tokens.astype(jnp.float32), seq_coeffs.astype(jnp.float32), weights)
        tok_grad, coef_grad, param_grads = pullback(seq_cot.astype(jnp.float32))
        totals = tuple((running + adding for running, adding in zip(totals, param_grads)))
        return (totals, (result.astype(jnp.bfloat16), tok_grad, coef_grad))
    zero_grads = tuple((jnp.zeros_like(array_in) for array_in in weights))
    totals, outs_all = lax.scan(sequence_step, zero_grads, (tokens, coeffs, present_flag, sticky_pos, cotangent))
    output, token_grad, coeff_grad = outs_all
    return (output, token_grad, coeff_grad, totals[0], totals[1], totals[2], totals[3], totals[4], totals[5], totals[6], totals[7], totals[8], totals[9])
```

```python
import math

import jax
import jax.numpy as jnp
import numpy as np
from jax import lax
from jax.sharding import PartitionSpec as P

HD = 64
NB = 256
SEGMENT_TOKENS = 256
BOTH = ("dp", "mp")

highest = lax.Precision.HIGHEST
epsilon = 1e-05
ridge = 0.5
spread_scale = 1.0 / 64.0
gelu_coef = 0.7978845608028654


def basis_tables(basis_count, seg_len):
    centers = (np.arange(basis_count) + 0.5) / basis_count
    width = 1.0 / basis_count
    times = (np.arange(2 * seg_len) + 0.5) / (2 * seg_len)
    design = np.exp(-((times[:, None] - centers[None, :]) ** 2) / (2.0 * width * width))
    normal = design.T @ design + ridge * np.eye(basis_count)
    fitting = np.linalg.solve(normal, design.T)
    return centers.astype(np.float32), fitting.astype(np.float32)


def norm_rows(values):
    centered = values - jnp.mean(values, axis=-1, keepdims=True)
    inverse = lax.rsqrt(jnp.mean(centered * centered, axis=-1, keepdims=True) + epsilon)
    return (centered * inverse, inverse)


def gelu_tanh(values):
    return (
        0.5 * values * (1.0 + jnp.tanh(gelu_coef * (values + 0.044715 * values * values * values)))
    )


def memory_reach(mem_scores, mu_in, sigma_in, centers):
    rbf_width = 1.0 / centers.shape[0]
    mu_logit = jnp.einsum("...hn,hn->...h", mem_scores, mu_in, precision=highest)
    sigma_logit = jnp.einsum("...hn,hn->...h", mem_scores, sigma_in, precision=highest)
    mean_pos = jax.nn.sigmoid(mu_logit)
    spread = jax.nn.softplus(sigma_logit) * spread_scale + rbf_width * rbf_width
    distance = mean_pos[..., None] - centers
    return (
        rbf_width
        * lax.rsqrt(spread)[..., None]
        * jnp.exp(-distance * distance / (2.0 * spread[..., None]))
    )


def mm(pattern, left_in, right_in):
    return jnp.einsum(pattern, left_in, right_in, preferred_element_type=jnp.float32)


def norm_back(grad, flat_rows, inverse, gain_vec):
    scaled = grad * gain_vec
    return inverse * (
        scaled
        - jnp.mean(scaled, axis=-1, keepdims=True)
        - flat_rows * jnp.mean(scaled * flat_rows, axis=-1, keepdims=True)
    )


def low(v):
    return v.astype(jnp.bfloat16)


def whole_sequences(
    tokens, coeffs, present_flag, sticky_pos, gain_one, wq, wk, wv, wo, mu, sigma, gain_two, wu, wdt, cot
):
    count, length, width = tokens.shape
    cur = cot.shape[1]
    past = length - cur
    heads = width // HD
    root = math.sqrt(HD)
    centers, fitting = basis_tables(NB, SEGMENT_TOKENS)
    rbf_width = 1.0 / NB
    past_fit = jnp.asarray(fitting[:, SEGMENT_TOKENS:]).astype(jnp.bfloat16)
    centers = jnp.asarray(centers)
    g1 = gain_one.astype(jnp.float32)
    g2 = gain_two.astype(jnp.float32)
    mu = mu.astype(jnp.float32)
    sigma = sigma.astype(jnp.float32)
    causal = jnp.arange(length)[None, :] <= (past + jnp.arange(cur))[:, None]
    present = present_flag.astype(jnp.float32)[:, None, None]
    spots = (sticky_pos.astype(jnp.float32) + 0.5) / (2 * SEGMENT_TOKENS)
    samples = jnp.exp(-((spots[:, :, None] - centers) ** 2) / (2.0 * rbf_width * rbf_width))
    sticky = low(
        jnp.einsum("nm,bmk->bnk", jnp.asarray(fitting[:, :SEGMENT_TOKENS]), samples, precision=highest)
    )
    rows = tokens.astype(jnp.float32)
    flat_one, inv_one = norm_rows(rows)
    normed = low(flat_one * g1)
    q = low(mm("bld,de->ble", normed[:, past:], wq))
    k = low(mm("bld,de->ble", normed, wk))
    v = low(mm("bld,de->ble", normed, wv))
    ck = low(present * mm("bnd,de->bne", coeffs, wk))
    cv = low(present * mm("bnd,de->bne", coeffs, wv))
    mk = low(mm("bnm,bme->bne", sticky, ck) + mm("np,bpe->bne", past_fit, k[:, :past]))
    mv = low(mm("bnm,bme->bne", sticky, cv) + mm("np,bpe->bne", past_fit, v[:, :past]))
    qh = q.reshape(count, cur, heads, HD)
    kh = k.reshape(count, length, heads, HD)
    vh = v.reshape(count, length, heads, HD)
    mkh = mk.reshape(count, NB, heads, HD)
    mvh = mv.reshape(count, NB, heads, HD)
    scores = mm("bqhd,bkhd->bhqk", qh, kh) / root
    masked = jnp.where(causal, scores, -1e30)
    probs = jax.nn.softmax(masked, axis=-1)
    probs_low = low(probs)
    short = mm("bhqk,bkhd->bqhd", probs_low, vh)
    mem_scores = mm("bqhd,bnhd->bqhn", qh, mkh) / root

    def reach_of(s, m, g):
        return memory_reach(s, m, g, centers)

    reach, reach_pull = jax.vjp(reach_of, mem_scores, mu, sigma)
    reach_low = low(reach)
    long_part = mm("bqhn,bnhd->bqhd", reach_low, mvh)
    context = low((short + long_part).reshape(count, cur, width))
    hidden = rows[:, past:] + mm("bqd,de->bqe", context, wo)
    flat_two, inv_two = norm_rows(hidden)
    normed_two = low(flat_two * g2)
    up = mm("bqd,df->bqf", normed_two, wu)
    active_rows, gelu_pull = jax.vjp(gelu_tanh, up)
    active = low(active_rows)
    output = low(hidden + mm("bqf,df->bqd", active, wdt))
    wdt_grad = mm("bqd,bqf->df", cot, active)
    d_up = low(gelu_pull(mm("bqd,df->bqf", cot, wdt))[0])
    wu_grad = mm("bqd,bqf->df", normed_two, d_up)
    d_n2 = mm("bqf,df->bqd", d_up, wu)
    g2_grad = jnp.sum(d_n2 * flat_two, axis=(0, 1))
    d_hidden = cot.astype(jnp.float32) + norm_back(d_n2, flat_two, inv_two, g2)
    d_hidden_low = low(d_hidden)
    wo_grad = mm("bqd,bqe->de", context, d_hidden_low)
    d_context = low(mm("bqe,de->bqd", d_hidden_low, wo)).reshape(count, cur, heads, HD)
    d_probs = mm("bqhd,bkhd->bhqk", d_context, vh)
    d_scores = low(probs * (d_probs - jnp.sum(probs * d_probs, axis=-1, keepdims=True)))
    d_reach = mm("bqhd,bnhd->bqhn", d_context, mvh)
    d_mv = low(mm("bqhn,bqhd->bnhd", reach_low, d_context)).reshape(count, NB, width)
    d_ms, mu_grad, sigma_grad = reach_pull(d_reach)
    d_ms = low(d_ms)
    dq = low(
        (mm("bhqk,bkhd->bqhd", d_scores, kh) + mm("bqhn,bnhd->bqhd", d_ms, mkh)) / root
    ).reshape(count, cur, width)
    d_mk = low(mm("bqhn,bqhd->bnhd", d_ms, qh) / root).reshape(count, NB, width)
    keep = present_flag.astype(jnp.bfloat16)[:, None, None]
    d_ck = low(mm("bnm,bne->bme", sticky, d_mk)) * keep
    d_cv = low(mm("bnm,bne->bme", sticky, d_mv)) * keep
    dk = (mm("bhqk,bqhd->bkhd", d_scores, qh) / root).reshape(count, length, width)
    dv = mm("bhqk,bqhd->bkhd", probs_low, d_context).reshape(count, length, width)
    pad = ((0, 0), (0, cur), (0, 0))
    dk = low(dk + jnp.pad(mm("np,bne->bpe", past_fit, d_mk), pad))
    dv = low(dv + jnp.pad(mm("np,bne->bpe", past_fit, d_mv), pad))
    wq_grad = mm("bqd,bqe->de", normed[:, past:], dq)
    wk_grad = mm("bld,ble->de", normed, dk) + mm("bnd,bne->de", coeffs, d_ck)
    wv_grad = mm("bld,ble->de", normed, dv) + mm("bnd,bne->de", coeffs, d_cv)
    d_n1 = mm("ble,de->bld", dk, wk) + mm("ble,de->bld", dv, wv)
    d_n1 = d_n1 + jnp.pad(mm("bqe,de->bqd", dq, wq), ((0, 0), (past, 0), (0, 0)))
    coeff_grad = mm("bne,de->bnd", d_ck, wk) + mm("bne,de->bnd", d_cv, wv)
    g1_grad = jnp.sum(d_n1 * flat_one, axis=(0, 1))
    token_grad = norm_back(d_n1, flat_one, inv_one, g1) + jnp.pad(
        d_hidden, ((0, 0), (past, 0), (0, 0))
    )
    return (
        output, token_grad, coeff_grad, g1_grad, wq_grad, wk_grad, wv_grad, wo_grad,
        mu_grad, sigma_grad, g2_grad, wu_grad, wdt_grad,
    )


def to_sequences(rows):
    return lax.all_to_all(rows, "mp", 0, 1, tiled=True)


def to_rows(rows):
    return lax.all_to_all(rows, "mp", 1, 0, tiled=True)


def body(
    tokens, coeffs, present_flag, sticky_pos, gain_one, w_query, w_key, w_value, w_out, mu_weight,
    sigma_weight, gain_two, w_up, w_down, cotangent,
):
    dp, mp = lax.axis_size("dp"), lax.axis_size("mp")
    me = lax.axis_index("mp")
    count = tokens.shape[0] // mp
    depth, share = w_query.shape
    inner = w_up.shape[1]
    width = depth * dp
    seq_tokens = to_sequences(tokens)
    seq_coeffs = to_sequences(coeffs)
    seq_cot = to_sequences(cotangent)
    flags = lax.dynamic_slice_in_dim(present_flag, me * count, count, 0)
    spots = lax.dynamic_slice_in_dim(sticky_pos, me * count, count, 0)
    heads_local = mu_weight.shape[0]
    mu, sigma = lax.all_gather((mu_weight, sigma_weight), "mp", axis=0, tiled=True)
    square = jnp.concatenate([w_query, w_key, w_value, w_out.T], axis=1)
    packed = jnp.concatenate([square, w_up, w_down.T], axis=1)
    whole = lax.all_gather(packed, BOTH, axis=0, tiled=False)
    whole = whole.reshape(dp, mp, depth, packed.shape[1]).transpose(0, 2, 1, 3)
    whole = whole.reshape(width, mp, packed.shape[1])

    def columns(first, size):
        return whole[:, :, first : first + size].reshape(width, mp * size)

    wq, wk, wv, wot = (columns(i * share, share) for i in range(4))
    wu = columns(4 * share, inner)
    wdt = columns(4 * share + inner, inner)
    (
        output, token_grad, coeff_grad, g1_grad, wq_grad, wk_grad, wv_grad, wo_grad,
        mu_grad, sigma_grad, g2_grad, wu_grad, wdt_grad,
    ) = whole_sequences(
        seq_tokens, seq_coeffs, flags, spots, gain_one, wq, wk, wv, wot.T, mu, sigma, gain_two, wu, wdt, seq_cot
    )

    def blocks(grad):
        return low(grad).reshape(dp, depth, mp, grad.shape[1] // mp).transpose(0, 2, 1, 3)

    def scatter(grad):
        stacked = blocks(grad)
        stacked = stacked.reshape((dp * mp * depth, stacked.shape[3]))
        return lax.psum_scatter(stacked, BOTH, scatter_dimension=0, tiled=True).astype(jnp.float32)

    wdt_own = scatter(wdt_grad)
    wu_own = scatter(wu_grad)
    square_own = scatter(
        jnp.concatenate(
            [g.reshape(width, mp, share) for g in (wq_grad, wk_grad, wv_grad, wo_grad.T)], axis=2
        ).reshape(width, mp * 4 * share)
    )
    small = lax.psum((mu_grad, sigma_grad, g1_grad, g2_grad), BOTH)
    mu_own = lax.dynamic_slice_in_dim(small[0], me * heads_local, heads_local, 0)
    sigma_own = lax.dynamic_slice_in_dim(small[1], me * heads_local, heads_local, 0)
    return (
        to_rows(output),
        to_rows(low(token_grad)).astype(jnp.float32),
        to_rows(low(coeff_grad)).astype(jnp.float32),
        small[2],
        square_own[:, :share],
        square_own[:, share : 2 * share],
        square_own[:, 2 * share : 3 * share],
        square_own[:, 3 * share :].T,
        mu_own,
        sigma_own,
        small[3],
        wu_own,
        wdt_own.T,
    )


def solution(mesh):
    in_specs = (
        P("dp", "mp", None), P("dp", "mp", None), P("dp"), P("dp", None), P(), P("dp", "mp"), P("dp", "mp"),
        P("dp", "mp"), P("mp", "dp"), P("mp", None), P("mp", None), P(), P("dp", "mp"), P("mp", "dp"),
        P("dp", "mp", None),
    )
    out_specs = (
        P("dp", "mp", None), P("dp", "mp", None), P("dp", "mp", None), P(), P("dp", "mp"), P("dp", "mp"),
        P("dp", "mp"), P("mp", "dp"), P("mp", None), P("mp", None), P(), P("dp", "mp"), P("mp", "dp"),
    )
    return jax.shard_map(body, mesh=mesh, in_specs=in_specs, out_specs=out_specs, check_vma=False)
```

```python
import math

import jax
import jax.numpy as jnp
import numpy as np
from jax import lax
from jax.experimental import pallas as pl
from jax.experimental.pallas import tpu as pltpu
from jax.sharding import PartitionSpec as P

HD = 64
NB = 256
SEGMENT_TOKENS = 256
BOTH = ("dp", "mp")

highest = lax.Precision.HIGHEST
epsilon = 1e-05
ridge = 0.5
spread_scale = 1.0 / 64.0
gelu_coef = 0.7978845608028654


def basis_tables(basis_count, seg_len):
    centers = (np.arange(basis_count) + 0.5) / basis_count
    width = 1.0 / basis_count
    times = (np.arange(2 * seg_len) + 0.5) / (2 * seg_len)
    design = np.exp(-((times[:, None] - centers[None, :]) ** 2) / (2.0 * width * width))
    normal = design.T @ design + ridge * np.eye(basis_count)
    fitting = np.linalg.solve(normal, design.T)
    return centers.astype(np.float32), fitting.astype(np.float32)


def norm_rows(values):
    centered = values - jnp.mean(values, axis=-1, keepdims=True)
    inverse = lax.rsqrt(jnp.mean(centered * centered, axis=-1, keepdims=True) + epsilon)
    return (centered * inverse, inverse)


def gelu_tanh(values):
    return (
        0.5 * values * (1.0 + jnp.tanh(gelu_coef * (values + 0.044715 * values * values * values)))
    )


def memory_reach(mem_scores, mu_in, sigma_in, centers):
    rbf_width = 1.0 / centers.shape[0]
    mu_logit = jnp.einsum("...hn,hn->...h", mem_scores, mu_in, precision=highest)
    sigma_logit = jnp.einsum("...hn,hn->...h", mem_scores, sigma_in, precision=highest)
    mean_pos = jax.nn.sigmoid(mu_logit)
    spread = jax.nn.softplus(sigma_logit) * spread_scale + rbf_width * rbf_width
    distance = mean_pos[..., None] - centers
    return (
        rbf_width
        * lax.rsqrt(spread)[..., None]
        * jnp.exp(-distance * distance / (2.0 * spread[..., None]))
    )


def mm(pattern, left_in, right_in):
    return jnp.einsum(pattern, left_in, right_in, preferred_element_type=jnp.float32)


def norm_back(grad, flat_rows, inverse, gain_vec):
    scaled = grad * gain_vec
    return inverse * (
        scaled
        - jnp.mean(scaled, axis=-1, keepdims=True)
        - flat_rows * jnp.mean(scaled * flat_rows, axis=-1, keepdims=True)
    )


def low(v):
    return v.astype(jnp.bfloat16)


def whole_sequences(
    tokens, coeffs, present_flag, sticky_pos, gain_one, wq, wk, wv, wo, mu, sigma, gain_two, wu, wdt, cot
):
    count, length, width = tokens.shape
    cur = cot.shape[1]
    past = length - cur
    heads = width // HD
    root = math.sqrt(HD)
    centers, fitting = basis_tables(NB, SEGMENT_TOKENS)
    rbf_width = 1.0 / NB
    past_fit = jnp.asarray(fitting[:, SEGMENT_TOKENS:]).astype(jnp.bfloat16)
    centers = jnp.asarray(centers)
    g1 = gain_one.astype(jnp.float32)
    g2 = gain_two.astype(jnp.float32)
    mu = mu.astype(jnp.float32)
    sigma = sigma.astype(jnp.float32)
    causal = jnp.arange(length)[None, :] <= (past + jnp.arange(cur))[:, None]
    present = present_flag.astype(jnp.float32)[:, None, None]
    spots = (sticky_pos.astype(jnp.float32) + 0.5) / (2 * SEGMENT_TOKENS)
    samples = jnp.exp(-((spots[:, :, None] - centers) ** 2) / (2.0 * rbf_width * rbf_width))
    sticky = low(
        jnp.einsum("nm,bmk->bnk", jnp.asarray(fitting[:, :SEGMENT_TOKENS]), samples, precision=highest)
    )
    rows = tokens.astype(jnp.float32)
    flat_one, inv_one = norm_rows(rows)
    normed = low(flat_one * g1)
    q = low(mm("bld,de->ble", normed[:, past:], wq))
    k = low(mm("bld,de->ble", normed, wk))
    v = low(mm("bld,de->ble", normed, wv))
    ck = low(present * mm("bnd,de->bne", coeffs, wk))
    cv = low(present * mm("bnd,de->bne", coeffs, wv))
    mk = low(mm("bnm,bme->bne", sticky, ck) + mm("np,bpe->bne", past_fit, k[:, :past]))
    mv = low(mm("bnm,bme->bne", sticky, cv) + mm("np,bpe->bne", past_fit, v[:, :past]))
    qh = q.reshape(count, cur, heads, HD)
    kh = k.reshape(count, length, heads, HD)
    vh = v.reshape(count, length, heads, HD)
    mkh = mk.reshape(count, NB, heads, HD)
    mvh = mv.reshape(count, NB, heads, HD)
    scores = mm("bqhd,bkhd->bhqk", qh, kh) / root
    masked = jnp.where(causal, scores, -1e30)
    probs = jax.nn.softmax(masked, axis=-1)
    probs_low = low(probs)
    short = mm("bhqk,bkhd->bqhd", probs_low, vh)
    mem_scores = mm("bqhd,bnhd->bqhn", qh, mkh) / root

    def reach_of(s, m, g):
        return memory_reach(s, m, g, centers)

    reach, reach_pull = jax.vjp(reach_of, mem_scores, mu, sigma)
    reach_low = low(reach)
    long_part = mm("bqhn,bnhd->bqhd", reach_low, mvh)
    context = low((short + long_part).reshape(count, cur, width))
    hidden = rows[:, past:] + mm("bqd,de->bqe", context, wo)
    flat_two, inv_two = norm_rows(hidden)
    normed_two = low(flat_two * g2)
    up = mm("bqd,df->bqf", normed_two, wu)
    active_rows, gelu_pull = jax.vjp(gelu_tanh, up)
    active = low(active_rows)
    output = low(hidden + mm("bqf,df->bqd", active, wdt))
    wdt_grad = mm("bqd,bqf->df", cot, active)
    d_up = low(gelu_pull(mm("bqd,df->bqf", cot, wdt))[0])
    wu_grad = mm("bqd,bqf->df", normed_two, d_up)
    d_n2 = mm("bqf,df->bqd", d_up, wu)
    g2_grad = jnp.sum(d_n2 * flat_two, axis=(0, 1))
    d_hidden = cot.astype(jnp.float32) + norm_back(d_n2, flat_two, inv_two, g2)
    d_hidden_low = low(d_hidden)
    wo_grad = mm("bqd,bqe->de", context, d_hidden_low)
    d_context = low(mm("bqe,de->bqd", d_hidden_low, wo)).reshape(count, cur, heads, HD)
    d_probs = mm("bqhd,bkhd->bhqk", d_context, vh)
    d_scores = low(probs * (d_probs - jnp.sum(probs * d_probs, axis=-1, keepdims=True)))
    d_reach = mm("bqhd,bnhd->bqhn", d_context, mvh)
    d_mv = low(mm("bqhn,bqhd->bnhd", reach_low, d_context)).reshape(count, NB, width)
    d_ms, mu_grad, sigma_grad = reach_pull(d_reach)
    d_ms = low(d_ms)
    dq = low(
        (mm("bhqk,bkhd->bqhd", d_scores, kh) + mm("bqhn,bnhd->bqhd", d_ms, mkh)) / root
    ).reshape(count, cur, width)
    d_mk = low(mm("bqhn,bqhd->bnhd", d_ms, qh) / root).reshape(count, NB, width)
    keep = present_flag.astype(jnp.bfloat16)[:, None, None]
    d_ck = low(mm("bnm,bne->bme", sticky, d_mk)) * keep
    d_cv = low(mm("bnm,bne->bme", sticky, d_mv)) * keep
    dk = (mm("bhqk,bqhd->bkhd", d_scores, qh) / root).reshape(count, length, width)
    dv = mm("bhqk,bqhd->bkhd", probs_low, d_context).reshape(count, length, width)
    pad = ((0, 0), (0, cur), (0, 0))
    dk = low(dk + jnp.pad(mm("np,bne->bpe", past_fit, d_mk), pad))
    dv = low(dv + jnp.pad(mm("np,bne->bpe", past_fit, d_mv), pad))
    wq_grad = mm("bqd,bqe->de", normed[:, past:], dq)
    wk_grad = mm("bld,ble->de", normed, dk) + mm("bnd,bne->de", coeffs, d_ck)
    wv_grad = mm("bld,ble->de", normed, dv) + mm("bnd,bne->de", coeffs, d_cv)
    d_n1 = mm("ble,de->bld", dk, wk) + mm("ble,de->bld", dv, wv)
    d_n1 = d_n1 + jnp.pad(mm("bqe,de->bqd", dq, wq), ((0, 0), (past, 0), (0, 0)))
    coeff_grad = mm("bne,de->bnd", d_ck, wk) + mm("bne,de->bnd", d_cv, wv)
    g1_grad = jnp.sum(d_n1 * flat_one, axis=(0, 1))
    token_grad = norm_back(d_n1, flat_one, inv_one, g1) + jnp.pad(
        d_hidden, ((0, 0), (past, 0), (0, 0))
    )
    return (
        output, token_grad, coeff_grad, g1_grad, wq_grad, wk_grad, wv_grad, wo_grad,
        mu_grad, sigma_grad, g2_grad, wu_grad, wdt_grad,
    )


def to_sequences(rows):
    return lax.all_to_all(rows, "mp", 0, 1, tiled=True)


def to_rows(rows):
    return lax.all_to_all(rows, "mp", 1, 0, tiled=True)


def body(
    tokens, coeffs, present_flag, sticky_pos, gain_one, w_query, w_key, w_value, w_out, mu_weight,
    sigma_weight, gain_two, w_up, w_down, cotangent,
):
    dp, mp = lax.axis_size("dp"), lax.axis_size("mp")
    me = lax.axis_index("mp")
    count = tokens.shape[0] // mp
    depth, share = w_query.shape
    inner = w_up.shape[1]
    width = depth * dp
    seq_tokens = to_sequences(tokens)
    seq_coeffs = to_sequences(coeffs)
    seq_cot = to_sequences(cotangent)
    flags = lax.dynamic_slice_in_dim(present_flag, me * count, count, 0)
    spots = lax.dynamic_slice_in_dim(sticky_pos, me * count, count, 0)
    heads_local = mu_weight.shape[0]
    mu, sigma = lax.all_gather((mu_weight, sigma_weight), "mp", axis=0, tiled=True)
    square = jnp.concatenate([w_query, w_key, w_value, w_out.T], axis=1)
    packed = jnp.concatenate([square, w_up, w_down.T], axis=1)
    whole = lax.all_gather(packed, BOTH, axis=0, tiled=False)
    whole = whole.reshape(dp, mp, depth, packed.shape[1]).transpose(0, 2, 1, 3)
    whole = whole.reshape(width, mp, packed.shape[1])

    def columns(first, size):
        return whole[:, :, first : first + size].reshape(width, mp * size)

    wq, wk, wv, wot = (columns(i * share, share) for i in range(4))
    wu = columns(4 * share, inner)
    wdt = columns(4 * share + inner, inner)
    (
        output, token_grad, coeff_grad, g1_grad, wq_grad, wk_grad, wv_grad, wo_grad,
        mu_grad, sigma_grad, g2_grad, wu_grad, wdt_grad,
    ) = whole_sequences(
        seq_tokens, seq_coeffs, flags, spots, gain_one, wq, wk, wv, wot.T, mu, sigma, gain_two, wu, wdt, seq_cot
    )

    def blocks(grad):
        return low(grad).reshape(dp, depth, mp, grad.shape[1] // mp).transpose(0, 2, 1, 3)

    def scatter(grad):
        stacked = blocks(grad)
        stacked = stacked.reshape((dp * mp * depth, stacked.shape[3]))
        return lax.psum_scatter(stacked, BOTH, scatter_dimension=0, tiled=True).astype(jnp.float32)

    wdt_own = scatter(wdt_grad)
    wu_own = scatter(wu_grad)
    square_own = scatter(
        jnp.concatenate(
            [g.reshape(width, mp, share) for g in (wq_grad, wk_grad, wv_grad, wo_grad.T)], axis=2
        ).reshape(width, mp * 4 * share)
    )
    small = lax.psum((mu_grad, sigma_grad, g1_grad, g2_grad), BOTH)
    mu_own = lax.dynamic_slice_in_dim(small[0], me * heads_local, heads_local, 0)
    sigma_own = lax.dynamic_slice_in_dim(small[1], me * heads_local, heads_local, 0)
    return (
        to_rows(output),
        to_rows(low(token_grad)).astype(jnp.float32),
        to_rows(low(coeff_grad)).astype(jnp.float32),
        small[2],
        square_own[:, :share],
        square_own[:, share : 2 * share],
        square_own[:, 2 * share : 3 * share],
        square_own[:, 3 * share :].T,
        mu_own,
        sigma_own,
        small[3],
        wu_own,
        wdt_own.T,
    )


f32 = jnp.float32
bf16 = jnp.bfloat16
MESH = pl.DeviceIdType.MESH
HALF = 48


def nn(a, b):
    return jnp.dot(a, b, preferred_element_type=f32)


def nt(a, b):
    return lax.dot_general(a, b, (((1,), (1,)), ((), ())), preferred_element_type=f32)


def tn(a, b):
    return lax.dot_general(a, b, (((0,), (0,)), ((), ())), preferred_element_type=f32)


class Sems:
    def __init__(self, send, recv, local):
        self.send, self.recv, self.local, self.names, self.locals = send, recv, local, {}, {}

    def pair(self, name):
        i = self.names.setdefault(name, len(self.names))
        return self.send.at[i], self.recv.at[i]

    def one(self, name):
        return self.local.at[self.locals.setdefault(name, len(self.locals))]


PAIRS = 96
LOCALS = 16


def fused_kernel(
    tok_in, coef_in, cot_in, w_in, sm_in, aux_ref, gain_ref, fita_ref, past_ref, cen_ref,
    out_o, tg_o, cg_o, wg_o, small_o,
    W, G, RC, R1X, R1Y, R2Y, R2X, R3, RS, RZ,
    TOK, COEF, COT, X0, X0T, COTT, N2, N2T, DHL, DHLT, PK, MEM, PR, CTX, HID, DH, ACC, ACT, GP, SMP,
    TK, DQ, DM, SP, SPT, OUTS, MEAN1, INV1, MEAN2, INV2,
    send, recv, local,
):
    sems = Sems(send, recv, local)
    dp, mp = lax.axis_index("dp"), lax.axis_index("mp")
    z, x, y, c = dp // 2, dp % 2, mp // 2, mp % 2
    cur = 256
    root = 0.125
    to_c = (dp, y * 2 + 1 - c)
    to_y = (dp, (1 - y) * 2 + c)
    to_x = (z * 2 + 1 - x, mp)

    def to_mp(k):
        return (dp, (mp + k) % 4)

    def to_z(k):
        return (((z + k) % 4) * 2 + x, mp)

    pending = []

    def start(name, src, dst, dev):
        s, r = sems.pair(name)
        pltpu.make_async_remote_copy(
            src_ref=src, dst_ref=dst, send_sem=s, recv_sem=r, device_id=dev, device_id_type=MESH
        ).start()
        pending.append((name, src, dst, dev))

    def wait_recv(name, region, dev):
        s, r = sems.pair(name)
        pltpu.make_async_remote_copy(
            src_ref=region, dst_ref=region, send_sem=s, recv_sem=r, device_id=dev, device_id_type=MESH
        ).wait_recv()

    def drain():
        for name, src, dst, dev in pending:
            s, r = sems.pair(name)
            pltpu.make_async_remote_copy(
                src_ref=src, dst_ref=dst, send_sem=s, recv_sem=r, device_id=dev, device_id_type=MESH
            ).wait_send()
        pending.clear()

    barrier = pltpu.get_barrier_semaphore()
    for dev in (to_mp(1), to_mp(2), to_mp(3), to_x, to_z(1), to_z(2), to_z(3)):
        pl.semaphore_signal(barrier, inc=1, device_id=dev, device_id_type=MESH)
    pl.semaphore_wait(barrier, 7)

    def rows_in(name, src, dst, n):
        for k in (1, 2, 3):
            start(f"{name}{k}", src.at[(mp + k) % 4], dst.at[pl.ds(mp * n, n)], to_mp(k))
        pltpu.make_async_copy(src.at[mp], dst.at[pl.ds(mp * n, n)], sems.one(name)).start()

    def rows_in_wait(name, src, dst, n):
        for k in (1, 2, 3):
            wait_recv(f"{name}{k}", dst.at[pl.ds(((mp - k + 4) % 4) * n, n)], to_mp(k))
        pltpu.make_async_copy(src.at[mp], dst.at[pl.ds(mp * n, n)], sems.one(name)).wait()

    def z_start(a):
        for k in (1, 2, 3):
            start(f"z{a}{k}", w_in.at[a], W.at[a, y, c, z, x], to_z(k))

    def z_wait(a):
        for k in (1, 2, 3):
            wait_recv(f"z{a}{k}", W.at[a, y, c, (z - k + 4) % 4, x], to_z(k))

    lo, hi = pl.ds(0, HALF), pl.ds(HALF, HALF)
    every = slice(None)

    def hop1_start(a):
        start(f"x0{a}", W.at[a, y, c, every, x, lo], W.at[a, y, c, every, x, lo], to_x)
        start(f"y1{a}", W.at[a, y, c, every, x, hi], W.at[a, y, c, every, x, hi], to_y)
        start(f"c1{a}", W.at[a, y, c, every, x], W.at[a, y, c, every, x], to_c)

    def hop1_wait(a):
        wait_recv(f"x0{a}", W.at[a, y, c, every, 1 - x, lo], to_x)
        wait_recv(f"y1{a}", W.at[a, 1 - y, c, every, x, hi], to_y)

    def hop2_start(a):
        start(f"y0{a}", W.at[a, y, c, every, every, lo], W.at[a, y, c, every, every, lo], to_y)
        start(f"x1{a}", W.at[a, every, c, every, x, hi], W.at[a, every, c, every, x, hi], to_x)
        start(f"c2{a}", W.at[a, y, c, every, 1 - x, lo], W.at[a, y, c, every, 1 - x, lo], to_c)
        start(f"c3{a}", W.at[a, 1 - y, c, every, x, hi], W.at[a, 1 - y, c, every, x, hi], to_c)

    def hop2_wait(a):
        wait_recv(f"y0{a}", W.at[a, 1 - y, c, every, every, lo], to_y)
        wait_recv(f"x1{a}", W.at[a, every, c, every, 1 - x, hi], to_x)

    def hop3_start(a):
        start(f"c4{a}", W.at[a, 1 - y, c, every, every, lo], W.at[a, 1 - y, c, every, every, lo], to_c)
        start(f"c5{a}", W.at[a, every, c, every, 1 - x, hi], W.at[a, every, c, every, 1 - x, hi], to_c)

    def core_wait(a):
        o = 1 - c
        wait_recv(f"c1{a}", W.at[a, y, o, every, x], to_c)
        wait_recv(f"c2{a}", W.at[a, y, o, every, 1 - x, lo], to_c)
        wait_recv(f"c3{a}", W.at[a, 1 - y, o, every, x, hi], to_c)
        wait_recv(f"c4{a}", W.at[a, 1 - y, o, every, every, lo], to_c)
        wait_recv(f"c5{a}", W.at[a, every, o, every, 1 - x, hi], to_c)

    def own_copy(a):
        return pltpu.make_async_copy(w_in.at[a], W.at[a, y, c, z, x], sems.one(f"w{a}"))

    def rc_start(a, g, s):
        start(f"rc{a}", g.at[every, 1 - c], RC.at[s], to_c)

    def rc_finish(a, g, s):
        wait_recv(f"rc{a}", RC.at[s], to_c)

        def add(i, carry):
            yy, zz, xx = i // 8, (i // 2) % 4, i % 2
            g[yy, c, zz, xx] = g[yy, c, zz, xx] + RC[s, yy, zz, xx]
            return carry

        lax.fori_loop(0, 16, add, 0)

    def r1_start(a, g, s):
        start(f"r1x{a}", g.at[every, c, every, 1 - x, lo], R1X.at[s], to_x)
        start(f"r1y{a}", g.at[1 - y, c, every, every, hi], R1Y.at[s], to_y)

    def r1_finish(a, g, s):
        wait_recv(f"r1x{a}", R1X.at[s], to_x)
        wait_recv(f"r1y{a}", R1Y.at[s], to_y)

        def add(i, carry):
            aa, zz = i // 4, i % 4
            g[aa, c, zz, x, lo] = g[aa, c, zz, x, lo] + R1X[s, aa, zz]
            g[y, c, zz, aa, hi] = g[y, c, zz, aa, hi] + R1Y[s, zz, aa]
            return carry

        lax.fori_loop(0, 8, add, 0)

    def r2_start(a, g, s):
        start(f"r2y{a}", g.at[1 - y, c, every, x, lo], R2Y.at[s], to_y)
        start(f"r2x{a}", g.at[y, c, every, 1 - x, hi], R2X.at[s], to_x)

    def r2_finish(a, g, s):
        wait_recv(f"r2y{a}", R2Y.at[s], to_y)
        wait_recv(f"r2x{a}", R2X.at[s], to_x)

        def add(zz, carry):
            g[y, c, zz, x, lo] = g[y, c, zz, x, lo] + R2Y[s, zz]
            g[y, c, zz, x, hi] = g[y, c, zz, x, hi] + R2X[s, zz]
            return carry

        lax.fori_loop(0, 4, add, 0)

    def r3_start(a, g, s):
        for k in (1, 2, 3):
            start(f"r3{a}{k}", g.at[y, c, (z + k) % 4, x], R3.at[s, k - 1], to_z(k))

    def r3_finish(a, g, s):
        for k in (1, 2, 3):
            wait_recv(f"r3{a}{k}", R3.at[s, k - 1], to_z(k))
        total = g[y, c, z, x].astype(f32)
        for k in (0, 1, 2):
            total = total + R3[s, k].astype(f32)
        wg_o[a] = total

    GD, GU, GA = G.at[0], G.at[1], W.at[1]

    rows_in("tok", tok_in, TOK, 128)
    for a in (0, 1, 2):
        own_copy(a).start()
    z_start(0)
    rows_in("coef", coef_in, COEF, 64)
    for k in (1, 2, 3):
        start(f"sm{k}", sm_in, SMP.at[mp], to_mp(k))
    pltpu.make_async_copy(sm_in, SMP.at[mp], sems.one("sm")).start()

    width_rbf = 1.0 / NB
    cen = cen_ref[0:1, :]
    spots = aux_ref[:, 0:1]
    present = aux_ref[:, 1:2]
    g1 = gain_ref[0:1, :]
    g2 = gain_ref[1:2, :]

    samples = jnp.exp(-((spots - cen) ** 2) / (2.0 * width_rbf * width_rbf))
    sticky = jnp.dot(fita_ref[...], samples, precision=highest, preferred_element_type=f32)
    SP[:, 0:256] = sticky.astype(bf16)
    SP[:, 256:512] = past_ref[...]
    SPT[0:256, :] = sticky.T.astype(bf16)
    SPT[256:512, :] = past_ref[...].astype(f32).T.astype(bf16)

    rows_in_wait("tok", tok_in, TOK, 128)

    def norm_one(i, carry):
        rows = pl.ds(pl.multiple_of(i * 128, 128), 128)
        v = TOK[rows, :].astype(f32)
        mean = jnp.mean(v, axis=-1, keepdims=True)
        centred = v - mean
        inv = lax.rsqrt(jnp.mean(centred * centred, axis=-1, keepdims=True) + epsilon)
        MEAN1[rows, :] = jnp.broadcast_to(mean, (128, 128))
        INV1[rows, :] = jnp.broadcast_to(inv, (128, 128))
        X0[pl.ds(pl.multiple_of(256 + i * 128, 128), 128), :] = (centred * inv * g1).astype(bf16)
        return carry

    lax.fori_loop(0, 4, norm_one, 0)
    z_wait(0)
    own_copy(0).wait()
    hop1_start(0)
    z_start(1)
    rows_in_wait("coef", coef_in, COEF, 64)
    X0[0:256, :] = (COEF[...].astype(f32) * present).astype(bf16)
    for r in range(3):
        X0T[:, r * 256 : (r + 1) * 256] = X0[r * 256 : (r + 1) * 256, :].astype(f32).T.astype(bf16)
    hop1_wait(0)
    hop2_start(0)
    rows_in("cot", cot_in, COT, 64)
    for k in (1, 2, 3):
        wait_recv(f"sm{k}", SMP.at[(mp - k + 4) % 4], to_mp(k))
    pltpu.make_async_copy(sm_in, SMP.at[mp], sems.one("sm")).wait()
    hop2_wait(0)
    hop3_start(0)
    z_wait(1)
    own_copy(1).wait()
    hop1_start(1)
    z_start(2)
    core_wait(0)

    def weight(a, m):
        return W[a, m // 2, m % 2].reshape(768, 768)

    def project(i, carry):
        m, r = i // 3, i % 3
        rows = pl.ds(pl.multiple_of(r * 256, 256), 256)
        PK[m, rows, :] = nn(X0[rows, :], weight(0, m)).astype(bf16)
        return carry

    lax.fori_loop(0, 12, project, 0)
    hop1_wait(1)
    hop2_start(1)

    def memory(m, carry):
        for first in (128, 512):
            col = 0 if first == 128 else 256
            MEM[m, :, col : col + 256] = nn(SP[...], PK[m, 0:512, first : first + 256]).astype(bf16)
        return carry

    lax.fori_loop(0, 4, memory, 0)

    lane = lax.broadcasted_iota(jnp.int32, (256, 128), 1)
    row_i = lax.broadcasted_iota(jnp.int32, (256, 512), 0)
    col_i = lax.broadcasted_iota(jnp.int32, (256, 512), 1)
    upper = lane >= 64

    def head_blocks(h):
        return (0, 1, 2, 0, 128) if h < 2 else (3, 4, 5, 256, 384)

    def own_lanes(h):
        return upper if h == 1 else jnp.logical_not(upper)

    def head_query(m, h):
        qb = head_blocks(h)[0]
        q = PK[m, 512:768, qb * 128 : qb * 128 + 128].astype(f32)
        return jnp.where(own_lanes(h), q * root, 0.0).astype(bf16)

    def logits(m, h, qm):
        ms = nt(qm, MEM[m, :, head_blocks(h)[3] : head_blocks(h)[3] + 128])
        mu = SMP[m, h : h + 1, :]
        sg = SMP[m, 3 + h : 4 + h, :]
        mul = jnp.sum(ms * mu, axis=-1, keepdims=True)
        sil = jnp.sum(ms * sg, axis=-1, keepdims=True)
        mean = 1.0 / (1.0 + jnp.exp(-mul))
        soft = jnp.maximum(sil, 0.0) + jnp.log1p(jnp.exp(-jnp.abs(sil)))
        spread = soft * spread_scale + width_rbf * width_rbf
        dist = mean - cen
        reach = width_rbf * lax.rsqrt(spread) * jnp.exp(-dist * dist / (2.0 * spread))
        return ms, mu, sg, sil, mean, spread, dist, reach

    def attend(m, carry):
        for h in range(3):
            qb, kb, vb, mk0, mv0 = head_blocks(h)
            qm = head_query(m, h)
            s = nt(qm, PK[m, 256:768, kb * 128 : kb * 128 + 128])
            s = jnp.where(col_i - 256 <= row_i, s, -1e30)
            top = jnp.max(s, axis=-1, keepdims=True)
            e = jnp.exp(s - top)
            p = (e * (1.0 / jnp.sum(e, axis=-1, keepdims=True))).astype(bf16)
            PR[m, h] = p
            ctx = nn(p, PK[m, 256:768, vb * 128 : vb * 128 + 128])
            reach = logits(m, h, qm)[-1]
            ctx = ctx + nn(reach.astype(bf16), MEM[m, :, mv0 : mv0 + 128])
            if h != 1:
                ctx = pltpu.roll(ctx, 64, 1)
            CTX[m, :, h * 128 : h * 128 + 128] = jnp.where(upper, ctx, 0.0).astype(bf16)
        return carry

    lax.fori_loop(0, 4, attend, 0)
    hop2_wait(1)
    hop3_start(1)
    z_wait(2)
    own_copy(2).wait()
    hop1_start(2)

    HID[...] = TOK[256:512, :].astype(f32)

    def out_weight(m):
        return W[0, m // 2, m % 2, :, :, :, 384:768].reshape(768, 384)

    def attn_out(m, carry):
        HID[...] += nt(CTX[m], out_weight(m))
        return carry

    lax.fori_loop(0, 4, attn_out, 0)
    hid = HID[...]
    mean = jnp.mean(hid, axis=-1, keepdims=True)
    centred = hid - mean
    inv = lax.rsqrt(jnp.mean(centred * centred, axis=-1, keepdims=True) + epsilon)
    MEAN2[...] = jnp.broadcast_to(mean, (256, 128))
    INV2[...] = jnp.broadcast_to(inv, (256, 128))
    normed = centred * inv * g2
    N2[...] = normed.astype(bf16)
    N2T[...] = normed.T.astype(bf16)
    hop1_wait(2)
    hop2_start(2)
    core_wait(1)

    def up(m, carry):
        u = nn(N2[...], weight(1, m))
        u2 = u * u
        th = jnp.tanh(gelu_coef * (u + 0.044715 * u2 * u))
        ACT[m] = (0.5 * u * (1.0 + th)).astype(bf16)
        GP[m] = 0.5 * (1.0 + th) + (0.5 * gelu_coef) * u * (1.0 - th * th) * (1.0 + 0.134145 * u2)
        return carry

    lax.fori_loop(0, 4, up, 0)
    rows_in_wait("cot", cot_in, COT, 64)
    COTT[...] = COT[...].astype(f32).T.astype(bf16)

    def put(g, m, zz, val):
        g[m // 2, m % 2, zz] = val.reshape(2, 96, 768).astype(bf16)

    def grad_down(i, carry):
        m, zz = i // 4, i % 4
        rows = pl.ds(pl.multiple_of(zz * 192, 64), 192)
        put(GD, m, zz, nn(COTT[rows, :], ACT[m]))
        return carry

    lax.fori_loop(0, 16, grad_down, 0)
    rc_start(2, GD, 0)
    hop2_wait(2)
    hop3_start(2)
    rc_finish(2, GD, 0)
    r1_start(2, GD, 0)
    core_wait(2)

    ACC[...] = HID[...]

    def down(m, carry):
        wd = weight(2, m)
        ACC[...] += nt(ACT[m], wd)
        d_act = nn(COT[...], wd)
        ACT[m] = (d_act * GP[m]).astype(bf16)
        return carry

    lax.fori_loop(0, 4, down, 0)
    OUTS[...] = ACC[...].astype(bf16)

    def rows_out(name, src, dst, n):
        for k in (1, 2, 3):
            start(f"{name}{k}", src.at[pl.ds(((mp + k) % 4) * n, n)], dst.at[mp], to_mp(k))
        pltpu.make_async_copy(src.at[pl.ds(mp * n, n)], dst.at[mp], sems.one(name)).start()

    def rows_out_wait(name, src, dst, n):
        for k in (1, 2, 3):
            wait_recv(f"{name}{k}", dst.at[(mp - k + 4) % 4], to_mp(k))
        pltpu.make_async_copy(src.at[pl.ds(mp * n, n)], dst.at[mp], sems.one(name)).wait()

    rows_out("out", OUTS, out_o, 64)

    def grad_up(i, carry):
        m, zz = i // 4, i % 4
        rows = pl.ds(pl.multiple_of(zz * 192, 64), 192)
        put(GU, m, zz, nn(N2T[rows, :], ACT[m]))
        return carry

    lax.fori_loop(0, 16, grad_up, 0)
    rc_start(1, GU, 1)
    ACC[...] = jnp.zeros_like(ACC)

    def back_up(m, carry):
        ACC[...] += nt(ACT[m], weight(1, m))
        return carry

    lax.fori_loop(0, 4, back_up, 0)
    rc_finish(1, GU, 1)
    d_n2 = ACC[...]
    flat = (HID[...] - MEAN2[:, 0:1]) * INV2[:, 0:1]
    g2_grad = jnp.sum(d_n2 * flat, axis=0, keepdims=True)
    e = d_n2 * g2
    d_hidden = COT[...].astype(f32) + INV2[:, 0:1] * (
        e - jnp.mean(e, axis=-1, keepdims=True) - flat * jnp.mean(e * flat, axis=-1, keepdims=True)
    )
    DH[...] = d_hidden
    DHL[...] = d_hidden.astype(bf16)
    DHLT[...] = d_hidden.T.astype(bf16)
    r1_finish(2, GD, 0)
    r2_start(2, GD, 0)
    r1_start(1, GU, 1)

    def attend_back(m, carry):
        ow = out_weight(m)
        d_ctx = nn(DHL[...], ow)
        for h in range(3):
            qb, kb, vb, mk0, mv0 = head_blocks(h)
            qm = head_query(m, h)
            dc = d_ctx[:, h * 128 : h * 128 + 128]
            if h != 1:
                dc = pltpu.roll(dc, 64, 1)
            dc = jnp.where(own_lanes(h), dc, 0.0).astype(bf16)
            p = PR[m, h]
            kv = PK[m, 256:768, kb * 128 : kb * 128 + 128]
            d_p = nt(dc, PK[m, 256:768, vb * 128 : vb * 128 + 128])
            pf = p.astype(f32)
            t = pf * d_p
            d_s = (t - pf * jnp.sum(t, axis=-1, keepdims=True)).astype(bf16)
            d_v = tn(p, dc)
            d_k = tn(d_s, qm)
            mkv = MEM[m, :, mk0 : mk0 + 128]
            ms, mu, sg, sil, mean, spread, dist, reach = logits(m, h, qm)
            d_r = nt(dc, MEM[m, :, mv0 : mv0 + 128])
            d_mv = tn(reach.astype(bf16), dc)
            t = d_r * reach
            td = t * dist
            inv_s = 1.0 / spread
            g_mean = -jnp.sum(td, axis=-1, keepdims=True) * inv_s
            g_s = (jnp.sum(td * dist, axis=-1, keepdims=True) * inv_s - jnp.sum(t, axis=-1, keepdims=True)) * (
                0.5 * inv_s
            )
            g_mu = g_mean * mean * (1.0 - mean)
            g_sg = g_s * spread_scale * (1.0 / (1.0 + jnp.exp(-sil)))
            d_ms = (g_mu * mu + g_sg * sg).astype(bf16)
            small_o[pl.ds(m * 3 + h, 1), :] = jnp.sum(g_mu * ms, axis=0, keepdims=True)
            small_o[pl.ds(12 + m * 3 + h, 1), :] = jnp.sum(g_sg * ms, axis=0, keepdims=True)
            d_mk = tn(d_ms, qm)
            d_q = (nn(d_s, kv) + nn(d_ms, mkv)) * root
            d_q = jnp.where(own_lanes(h), d_q, 0.0)
            j = 0 if h < 2 else 1
            if h == 1:
                TK[0] += d_k
                TK[1] += d_v
                DQ[0] += d_q
                DM[:, 0:128] += d_mk.astype(bf16)
                DM[:, 128:256] += d_mv.astype(bf16)
            else:
                TK[2 * j] = d_k
                TK[2 * j + 1] = d_v
                DQ[j] = d_q
                DM[:, 256 * j : 256 * j + 128] = d_mk.astype(bf16)
                DM[:, 256 * j + 128 : 256 * j + 256] = d_mv.astype(bf16)
        back = nn(SPT[...], DM[...])
        for j, first in ((0, 128), (1, 512)):
            for i in range(2):
                b = back[:, 256 * j + 128 * i : 256 * j + 128 * i + 128]
                cols = slice(first + 128 * i, first + 128 * i + 128)
                PK[m, 0:256, cols] = (b[0:256] * present).astype(bf16)
                PK[m, 256:512, cols] = (TK[2 * j + i, 0:256] + b[256:512]).astype(bf16)
                PK[m, 512:768, cols] = TK[2 * j + i, 256:512].astype(bf16)
            qcols = slice(384 * j, 384 * j + 128)
            PK[m, 0:512, qcols] = jnp.zeros((512, 128), bf16)
            PK[m, 512:768, qcols] = DQ[j].astype(bf16)
        return carry

    lax.fori_loop(0, 4, attend_back, 0)
    drain()

    r2_finish(2, GD, 0)
    r3_start(2, GD, 0)
    r1_finish(1, GU, 1)
    r2_start(1, GU, 1)

    def grad_square(i, carry):
        m, zz = i // 4, i % 4
        rows = pl.ds(pl.multiple_of(zz * 192, 64), 192)
        first = nn(X0T[rows, :], PK[m])
        second = nn(DHLT[rows, :], CTX[m])
        both = jnp.concatenate([first[:, 0:384], first[:, 384:768] + second], axis=1)
        put(GA, m, zz, both)
        return carry

    lax.fori_loop(0, 16, grad_square, 0)
    rc_start(0, GA, 0)

    def rows_back(r):
        ACC[...] = jnp.zeros_like(ACC)

        def one(m, carry):
            ACC[...] += nt(PK[m, r * 256 : (r + 1) * 256, :], weight(0, m))
            return carry

        lax.fori_loop(0, 4, one, 0)

    def token_rows(r, first, extra):
        rows_back(r)
        d_n1 = ACC[...]
        rows = slice(first, first + 256)
        inv_1 = INV1[rows, 0:1]
        flat_1 = (TOK[rows, :].astype(f32) - MEAN1[rows, 0:1]) * inv_1
        part = jnp.sum(d_n1 * flat_1, axis=0, keepdims=True)
        e = d_n1 * g1
        grad = inv_1 * (
            e - jnp.mean(e, axis=-1, keepdims=True) - flat_1 * jnp.mean(e * flat_1, axis=-1, keepdims=True)
        )
        if extra:
            grad = grad + DH[...]
        X0[256 + first : 512 + first, :] = grad.astype(bf16)
        return part

    rows_back(0)
    X0[0:256, :] = ACC[...].astype(bf16)
    rc_finish(0, GA, 0)
    r1_start(0, GA, 0)
    rows_out("cg", X0.at[pl.ds(0, 256)], cg_o, 64)
    r2_finish(1, GU, 1)
    r3_finish(2, GD, 0)
    r3_start(1, GU, 1)
    part = token_rows(1, 0, False)
    part = part + token_rows(2, 256, True)
    rows_out("tg", X0.at[pl.ds(256, 512)], tg_o, 128)
    for i in range(3):
        small_o[24 + i : 25 + i, :] = part[:, i * 256 : (i + 1) * 256]
        small_o[27 + i : 28 + i, :] = g2_grad[:, i * 256 : (i + 1) * 256]
    small_o[30:32, :] = jnp.zeros((2, 256), f32)

    for i, dev in ((0, to_c), (1, to_x), (2, to_y)):
        RS[2 * i] = small_o[...]
        start(f"sr{i}", RS.at[2 * i], RS.at[2 * i + 1], dev)
        wait_recv(f"sr{i}", RS.at[2 * i + 1], dev)
        small_o[...] = small_o[...] + RS[2 * i + 1]
    RS[6] = small_o[...]
    for k in (1, 2, 3):
        start(f"sz{k}", RS.at[6], RZ.at[k - 1], to_z(k))
    r1_finish(0, GA, 0)
    r2_start(0, GA, 0)
    r3_finish(1, GU, 1)
    r2_finish(0, GA, 0)
    r3_start(0, GA, 0)
    for k in (1, 2, 3):
        wait_recv(f"sz{k}", RZ.at[k - 1], to_z(k))
    small_o[...] = RS[6] + RZ[0] + RZ[1] + RZ[2]
    rows_out_wait("out", OUTS, out_o, 64)
    rows_out_wait("cg", X0.at[pl.ds(0, 256)], cg_o, 64)
    rows_out_wait("tg", X0.at[pl.ds(256, 512)], tg_o, 128)
    r3_finish(0, GA, 0)
    drain()


def fused_call(tok, coef, cot, weights, small, aux, gains, fita, past, cen):
    any_ = pl.BlockSpec(memory_space=pl.ANY)
    vm = pl.BlockSpec(memory_space=pltpu.VMEM)
    V = pltpu.VMEM
    return pl.pallas_call(
        fused_kernel,
        out_shape=(
            jax.ShapeDtypeStruct((4, 64, 768), bf16),
            jax.ShapeDtypeStruct((4, 128, 768), bf16),
            jax.ShapeDtypeStruct((4, 64, 768), bf16),
            jax.ShapeDtypeStruct((3, 96, 768), f32),
            jax.ShapeDtypeStruct((32, 256), f32),
        ),
        in_specs=[any_, any_, any_, any_, any_, vm, vm, vm, vm, vm],
        out_specs=(any_, any_, any_, vm, vm),
        scratch_shapes=[
            V((3, 2, 2, 4, 2, 96, 768), bf16),
            V((2, 2, 2, 4, 2, 96, 768), bf16),
            V((2, 2, 4, 2, 96, 768), bf16),
            V((2, 2, 4, HALF, 768), bf16),
            V((2, 4, 2, HALF, 768), bf16),
            V((2, 4, HALF, 768), bf16),
            V((2, 4, HALF, 768), bf16),
            V((2, 3, 96, 768), bf16),
            V((7, 32, 256), f32),
            V((3, 32, 256), f32),
            V((512, 768), bf16),
            V((256, 768), bf16),
            V((256, 768), bf16),
            V((768, 768), bf16),
            V((768, 768), bf16),
            V((768, 256), bf16),
            V((256, 768), bf16),
            V((768, 256), bf16),
            V((256, 768), bf16),
            V((768, 256), bf16),
            V((4, 768, 768), bf16),
            V((4, 256, 512), bf16),
            V((4, 3, 256, 512), bf16),
            V((4, 256, 384), bf16),
            V((256, 768), f32),
            V((256, 768), f32),
            V((256, 768), f32),
            V((4, 256, 768), bf16),
            V((4, 256, 768), f32),
            V((4, 8, 256), f32),
            V((4, 512, 128), f32),
            V((2, 256, 128), f32),
            V((256, 512), bf16),
            V((256, 512), bf16),
            V((512, 256), bf16),
            V((256, 768), bf16),
            V((512, 128), f32),
            V((512, 128), f32),
            V((256, 128), f32),
            V((256, 128), f32),
            pltpu.SemaphoreType.DMA((PAIRS,)),
            pltpu.SemaphoreType.DMA((PAIRS,)),
            pltpu.SemaphoreType.DMA((LOCALS,)),
        ],
        compiler_params=pltpu.CompilerParams(
            collective_id=0, has_side_effects=True, vmem_limit_bytes=63 * 1024 * 1024
        ),
    )(tok, coef, cot, weights, small, aux, gains, fita, past, cen)


def fused_body(
    tokens, coeffs, present_flag, sticky_pos, gain_one, w_query, w_key, w_value, w_out, mu_weight,
    sigma_weight, gain_two, w_up, w_down, cotangent,
):
    me = lax.axis_index("mp")
    centers, fitting = basis_tables(NB, SEGMENT_TOKENS)
    wo = w_out.T
    pieces = []
    for parts in ((w_query, w_key, w_value),):
        for p in parts:
            pieces.append(p[:, 0:128])
        for i, p in enumerate(parts):
            pieces.append(p[:, 128:192])
            pieces.append(wo[:, i * 64 : i * 64 + 64])
    weights = jnp.stack([jnp.concatenate(pieces, axis=1), w_up, w_down.T])
    small = jnp.concatenate([mu_weight, sigma_weight, jnp.zeros((2, NB), mu_weight.dtype)], axis=0).astype(f32)
    spot = (lax.dynamic_slice_in_dim(sticky_pos, me, 1, 0)[0].astype(f32) + 0.5) / (2 * SEGMENT_TOKENS)
    flag = lax.dynamic_slice_in_dim(present_flag, me, 1, 0).astype(f32)
    lanes = lax.broadcasted_iota(jnp.int32, (NB, 128), 1)
    aux = jnp.where(lanes == 0, spot[:, None], flag[0])
    gains = jnp.concatenate(
        [gain_one[None], gain_two[None], jnp.zeros((6, gain_one.shape[0]), gain_one.dtype)], axis=0
    ).astype(f32)
    fita = jnp.asarray(fitting[:, :SEGMENT_TOKENS])
    past = jnp.asarray(fitting[:, SEGMENT_TOKENS:]).astype(bf16)
    cen = jnp.broadcast_to(jnp.asarray(centers)[None], (8, NB))
    out, tg, cg, wg, sums = fused_call(tokens, coeffs, cotangent, weights, small, aux, gains, fita, past, cen)
    sq = wg[0]

    def three(i):
        return jnp.concatenate([sq[:, 128 * i : 128 * i + 128], sq[:, 384 + 128 * i : 448 + 128 * i]], axis=1)

    wo_grad = jnp.concatenate([sq[:, 448 + 128 * i : 512 + 128 * i] for i in range(3)], axis=1).T
    local = mu_weight.shape[0]
    return (
        out, tg.astype(f32), cg.astype(f32), sums[24:27].reshape(-1), three(0), three(1), three(2), wo_grad,
        lax.dynamic_slice_in_dim(sums[0:12], me * local, local, 0),
        lax.dynamic_slice_in_dim(sums[12:24], me * local, local, 0),
        sums[27:30].reshape(-1), wg[1], wg[2].T,
    )


def solution(mesh):
    in_specs = (
        P("dp", "mp", None), P("dp", "mp", None), P("dp"), P("dp", None), P(), P("dp", "mp"), P("dp", "mp"),
        P("dp", "mp"), P("mp", "dp"), P("mp", None), P("mp", None), P(), P("dp", "mp"), P("mp", "dp"),
        P("dp", "mp", None),
    )
    out_specs = (
        P("dp", "mp", None), P("dp", "mp", None), P("dp", "mp", None), P(), P("dp", "mp"), P("dp", "mp"),
        P("dp", "mp"), P("mp", "dp"), P("mp", None), P("mp", None), P(), P("dp", "mp"), P("mp", "dp"),
    )
    whole = body
    if mesh.shape["dp"] == 8 and mesh.shape["mp"] == 4:
        whole = fused_body
    return jax.shard_map(whole, mesh=mesh, in_specs=in_specs, out_specs=out_specs, check_vma=False)
```

```python
import math

import jax
import jax.numpy as jnp
import numpy as np
from jax import lax
from jax.experimental import pallas as pl
from jax.experimental.pallas import tpu as pltpu
from jax.sharding import PartitionSpec as P

HD = 64
NB = 256
SEGMENT_TOKENS = 256
BOTH = ("dp", "mp")

highest = lax.Precision.HIGHEST
epsilon = 1e-05
ridge = 0.5
spread_scale = 1.0 / 64.0
gelu_coef = 0.7978845608028654


def basis_tables(basis_count, seg_len):
    centers = (np.arange(basis_count) + 0.5) / basis_count
    width = 1.0 / basis_count
    times = (np.arange(2 * seg_len) + 0.5) / (2 * seg_len)
    design = np.exp(-((times[:, None] - centers[None, :]) ** 2) / (2.0 * width * width))
    normal = design.T @ design + ridge * np.eye(basis_count)
    fitting = np.linalg.solve(normal, design.T)
    return centers.astype(np.float32), fitting.astype(np.float32)


def norm_rows(values):
    centered = values - jnp.mean(values, axis=-1, keepdims=True)
    inverse = lax.rsqrt(jnp.mean(centered * centered, axis=-1, keepdims=True) + epsilon)
    return (centered * inverse, inverse)


def gelu_tanh(values):
    return (
        0.5 * values * (1.0 + jnp.tanh(gelu_coef * (values + 0.044715 * values * values * values)))
    )


def memory_reach(mem_scores, mu_in, sigma_in, centers):
    rbf_width = 1.0 / centers.shape[0]
    mu_logit = jnp.einsum("...hn,hn->...h", mem_scores, mu_in, precision=highest)
    sigma_logit = jnp.einsum("...hn,hn->...h", mem_scores, sigma_in, precision=highest)
    mean_pos = jax.nn.sigmoid(mu_logit)
    spread = jax.nn.softplus(sigma_logit) * spread_scale + rbf_width * rbf_width
    distance = mean_pos[..., None] - centers
    return (
        rbf_width
        * lax.rsqrt(spread)[..., None]
        * jnp.exp(-distance * distance / (2.0 * spread[..., None]))
    )


def mm(pattern, left_in, right_in):
    return jnp.einsum(pattern, left_in, right_in, preferred_element_type=jnp.float32)


def norm_back(grad, flat_rows, inverse, gain_vec):
    scaled = grad * gain_vec
    return inverse * (
        scaled
        - jnp.mean(scaled, axis=-1, keepdims=True)
        - flat_rows * jnp.mean(scaled * flat_rows, axis=-1, keepdims=True)
    )


def low(v):
    return v.astype(jnp.bfloat16)


def whole_sequences(
    tokens, coeffs, present_flag, sticky_pos, gain_one, wq, wk, wv, wo, mu, sigma, gain_two, wu, wdt, cot
):
    count, length, width = tokens.shape
    cur = cot.shape[1]
    past = length - cur
    heads = width // HD
    root = math.sqrt(HD)
    centers, fitting = basis_tables(NB, SEGMENT_TOKENS)
    rbf_width = 1.0 / NB
    past_fit = jnp.asarray(fitting[:, SEGMENT_TOKENS:]).astype(jnp.bfloat16)
    centers = jnp.asarray(centers)
    g1 = gain_one.astype(jnp.float32)
    g2 = gain_two.astype(jnp.float32)
    mu = mu.astype(jnp.float32)
    sigma = sigma.astype(jnp.float32)
    causal = jnp.arange(length)[None, :] <= (past + jnp.arange(cur))[:, None]
    present = present_flag.astype(jnp.float32)[:, None, None]
    spots = (sticky_pos.astype(jnp.float32) + 0.5) / (2 * SEGMENT_TOKENS)
    samples = jnp.exp(-((spots[:, :, None] - centers) ** 2) / (2.0 * rbf_width * rbf_width))
    sticky = low(
        jnp.einsum("nm,bmk->bnk", jnp.asarray(fitting[:, :SEGMENT_TOKENS]), samples, precision=highest)
    )
    rows = tokens.astype(jnp.float32)
    flat_one, inv_one = norm_rows(rows)
    normed = low(flat_one * g1)
    q = low(mm("bld,de->ble", normed[:, past:], wq))
    k = low(mm("bld,de->ble", normed, wk))
    v = low(mm("bld,de->ble", normed, wv))
    ck = low(present * mm("bnd,de->bne", coeffs, wk))
    cv = low(present * mm("bnd,de->bne", coeffs, wv))
    mk = low(mm("bnm,bme->bne", sticky, ck) + mm("np,bpe->bne", past_fit, k[:, :past]))
    mv = low(mm("bnm,bme->bne", sticky, cv) + mm("np,bpe->bne", past_fit, v[:, :past]))
    qh = q.reshape(count, cur, heads, HD)
    kh = k.reshape(count, length, heads, HD)
    vh = v.reshape(count, length, heads, HD)
    mkh = mk.reshape(count, NB, heads, HD)
    mvh = mv.reshape(count, NB, heads, HD)
    scores = mm("bqhd,bkhd->bhqk", qh, kh) / root
    masked = jnp.where(causal, scores, -1e30)
    probs = jax.nn.softmax(masked, axis=-1)
    probs_low = low(probs)
    short = mm("bhqk,bkhd->bqhd", probs_low, vh)
    mem_scores = mm("bqhd,bnhd->bqhn", qh, mkh) / root

    def reach_of(s, m, g):
        return memory_reach(s, m, g, centers)

    reach, reach_pull = jax.vjp(reach_of, mem_scores, mu, sigma)
    reach_low = low(reach)
    long_part = mm("bqhn,bnhd->bqhd", reach_low, mvh)
    context = low((short + long_part).reshape(count, cur, width))
    hidden = rows[:, past:] + mm("bqd,de->bqe", context, wo)
    flat_two, inv_two = norm_rows(hidden)
    normed_two = low(flat_two * g2)
    up = mm("bqd,df->bqf", normed_two, wu)
    active_rows, gelu_pull = jax.vjp(gelu_tanh, up)
    active = low(active_rows)
    output = low(hidden + mm("bqf,df->bqd", active, wdt))
    wdt_grad = mm("bqd,bqf->df", cot, active)
    d_up = low(gelu_pull(mm("bqd,df->bqf", cot, wdt))[0])
    wu_grad = mm("bqd,bqf->df", normed_two, d_up)
    d_n2 = mm("bqf,df->bqd", d_up, wu)
    g2_grad = jnp.sum(d_n2 * flat_two, axis=(0, 1))
    d_hidden = cot.astype(jnp.float32) + norm_back(d_n2, flat_two, inv_two, g2)
    d_hidden_low = low(d_hidden)
    wo_grad = mm("bqd,bqe->de", context, d_hidden_low)
    d_context = low(mm("bqe,de->bqd", d_hidden_low, wo)).reshape(count, cur, heads, HD)
    d_probs = mm("bqhd,bkhd->bhqk", d_context, vh)
    d_scores = low(probs * (d_probs - jnp.sum(probs * d_probs, axis=-1, keepdims=True)))
    d_reach = mm("bqhd,bnhd->bqhn", d_context, mvh)
    d_mv = low(mm("bqhn,bqhd->bnhd", reach_low, d_context)).reshape(count, NB, width)
    d_ms, mu_grad, sigma_grad = reach_pull(d_reach)
    d_ms = low(d_ms)
    dq = low(
        (mm("bhqk,bkhd->bqhd", d_scores, kh) + mm("bqhn,bnhd->bqhd", d_ms, mkh)) / root
    ).reshape(count, cur, width)
    d_mk = low(mm("bqhn,bqhd->bnhd", d_ms, qh) / root).reshape(count, NB, width)
    keep = present_flag.astype(jnp.bfloat16)[:, None, None]
    d_ck = low(mm("bnm,bne->bme", sticky, d_mk)) * keep
    d_cv = low(mm("bnm,bne->bme", sticky, d_mv)) * keep
    dk = (mm("bhqk,bqhd->bkhd", d_scores, qh) / root).reshape(count, length, width)
    dv = mm("bhqk,bqhd->bkhd", probs_low, d_context).reshape(count, length, width)
    pad = ((0, 0), (0, cur), (0, 0))
    dk = low(dk + jnp.pad(mm("np,bne->bpe", past_fit, d_mk), pad))
    dv = low(dv + jnp.pad(mm("np,bne->bpe", past_fit, d_mv), pad))
    wq_grad = mm("bqd,bqe->de", normed[:, past:], dq)
    wk_grad = mm("bld,ble->de", normed, dk) + mm("bnd,bne->de", coeffs, d_ck)
    wv_grad = mm("bld,ble->de", normed, dv) + mm("bnd,bne->de", coeffs, d_cv)
    d_n1 = mm("ble,de->bld", dk, wk) + mm("ble,de->bld", dv, wv)
    d_n1 = d_n1 + jnp.pad(mm("bqe,de->bqd", dq, wq), ((0, 0), (past, 0), (0, 0)))
    coeff_grad = mm("bne,de->bnd", d_ck, wk) + mm("bne,de->bnd", d_cv, wv)
    g1_grad = jnp.sum(d_n1 * flat_one, axis=(0, 1))
    token_grad = norm_back(d_n1, flat_one, inv_one, g1) + jnp.pad(
        d_hidden, ((0, 0), (past, 0), (0, 0))
    )
    return (
        output, token_grad, coeff_grad, g1_grad, wq_grad, wk_grad, wv_grad, wo_grad,
        mu_grad, sigma_grad, g2_grad, wu_grad, wdt_grad,
    )


def to_sequences(rows):
    return lax.all_to_all(rows, "mp", 0, 1, tiled=True)


def to_rows(rows):
    return lax.all_to_all(rows, "mp", 1, 0, tiled=True)


def body(
    tokens, coeffs, present_flag, sticky_pos, gain_one, w_query, w_key, w_value, w_out, mu_weight,
    sigma_weight, gain_two, w_up, w_down, cotangent,
):
    dp, mp = lax.axis_size("dp"), lax.axis_size("mp")
    me = lax.axis_index("mp")
    count = tokens.shape[0] // mp
    depth, share = w_query.shape
    inner = w_up.shape[1]
    width = depth * dp
    seq_tokens = to_sequences(tokens)
    seq_coeffs = to_sequences(coeffs)
    seq_cot = to_sequences(cotangent)
    flags = lax.dynamic_slice_in_dim(present_flag, me * count, count, 0)
    spots = lax.dynamic_slice_in_dim(sticky_pos, me * count, count, 0)
    heads_local = mu_weight.shape[0]
    mu, sigma = lax.all_gather((mu_weight, sigma_weight), "mp", axis=0, tiled=True)
    square = jnp.concatenate([w_query, w_key, w_value, w_out.T], axis=1)
    packed = jnp.concatenate([square, w_up, w_down.T], axis=1)
    whole = lax.all_gather(packed, BOTH, axis=0, tiled=False)
    whole = whole.reshape(dp, mp, depth, packed.shape[1]).transpose(0, 2, 1, 3)
    whole = whole.reshape(width, mp, packed.shape[1])

    def columns(first, size):
        return whole[:, :, first : first + size].reshape(width, mp * size)

    wq, wk, wv, wot = (columns(i * share, share) for i in range(4))
    wu = columns(4 * share, inner)
    wdt = columns(4 * share + inner, inner)
    (
        output, token_grad, coeff_grad, g1_grad, wq_grad, wk_grad, wv_grad, wo_grad,
        mu_grad, sigma_grad, g2_grad, wu_grad, wdt_grad,
    ) = whole_sequences(
        seq_tokens, seq_coeffs, flags, spots, gain_one, wq, wk, wv, wot.T, mu, sigma, gain_two, wu, wdt, seq_cot
    )

    def blocks(grad):
        return low(grad).reshape(dp, depth, mp, grad.shape[1] // mp).transpose(0, 2, 1, 3)

    def scatter(grad):
        stacked = blocks(grad)
        stacked = stacked.reshape((dp * mp * depth, stacked.shape[3]))
        return lax.psum_scatter(stacked, BOTH, scatter_dimension=0, tiled=True).astype(jnp.float32)

    wdt_own = scatter(wdt_grad)
    wu_own = scatter(wu_grad)
    square_own = scatter(
        jnp.concatenate(
            [g.reshape(width, mp, share) for g in (wq_grad, wk_grad, wv_grad, wo_grad.T)], axis=2
        ).reshape(width, mp * 4 * share)
    )
    small = lax.psum((mu_grad, sigma_grad, g1_grad, g2_grad), BOTH)
    mu_own = lax.dynamic_slice_in_dim(small[0], me * heads_local, heads_local, 0)
    sigma_own = lax.dynamic_slice_in_dim(small[1], me * heads_local, heads_local, 0)
    return (
        to_rows(output),
        to_rows(low(token_grad)).astype(jnp.float32),
        to_rows(low(coeff_grad)).astype(jnp.float32),
        small[2],
        square_own[:, :share],
        square_own[:, share : 2 * share],
        square_own[:, 2 * share : 3 * share],
        square_own[:, 3 * share :].T,
        mu_own,
        sigma_own,
        small[3],
        wu_own,
        wdt_own.T,
    )


f32 = jnp.float32
bf16 = jnp.bfloat16
MESH = pl.DeviceIdType.MESH


def nn(a, b):
    return jnp.dot(a, b, preferred_element_type=f32)


def nt(a, b):
    return lax.dot_general(a, b, (((1,), (1,)), ((), ())), preferred_element_type=f32)


def tn(a, b):
    return lax.dot_general(a, b, (((0,), (0,)), ((), ())), preferred_element_type=f32)


class Sems:
    def __init__(self, send, recv, local):
        self.send, self.recv, self.local, self.names, self.locals = send, recv, local, {}, {}

    def pair(self, name):
        i = self.names.setdefault(name, len(self.names))
        return self.send.at[i], self.recv.at[i]

    def one(self, name):
        return self.local.at[self.locals.setdefault(name, len(self.locals))]


PAIRS = 304
LOCALS = 16
COLS = 384
PIECES = {"A1": (0, 0), "A2": (0, 384), "U1": (1, 0), "U2": (1, 384), "D1": (2, 0), "D2": (2, 384)}
SETS = {"D1": 0, "D2": 1, "U1": 2, "U2": 3, "A1": 0, "A2": 1}
SIZE = {"y": 2, "z": 4, "x": 2}
GATHER = {
    "A1": ((0, 16, "zyx"), (16, 40, "zyx"), (56, 40, "zyx"),),
    "A2": ((0, 40, "yzx"), (40, 32, "xyz"), (72, 24, "zxy"),),
    "U1": ((0, 24, "yzx"), (24, 64, "zxy"), (88, 8, "zyx"),),
    "U2": ((0, 24, "yzx"), (24, 64, "zxy"), (88, 8, "zyx"),),
    "D1": ((0, 48, "zxy"), (48, 24, "zyx"), (72, 24, "xyz"),),
    "D2": ((0, 48, "zxy"), (48, 24, "zyx"), (72, 24, "xyz"),),
}
SCATTER = {
    "D1": ((0, 8, "zyx"), (8, 40, "xzy"), (48, 48, "yzx"),),
    "D2": ((0, 8, "zyx"), (8, 40, "xzy"), (48, 48, "yzx"),),
    "U1": ((0, 48, "xyz"), (48, 16, "xyz"), (64, 32, "yxz"),),
    "U2": ((0, 48, "xyz"), (48, 16, "xyz"), (64, 32, "yxz"),),
    "A1": ((0, 48, "yxz"), (48, 48, "xzy"),),
    "A2": ((0, 32, "xyz"), (32, 24, "yzx"), (56, 40, "yxz"),),
}
SCHEDULE = [
    "+tok", "pack", "+pA1own", "+gA1.00", "+gA1.10", "+pA2own", "+gA2.10", "packud", "+pU1own", "+pU2own",
    "+pD1own", "+gD1.20", "+pD2own", "+gD2.20", "sticky", "-pA1own", "-pA2own", "-gA2.10", "-pU1own", "-pU2own",
    "-pD1own", "-pD2own", "+gA1.20", "+pgA2.10", "-gD1.20", "-gD2.20", "+pgD1.20", "+pgD2.20", "-gA1.00",
    "+pgA1.00", "-pgA2.10", "-pgD1.20", "-pgD2.20", "-pgA1.00", "+gA2.20", "-gA1.10", "+pgA1.10", "+gA1.01",
    "+gU1.10", "-pgA1.10", "+gA1.11", "+coef", "-gA1.01", "+pgA1.01", "+gA1.02", "-gA2.20", "+pgA2.20", "+gA2.21",
    "-gA1.20", "+pgA1.20", "-tok", "+gU1.20", "norm1", "-pgA1.01", "-pgA1.20", "-pgA2.20", "-gU1.20", "+pgU1.20",
    "+gU2.10", "+gA1.21", "-gU1.10", "+pgU1.10", "+gU1.11", "-gA1.11", "+pgA1.11", "-gA2.21", "+pgA2.21",
    "-pgU1.20", "-gA1.02", "+pgA1.02", "-pgU1.10", "+gU2.20", "-pgA1.11", "-pgA2.21", "-pgA1.02", "+gA2.00",
    "+gD1.00", "+gA1.12", "+gA2.11", "-gU2.20", "+gA2.22", "+pgU2.20", "-coef", "x0", "+gD1.10", "-gA2.00",
    "+pgA2.00", "-pgU2.20", "-gU1.11", "+pgU1.11", "-gU2.10", "+pgU2.10", "-pgA2.00", "+gA2.01", "+cot",
    "-gA1.21", "+pgA1.21", "+gA1.22", "-gA2.11", "+pgA2.11", "-pgU2.10", "-pgU1.11", "-pgA2.11", "-pgA1.21",
    "-gD1.10", "+pgD1.10", "-gD1.00", "+pgD1.00", "+gU1.00", "-gA2.22", "+pgA2.22", "+gU1.21", "-pgD1.10",
    "+gA2.12", "+gU1.12", "-pgD1.00", "-gA1.12", "+pgA1.12", "+gU2.11", "-pgA2.22", "-gU1.00", "+pgU1.00",
    "-pgA1.12", "-gU1.21", "+pgU1.21", "-pgU1.00", "-pgU1.21", "-cot", "-gA2.01", "+pgA2.01", "+gA2.02",
    "-gA1.22", "+pgA1.22", "-pgA2.01", "-pgA1.22", "pj1_0", "pj1_1", "+gU1.01", "+gU2.00", "+gU2.21", "pj1_2",
    "-gU2.11", "+pgU2.11", "+gU2.12", "pj1_3", "+gU1.22", "mem1_0", "mem1_1", "mem1_2", "mem1_3", "at1_0",
    "-pgU2.11", "-gU2.00", "-gU2.21", "+pgU2.00", "+pgU2.21", "+gU2.01", "+gU2.22", "+gD1.01", "at1_1", "-gA2.12",
    "-gU1.12", "-gU1.22", "-pgU2.00", "-pgU2.21", "+pgA2.12", "+pgU1.12", "+pgU1.22", "at1_2", "-gA2.02",
    "-gU1.01", "+pgA2.02", "+pgU1.01", "+gU1.02", "+gD2.00", "at1_3", "-pgA2.12", "-pgU1.22", "-pgU1.12",
    "-gU2.22", "+pgU2.22", "-pgU1.01", "-pgA2.02", "pj2_0", "+gD1.21", "+gD2.10", "pj2_1", "-pgU2.22", "-gU2.01",
    "+pgU2.01", "+gU2.02", "+gD1.11", "pj2_2", "pj2_3", "-pgU2.01", "-gD1.01", "+pgD1.01", "+gD1.02", "mem2_0",
    "mem2_1", "mem2_2", "mem2_3", "-gD1.21", "+pgD1.21", "+gD1.22", "at2_0", "at2_1", "-pgD1.01", "-pgD1.21",
    "-gD2.00", "-gD2.10", "+pgD2.00", "+pgD2.10", "+gD2.01", "-gU2.12", "+pgU2.12", "at2_2", "-gU1.02",
    "+pgU1.02", "at2_3", "-gD1.11", "+pgD1.11", "x0t", "-pgD2.10", "-pgD2.00", "+gD1.12", "-pgU2.12", "-pgU1.02",
    "-gU2.02", "+pgU2.02", "attnout", "-pgD1.11", "+gD2.21", "norm2", "-pgU2.02", "+gD2.11", "up1_0", "up1_1",
    "up1_2", "-gD1.22", "-gD2.01", "+pgD1.22", "+pgD2.01", "+gD2.02", "up1_3", "up2_0", "-gD2.21", "+pgD2.21",
    "+gD2.22", "up2_1", "up2_2", "-gD1.02", "+pgD1.02", "up2_3", "-pgD1.22", "-gD1.12", "-pgD2.01", "+pgD1.12",
    "-pgD2.21", "cott", "gd1_0", "gd1_1", "-gD2.11", "+pgD2.11", "+gD2.12", "-pgD1.02", "gd1_2", "-pgD1.12",
    "gd1_3", "+rcD1", "gd2_0", "-pgD2.11", "gd2_1", "gd2_2", "gd2_3", "+rcD2", "dn1_0", "dn1_1", "dn1_2",
    "-gD2.12", "-rcD1", "+pgD2.12", "+rD1.00", "+rD1.10", "+rD1.20", "-gD2.22", "-gD2.02", "+pgD2.22", "+pgD2.02",
    "dn1_3", "gu1_0", "gu1_1", "gu1_2", "-pgD2.12", "gu1_3", "-pgD2.22", "-rcD2", "+rD2.00", "+rcU1", "-pgD2.02",
    "dn2_0", "-rD1.00", "+rD2.10", "dn2_1", "dn2_2", "+rD1.01", "+rD2.20", "dn2_3", "outs", "gu2_0", "gu2_1",
    "-rD2.00", "gu2_2", "-rD1.01", "-rcU1", "gu2_3", "-rD1.10", "+rD1.11", "+rcU2", "bu_0", "+rD1.02", "+rU1.00",
    "bu_1", "bu_2", "-rD1.20", "bu_3", "-rD1.02", "norm2b", "-rcU2", "+rD1.21", "+rD2.01", "+rU1.20", "ab1_0",
    "-rD1.11", "-rD2.01", "-rD2.10", "-rD2.20", "+rD1.12", "+rD2.02", "+rU1.10", "ab1_1", "-rD1.12", "-rD2.02",
    "+rD2.11", "+rU2.00", "+rU2.20", "ab1_2", "-rU1.20", "-rU1.00", "-rU1.10", "+rU1.01", "-rD1.21", "ab1_3",
    "+rD1.22", "+rD2.21", "+rU1.21", "+rU1.11", "gs1_0", "-rU2.20", "+out", "gs1_1", "-rD2.11", "+rU2.21",
    "gs1_2", "-rU2.00", "gs1_3", "-rD1.22", "-rU1.11", "+rcA1", "+rU2.10", "ab2_0", "-rU1.01", "+rD2.12",
    "+rU1.12", "+rU1.02", "+rU2.01", "ab2_1", "-rU1.21", "ab2_2", "-rcA1", "-rD2.21", "-rU2.21", "+rA1.00",
    "+rA1.10", "+rU1.22", "-rD2.12", "-rU2.10", "-out", "ab2_3", "-rU1.12", "+rU2.22", "gs2_0", "gs2_1",
    "-rU2.01", "+rU2.02", "gs2_2", "-rU1.02", "+rD2.22", "gs2_3", "+rcA2", "+rU2.11", "rb0", "-rA1.10", "-rD2.22",
    "-rU1.22", "-rU2.22", "+cg", "+rA1.11", "tok1", "-rcA2", "-rA1.00", "-rU2.02", "-rU2.11", "+rA2.00",
    "+rA2.10", "tok2", "-cg", "+sc", "+rA2.20", "+rA1.01", "+rU2.12", "-rA1.11", "-sc", "-rA2.10", "+rA2.11",
    "-rU2.12", "+sx", "-rA2.00", "+rA2.01", "-sx", "-rA1.01", "+sy", "+rA1.02", "-rA2.11", "+rA2.12", "+tg",
    "-rA2.12", "-rA2.20", "+rA2.21", "-sy", "+sz", "-rA2.01", "-rA1.02", "+rA2.02", "-rA2.21", "+rA2.22", "-sz",
    "+rA1.12", "-rA2.02", "-tg", "-rA2.22", "-rA1.12",
]


def scatter_shape(rows, order, i):
    rest = [SIZE[d] for d in "yzx" if d in order[i + 1 :]]
    lead = [3] if order[i] == "z" else []
    return tuple(lead + rest + [rows, COLS])


SCATTER_KEYS = [(p, j, i) for p in SCATTER for j in range(len(SCATTER[p])) for i in range(3)]


def fused_kernel(
    tok_in, coef_in, cot_in, wq_ref, wk_ref, wv_ref, wo_ref, wu_ref, wd_ref, mu_ref, sigma_ref, flag_ref, spot_ref,
    gain1_ref, gain2_ref, fita_ref, past_ref,
    out_o, tg_o, cg_o, wg_o, small_o,
    W, G, RC, RS, RZ,
    TOK, COEF, COT, X0, X0T, COTT, N2, N2T, DHL, DHLT, PK, MEM, PR, CTX, HID, ACC, ACT, GP, SMP,
    TK, DQ, DM, SP, SPT, OUTS, ST1, ST2,
    *rest,
):
    bufs = dict(zip(SCATTER_KEYS, rest[: len(SCATTER_KEYS)]))
    send, recv, local = rest[len(SCATTER_KEYS) :]
    sems = Sems(send, recv, local)
    dp, mp = lax.axis_index("dp"), lax.axis_index("mp")
    z, x, y, c = dp // 2, dp % 2, mp // 2, mp % 2
    ox, oy, oc = 1 - x, 1 - y, 1 - c
    z_next = {k: (z + k) % 4 for k in (1, 2, 3)}
    z_prev = {k: (z - k + 4) % 4 for k in (1, 2, 3)}
    m_next = {k: (mp + k) % 4 for k in (1, 2, 3)}
    m_prev = {k: (mp - k + 4) % 4 for k in (1, 2, 3)}
    root = 0.125
    every = slice(None)
    to = {"c": (dp, y * 2 + oc), "y": (dp, oy * 2 + c), "x": (z * 2 + ox, mp)}
    to_mp = {k: (dp, m_next[k]) for k in (1, 2, 3)}
    to_z = {k: (z_next[k] * 2 + x, mp) for k in (1, 2, 3)}

    pending = {}

    def start(name, src, dst, dev):
        s, r = sems.pair(name)
        pltpu.make_async_remote_copy(
            src_ref=src, dst_ref=dst, send_sem=s, recv_sem=r, device_id=dev, device_id_type=MESH
        ).start()

    def wait_recv(name, region, dev):
        s, r = sems.pair(name)
        pltpu.make_async_remote_copy(
            src_ref=region, dst_ref=region, send_sem=s, recv_sem=r, device_id=dev, device_id_type=MESH
        ).wait_recv()

    def drain(group):
        for name in pending.pop(group, []):
            for tag, src, dst, dev, _ in copies(name):
                s, r = sems.pair(name + tag)
                pltpu.make_async_remote_copy(
                    src_ref=src, dst_ref=dst, send_sem=s, recv_sem=r, device_id=dev, device_id_type=MESH
                ).wait_send()

    barrier = pltpu.get_barrier_semaphore()
    for dev in (to_mp[1], to_mp[2], to_mp[3], to["x"], to_z[1], to_z[2], to_z[3]):
        pl.semaphore_signal(barrier, inc=1, device_id=dev, device_id_type=MESH)
    pl.semaphore_wait(barrier, 7)

    GD, GU, GA = G.at[0], G.at[1], W.at[1]
    grads = {0: GA, 1: GU, 2: GD}

    def rows_in(src, dst, n):
        return [
            (str(k), src.at[m_next[k]], dst.at[pl.ds(mp * n, n)], to_mp[k], dst.at[pl.ds(m_prev[k] * n, n)])
            for k in (1, 2, 3)
        ], (src.at[mp], dst.at[pl.ds(mp * n, n)])

    def rows_out(src, dst, n):
        return [
            (str(k), src.at[pl.ds(m_next[k] * n, n)], dst.at[mp], to_mp[k], dst.at[m_prev[k]]) for k in (1, 2, 3)
        ], (src.at[pl.ds(mp * n, n)], dst.at[mp])

    ROWS = {
        "tok": lambda: rows_in(tok_in, TOK, 128),
        "coef": lambda: rows_in(coef_in, COEF, 64),
        "cot": lambda: rows_in(cot_in, COT, 64),
        "out": lambda: rows_out(OUTS, out_o, 64),
        "cg": lambda: rows_out(X0.at[pl.ds(0, 256)], cg_o, 64),
        "tg": lambda: rows_out(X0.at[pl.ds(256, 512)], tg_o, 128),
    }

    def gather_part(name):
        piece, j, i = name[1:3], int(name[4]), int(name[5])
        a, col = PIECES[piece]
        lo, n, order = GATHER[piece][j]
        d = order[i]
        at = {ax: (every if ax in order[:i] else near) for ax, near in (("y", y), ("z", z), ("x", x))}

        def region(cc, **changed):
            use = {**at, **changed}
            return W.at[a, use["y"], cc, use["z"], use["x"], pl.ds(lo, n), pl.ds(col, COLS)]

        def brings(cc):
            if d == "z":
                return [(str(k), region(cc, z=z_prev[k])) for k in (1, 2, 3)]
            return [("", region(cc, **{d: oy if d == "y" else ox}))]

        return d, region(c), brings

    def scatter_part(name):
        piece, j, i = name[1:3], int(name[4]), int(name[5])
        a, col = PIECES[piece]
        lo, n, order = SCATTER[piece][j]
        rest_axes = [ax for ax in "yzx" if ax in order[i + 1 :]]
        return piece, a, col, lo, n, order[i], rest_axes, i, bufs[(piece, j, i)]

    def copies(name):
        if name in ROWS:
            return ROWS[name]()[0]
        if name == "sm":
            return [(str(k), SMP.at[mp], SMP.at[mp], to_mp[k], SMP.at[m_prev[k]]) for k in (1, 2, 3)]
        if name == "sz":
            return [(str(k), RS.at[6], RZ.at[k - 1], to_z[k], RZ.at[k - 1]) for k in (1, 2, 3)]
        if name[0] == "s":
            i = "cxy".index(name[1])
            return [("", RS.at[2 * i], RS.at[2 * i + 1], to[name[1]], RS.at[2 * i + 1])]
        if name.endswith("own"):
            a, col = PIECES[name[1:3]]
            mine = W.at[a, y, c, z, x, every, pl.ds(col, COLS)]
            return [("", mine, mine, to["c"], W.at[a, y, oc, z, x, every, pl.ds(col, COLS)])]
        if name[0] == "g":
            d, src, brings = gather_part(name)
            if d == "z":
                return [(tag, src, src, to_z[int(tag)], region) for tag, region in brings(c)]
            return [("", src, src, to[d], brings(c)[0][1])]
        if name[0] == "p":
            _, _, brings = gather_part(name[1:])
            return [(tag, mine, mine, to["c"], theirs) for (tag, mine), (_, theirs) in zip(brings(c), brings(oc))]
        if name.startswith("rc"):
            a, col = PIECES[name[2:]]
            buf = RC.at[SETS[name[2:]]]
            return [("", grads[a].at[every, oc, every, every, every, pl.ds(col, COLS)], buf, to["c"], buf)]
        piece, a, col, lo, n, d, rest_axes, i, buf = scatter_part(name)
        at = {ax: (every if ax in rest_axes else near) for ax, near in (("y", y), ("z", z), ("x", x))}

        def send(**changed):
            use = {**at, **changed}
            return grads[a].at[use["y"], c, use["z"], use["x"], pl.ds(lo, n), pl.ds(col, COLS)]

        if d == "z":
            return [(str(k), send(z=z_next[k]), buf.at[k - 1], to_z[k], buf.at[k - 1]) for k in (1, 2, 3)]
        return [("", send(**{d: oy if d == "y" else ox}), buf, to[d], buf)]

    def go(name):
        if name[0] == "s" and name not in ("sm", "sz"):
            RS[2 * "cxy".index(name[1])] = small_o[...]
        if name == "sz":
            RS[6] = small_o[...]
        group = name[1:3] if name[0] == "g" else name.strip("pg")[0:2] if name[0] == "p" else "end"
        pending.setdefault(group, []).append(name)
        for tag, src, dst, dev, _ in copies(name):
            start(name + tag, src, dst, dev)
        if name in ROWS:
            src, dst = ROWS[name]()[1]
            pltpu.make_async_copy(src, dst, sems.one(name)).start()

    def got(name):
        for tag, _, _, dev, region in copies(name):
            wait_recv(name + tag, region, dev)
        if name in ROWS:
            src, dst = ROWS[name]()[1]
            pltpu.make_async_copy(src, dst, sems.one(name)).wait()
        if name == "sz":
            small_o[...] = RS[6] + RZ[0] + RZ[1] + RZ[2]
        elif name[0] == "s" and name != "sm":
            small_o[...] = small_o[...] + RS[2 * "cxy".index(name[1]) + 1]
        elif name.startswith("rc"):
            core_sum(name[2:])
        elif name[0] == "r":
            stage_sum(name)

    def core_sum(piece):
        a, col = PIECES[piece]
        g, s = grads[a], SETS[piece]

        def add(q, carry):
            at = (q // 8, c, (q // 2) % 4, q % 2, every, pl.ds(col, COLS))
            g[at] = g[at] + RC[s, q // 8, (q // 2) % 4, q % 2]
            return carry

        lax.fori_loop(0, 16, add, 0)

    def stage_sum(name):
        piece, a, col, lo, n, d, rest_axes, i, buf = scatter_part(name)
        g, rows, cols = grads[a], pl.ds(lo, n), pl.ds(col, COLS)
        if i == 2:
            total = g[y, c, z, x, rows, cols].astype(f32)
            for part in [buf[k] for k in range(3)] if d == "z" else [buf[...]]:
                total = total + part.astype(f32)
            wg_o[a, rows, cols] = total
            return

        def add(q, carry):
            at = {"y": y, "z": z, "x": x}
            left = q
            for ax in reversed(rest_axes):
                at[ax] = left % SIZE[ax]
                left = left // SIZE[ax]
            inner = tuple(at[ax] for ax in rest_axes)
            here = (at["y"], c, at["z"], at["x"], rows, cols)
            if d == "z":
                total = g[here].astype(f32)
                for k in range(3):
                    total = total + buf[(k,) + inner].astype(f32)
                g[here] = total.astype(bf16)
            else:
                g[here] = g[here] + buf[inner]
            return carry

        lax.fori_loop(0, math.prod(SIZE[ax] for ax in rest_axes), add, 0)

    width_rbf = 1.0 / NB
    cen = (lax.broadcasted_iota(jnp.int32, (1, NB), 1).astype(f32) + 0.5) / NB
    present = flag_ref[mp].astype(f32)
    g1 = gain1_ref[...].astype(f32).reshape(1, 768)
    g2 = gain2_ref[...].astype(f32).reshape(1, 768)

    def weight(a, m, col=0, n=768):
        return W[a, m // 2, m % 2, :, :, :, col : col + n].reshape(768, n)

    def pack():
        wot = wo_ref[...].astype(f32).T
        for i, ref in enumerate((wq_ref, wk_ref, wv_ref)):
            W[0, y, c, z, x, :, i * 128 : i * 128 + 128] = ref[:, 0:128]
            tail = jnp.concatenate([ref[:, 128:192].astype(f32), wot[:, i * 64 : i * 64 + 64]], axis=1)
            W[0, y, c, z, x, :, 384 + i * 128 : 512 + i * 128] = tail.astype(bf16)

    def packud():
        W[1, y, c, z, x] = wu_ref[...]
        W[2, y, c, z, x] = wd_ref[...]
        SMP[mp, 0:3, :] = mu_ref[...].astype(f32)
        SMP[mp, 3:6, :] = sigma_ref[...].astype(f32)
        SMP[mp, 6:8, :] = jnp.zeros((2, 256), f32)
        go("sm")

    def sticky():
        cen_down = (lax.broadcasted_iota(jnp.int32, (NB, 1), 0).astype(f32) + 0.5) / NB
        spots = (spot_ref[pl.ds(mp, 1), :].astype(f32) + 0.5) / (2 * SEGMENT_TOKENS)
        samples = jnp.exp(-((spots - cen_down) ** 2) / (2.0 * width_rbf * width_rbf))
        fit = lax.dot_general(
            fita_ref[...], samples, (((1,), (1,)), ((), ())), precision=highest, preferred_element_type=f32
        )
        SP[:, 0:256] = fit.astype(bf16)
        SP[:, 256:512] = past_ref[...]
        SPT[0:256, :] = fit.T.astype(bf16)
        SPT[256:512, :] = past_ref[...].astype(f32).T.astype(bf16)

    def norm1():
        def one(i, carry):
            rows = pl.ds(pl.multiple_of(i * 128, 128), 128)
            v = TOK[rows, :].astype(f32)
            mean = jnp.mean(v, axis=-1, keepdims=True)
            centred = v - mean
            inv = lax.rsqrt(jnp.mean(centred * centred, axis=-1, keepdims=True) + epsilon)
            ST1[rows, 0:1] = mean
            ST1[rows, 1:2] = inv
            X0[pl.ds(pl.multiple_of(256 + i * 128, 128), 128), :] = (centred * inv * g1).astype(bf16)
            return carry

        lax.fori_loop(0, 4, one, 0)

    def x0():
        X0[0:256, :] = (COEF[...].astype(f32) * present).astype(bf16)
        got("sm")

    def x0t():
        for r in range(3):
            X0T[:, r * 256 : (r + 1) * 256] = X0[r * 256 : (r + 1) * 256, :].astype(f32).T.astype(bf16)

    def project(m, col):
        w = weight(0, m, col, COLS)
        for r in range(3):
            PK[m, r * 256 : r * 256 + 256, col : col + COLS] = nn(X0[r * 256 : r * 256 + 256, :], w).astype(bf16)

    def memory(m, first, col):
        MEM[m, :, col : col + 256] = nn(SP[...], PK[m, 0:512, first : first + 256]).astype(bf16)

    lane = lax.broadcasted_iota(jnp.int32, (256, 128), 1)
    row_i = lax.broadcasted_iota(jnp.int32, (256, 512), 0)
    col_i = lax.broadcasted_iota(jnp.int32, (256, 512), 1)
    upper = lane >= 64

    def head_blocks(h):
        return (0, 1, 2, 0, 128) if h < 2 else (3, 4, 5, 256, 384)

    def own_lanes(h):
        return upper if h == 1 else jnp.logical_not(upper)

    def head_query(m, h):
        qb = head_blocks(h)[0]
        q = PK[m, 512:768, qb * 128 : qb * 128 + 128].astype(f32)
        return jnp.where(own_lanes(h), q * root, 0.0).astype(bf16)

    def logits(m, h, qm):
        ms = nt(qm, MEM[m, :, head_blocks(h)[3] : head_blocks(h)[3] + 128])
        mu = SMP[m, h : h + 1, :]
        sg = SMP[m, 3 + h : 4 + h, :]
        mul = jnp.sum(ms * mu, axis=-1, keepdims=True)
        sil = jnp.sum(ms * sg, axis=-1, keepdims=True)
        mean = 1.0 / (1.0 + jnp.exp(-mul))
        soft = jnp.maximum(sil, 0.0) + jnp.log1p(jnp.exp(-jnp.abs(sil)))
        spread = soft * spread_scale + width_rbf * width_rbf
        dist = mean - cen
        reach = width_rbf * lax.rsqrt(spread) * jnp.exp(-dist * dist / (2.0 * spread))
        return ms, mu, sg, sil, mean, spread, dist, reach

    def attend(m, heads):
        for h in heads:
            qb, kb, vb, mk0, mv0 = head_blocks(h)
            qm = head_query(m, h)
            s = nt(qm, PK[m, 256:768, kb * 128 : kb * 128 + 128])
            s = jnp.where(col_i - 256 <= row_i, s, -1e30)
            top = jnp.max(s, axis=-1, keepdims=True)
            e = jnp.exp(s - top)
            p = (e * (1.0 / jnp.sum(e, axis=-1, keepdims=True))).astype(bf16)
            PR[m, h] = p
            ctx = nn(p, PK[m, 256:768, vb * 128 : vb * 128 + 128])
            reach = logits(m, h, qm)[-1]
            ctx = ctx + nn(reach.astype(bf16), MEM[m, :, mv0 : mv0 + 128])
            if h != 1:
                ctx = pltpu.roll(ctx, 64, 1)
            CTX[m, :, h * 128 : h * 128 + 128] = jnp.where(upper, ctx, 0.0).astype(bf16)

    def attnout():
        HID[...] = TOK[256:512, :].astype(f32)

        def one(m, carry):
            HID[...] += nt(CTX[m], weight(0, m, 384, 384))
            return carry

        lax.fori_loop(0, 4, one, 0)

    def norm2():
        hid = HID[...]
        mean = jnp.mean(hid, axis=-1, keepdims=True)
        centred = hid - mean
        inv = lax.rsqrt(jnp.mean(centred * centred, axis=-1, keepdims=True) + epsilon)
        ST2[:, 0:1] = mean
        ST2[:, 1:2] = inv
        normed = centred * inv * g2
        N2[...] = normed.astype(bf16)
        N2T[...] = normed.T.astype(bf16)
        ACC[...] = hid

    def up(m, col):
        cols = slice(col, col + COLS)
        u = nn(N2[...], weight(1, m, col, COLS))
        u2 = u * u
        th = jnp.tanh(gelu_coef * (u + 0.044715 * u2 * u))
        ACT[m, :, cols] = (0.5 * u * (1.0 + th)).astype(bf16)
        GP[m, :, cols] = 0.5 * (1.0 + th) + (0.5 * gelu_coef) * u * (1.0 - th * th) * (1.0 + 0.134145 * u2)

    def cott():
        COTT[...] = COT[...].astype(f32).T.astype(bf16)

    def put(g, m, col, left, right):
        def one(zz, carry):
            rows = pl.ds(pl.multiple_of(zz * 192, 64), 192)
            val = nn(left[rows, :], right)
            g[m // 2, m % 2, zz, :, :, col : col + COLS] = val.reshape(2, 96, COLS).astype(bf16)
            return carry

        lax.fori_loop(0, 4, one, 0)

    def grad_down(m, col):
        put(GD, m, col, COTT, ACT[m, :, col : col + COLS])

    def down(m, col):
        cols = slice(col, col + COLS)
        wd = weight(2, m, col, COLS)
        ACC[...] += nt(ACT[m, :, cols], wd)
        d_act = nn(COT[...], wd)
        ACT[m, :, cols] = (d_act * GP[m, :, cols]).astype(bf16)

    def outs():
        OUTS[...] = ACC[...].astype(bf16)
        ACC[...] = jnp.zeros_like(ACC)

    def grad_up(m, col):
        put(GU, m, col, N2T, ACT[m, :, col : col + COLS])

    def back_up(m):
        ACC[...] += nt(ACT[m], weight(1, m))

    def norm2b():
        d_n2 = ACC[...]
        flat = (HID[...] - ST2[:, 0:1]) * ST2[:, 1:2]
        g2_grad = jnp.sum(d_n2 * flat, axis=0, keepdims=True)
        e = d_n2 * g2
        d_hidden = COT[...].astype(f32) + ST2[:, 1:2] * (
            e - jnp.mean(e, axis=-1, keepdims=True) - flat * jnp.mean(e * flat, axis=-1, keepdims=True)
        )
        HID[...] = d_hidden
        DHL[...] = d_hidden.astype(bf16)
        DHLT[...] = d_hidden.T.astype(bf16)
        for i in range(3):
            small_o[27 + i : 28 + i, :] = g2_grad[:, i * 256 : (i + 1) * 256]

    def attend_back(m, heads):
        d_ctx = nn(DHL[...], weight(0, m, 384 + 128 * heads[0], 128 * len(heads)))
        for h in heads:
            qb, kb, vb, mk0, mv0 = head_blocks(h)
            qm = head_query(m, h)
            at = 128 * (h - heads[0])
            dc = d_ctx[:, at : at + 128]
            if h != 1:
                dc = pltpu.roll(dc, 64, 1)
            dc = jnp.where(own_lanes(h), dc, 0.0).astype(bf16)
            p = PR[m, h]
            kv = PK[m, 256:768, kb * 128 : kb * 128 + 128]
            d_p = nt(dc, PK[m, 256:768, vb * 128 : vb * 128 + 128])
            pf = p.astype(f32)
            t = pf * d_p
            d_s = (t - pf * jnp.sum(t, axis=-1, keepdims=True)).astype(bf16)
            d_v = tn(p, dc)
            d_k = tn(d_s, qm)
            mkv = MEM[m, :, mk0 : mk0 + 128]
            ms, mu, sg, sil, mean, spread, dist, reach = logits(m, h, qm)
            d_r = nt(dc, MEM[m, :, mv0 : mv0 + 128])
            d_mv = tn(reach.astype(bf16), dc)
            t = d_r * reach
            td = t * dist
            inv_s = 1.0 / spread
            g_mean = -jnp.sum(td, axis=-1, keepdims=True) * inv_s
            g_s = (jnp.sum(td * dist, axis=-1, keepdims=True) * inv_s - jnp.sum(t, axis=-1, keepdims=True)) * (
                0.5 * inv_s
            )
            g_mu = g_mean * mean * (1.0 - mean)
            g_sg = g_s * spread_scale * (1.0 / (1.0 + jnp.exp(-sil)))
            d_ms = (g_mu * mu + g_sg * sg).astype(bf16)
            small_o[pl.ds(m * 3 + h, 1), :] = jnp.sum(g_mu * ms, axis=0, keepdims=True)
            small_o[pl.ds(12 + m * 3 + h, 1), :] = jnp.sum(g_sg * ms, axis=0, keepdims=True)
            d_mk = tn(d_ms, qm)
            d_q = (nn(d_s, kv) + nn(d_ms, mkv)) * root
            d_q = jnp.where(own_lanes(h), d_q, 0.0)
            j = 0 if h < 2 else 1
            if h == 1:
                TK[0] += d_k
                TK[1] += d_v
                DQ[0] += d_q
                DM[:, 0:128] += d_mk.astype(bf16)
                DM[:, 128:256] += d_mv.astype(bf16)
            else:
                TK[2 * j] = d_k
                TK[2 * j + 1] = d_v
                DQ[j] = d_q
                DM[:, 256 * j : 256 * j + 128] = d_mk.astype(bf16)
                DM[:, 256 * j + 128 : 256 * j + 256] = d_mv.astype(bf16)
        j = 0 if heads[0] == 0 else 1
        first = 384 * j + 128
        back = nn(SPT[...], DM[:, 256 * j : 256 * j + 256])
        for i in range(2):
            b = back[:, 128 * i : 128 * i + 128]
            cols = slice(first + 128 * i, first + 128 * i + 128)
            PK[m, 0:256, cols] = (b[0:256] * present).astype(bf16)
            PK[m, 256:512, cols] = (TK[2 * j + i, 0:256] + b[256:512]).astype(bf16)
            PK[m, 512:768, cols] = TK[2 * j + i, 256:512].astype(bf16)
        qcols = slice(384 * j, 384 * j + 128)
        PK[m, 0:512, qcols] = jnp.zeros((512, 128), bf16)
        PK[m, 512:768, qcols] = DQ[j].astype(bf16)

    def grad_square(m, col):
        def one(zz, carry):
            rows = pl.ds(pl.multiple_of(zz * 192, 64), 192)
            val = nn(X0T[rows, :], PK[m, :, col : col + COLS])
            if col:
                val = val + nn(DHLT[rows, :], CTX[m])
            GA[m // 2, m % 2, zz, :, :, col : col + COLS] = val.reshape(2, 96, COLS).astype(bf16)
            return carry

        lax.fori_loop(0, 4, one, 0)

    def rows_back(r):
        ACC[...] = jnp.zeros_like(ACC)

        def one(m, carry):
            ACC[...] += nt(PK[m, r * 256 : (r + 1) * 256, :], weight(0, m))
            return carry

        lax.fori_loop(0, 4, one, 0)

    def token_rows(r, first, extra):
        rows_back(r)
        d_n1 = ACC[...]
        rows = slice(first, first + 256)
        inv_1 = ST1[rows, 1:2]
        flat_1 = (TOK[rows, :].astype(f32) - ST1[rows, 0:1]) * inv_1
        part = jnp.sum(d_n1 * flat_1, axis=0, keepdims=True)
        e = d_n1 * g1
        grad = inv_1 * (
            e - jnp.mean(e, axis=-1, keepdims=True) - flat_1 * jnp.mean(e * flat_1, axis=-1, keepdims=True)
        )
        if extra:
            grad = grad + HID[...]
        X0[256 + first : 512 + first, :] = grad.astype(bf16)
        return part

    def rb0():
        rows_back(0)
        X0[0:256, :] = ACC[...].astype(bf16)

    def tok1():
        part = token_rows(1, 0, False)
        for i in range(3):
            small_o[24 + i : 25 + i, :] = part[:, i * 256 : (i + 1) * 256]

    def tok2():
        part = token_rows(2, 256, True)
        for i in range(3):
            small_o[24 + i : 25 + i, :] = small_o[24 + i : 25 + i, :] + part[:, i * 256 : (i + 1) * 256]
        small_o[30:32, :] = jnp.zeros((2, 256), f32)

    single = {
        "pack": pack, "packud": packud, "sticky": sticky, "norm1": norm1, "x0": x0, "x0t": x0t, "attnout": attnout,
        "norm2": norm2, "cott": cott, "outs": outs, "norm2b": norm2b, "rb0": rb0, "tok1": tok1, "tok2": tok2,
    }
    looped = {
        "pj1": lambda m: project(m, 0), "pj2": lambda m: project(m, COLS),
        "mem1": lambda m: memory(m, 128, 0), "mem2": lambda m: memory(m, 512, 256),
        "at1": lambda m: attend(m, (0, 1)), "at2": lambda m: attend(m, (2,)),
        "up1": lambda m: up(m, 0), "up2": lambda m: up(m, COLS),
        "gd1": lambda m: grad_down(m, 0), "gd2": lambda m: grad_down(m, COLS),
        "dn1": lambda m: down(m, 0), "dn2": lambda m: down(m, COLS),
        "gu1": lambda m: grad_up(m, 0), "gu2": lambda m: grad_up(m, COLS), "bu": back_up,
        "ab1": lambda m: attend_back(m, (0, 1)), "ab2": lambda m: attend_back(m, (2,)),
        "gs1": lambda m: grad_square(m, 0), "gs2": lambda m: grad_square(m, COLS),
    }

    def transfer(item):
        if item[0] == "+":
            go(item[1:])
        else:
            got(item[1:])

    at = 0
    while at < len(SCHEDULE):
        item = SCHEDULE[at]
        at += 1
        if item[0] in "+-":
            transfer(item)
        elif item in single:
            single[item]()
        else:
            family = item[:-2]
            if family == "gs1":
                drain("U1")
                drain("U2")
            between = {}
            done = 0
            while done < 3:
                nxt = SCHEDULE[at]
                at += 1
                if nxt[0] in "+-":
                    between.setdefault(done, []).append(nxt)
                else:
                    done += 1

            def step(m, carry, family=family, between=between):
                looped[family](m)
                for i, items in between.items():

                    @pl.when(m == i)
                    def _(items=items):
                        for one in items:
                            transfer(one)

                return carry

            lax.fori_loop(0, 4, step, 0)
    for group in list(pending):
        drain(group)


def finish_kernel(
    out_b, tg_b, cg_b, wg, sums, out, tg, cg, g1, gq, gk, gv, go, gm, gs, g2, gu, gd,
):
    me = lax.axis_index("mp")
    out[...] = out_b[...]
    tg[...] = tg_b[...].astype(f32)
    cg[...] = cg_b[...].astype(f32)
    for i, ref in enumerate((gq, gk, gv)):
        ref[:, 0:128] = wg[0, :, 128 * i : 128 * i + 128]
        block = wg[0, :, 384 + 128 * i : 512 + 128 * i]
        ref[:, 128:192] = block[:, 0:64]
        go[64 * i : 64 * i + 64, :] = block.T[64:128, :]
    gu[...] = wg[1]
    gd[...] = wg[2]
    for h in range(3):
        gm[h : h + 1, :] = sums[pl.ds(me * 3 + h, 1), :]
        gs[h : h + 1, :] = sums[pl.ds(12 + me * 3 + h, 1), :]
    for i in range(3):
        g1[pl.ds(i * 256, 256)] = sums[24 + i]
        g2[pl.ds(i * 256, 256)] = sums[27 + i]


def fused_call(*args):
    any_ = pl.BlockSpec(memory_space=pl.ANY)
    vm = pl.BlockSpec(memory_space=pltpu.VMEM)
    sm = pl.BlockSpec(memory_space=pltpu.SMEM)
    V = pltpu.VMEM
    return pl.pallas_call(
        fused_kernel,
        out_shape=(
            jax.ShapeDtypeStruct((4, 64, 768), bf16),
            jax.ShapeDtypeStruct((4, 128, 768), bf16),
            jax.ShapeDtypeStruct((4, 64, 768), bf16),
            jax.ShapeDtypeStruct((3, 96, 768), f32),
            jax.ShapeDtypeStruct((32, 256), f32),
        ),
        in_specs=[any_] * 3 + [vm] * 8 + [sm] + [vm] * 5,
        out_specs=(any_, any_, any_, vm, vm),
        scratch_shapes=[
            V((3, 2, 2, 4, 2, 96, 768), bf16),
            V((2, 2, 2, 4, 2, 96, 768), bf16),
            V((4, 2, 4, 2, 96, COLS), bf16),
            V((7, 32, 256), f32),
            V((3, 32, 256), f32),
            V((512, 768), bf16),
            V((256, 768), bf16),
            V((256, 768), bf16),
            V((768, 768), bf16),
            V((768, 768), bf16),
            V((768, 256), bf16),
            V((256, 768), bf16),
            V((768, 256), bf16),
            V((256, 768), bf16),
            V((768, 256), bf16),
            V((4, 768, 768), bf16),
            V((4, 256, 512), bf16),
            V((4, 3, 256, 512), bf16),
            V((4, 256, 384), bf16),
            V((256, 768), f32),
            V((256, 768), f32),
            V((4, 256, 768), bf16),
            V((4, 256, 768), f32),
            V((4, 8, 256), f32),
            V((4, 512, 128), f32),
            V((2, 256, 128), f32),
            V((256, 512), bf16),
            V((256, 512), bf16),
            V((512, 256), bf16),
            V((256, 768), bf16),
            V((512, 128), f32),
            V((256, 128), f32),
            *(V(scatter_shape(SCATTER[p][j][1], SCATTER[p][j][2], i), bf16) for p, j, i in SCATTER_KEYS),
            pltpu.SemaphoreType.DMA((PAIRS,)),
            pltpu.SemaphoreType.DMA((PAIRS,)),
            pltpu.SemaphoreType.DMA((LOCALS,)),
        ],
        compiler_params=pltpu.CompilerParams(
            collective_id=0, has_side_effects=True, vmem_limit_bytes=63 * 1024 * 1024
        ),
    )(*args)


def fused_body(
    tokens, coeffs, present_flag, sticky_pos, gain_one, w_query, w_key, w_value, w_out, mu_weight,
    sigma_weight, gain_two, w_up, w_down, cotangent,
):
    _, fitting = basis_tables(NB, SEGMENT_TOKENS)
    fita = jnp.asarray(fitting[:, :SEGMENT_TOKENS])
    past = jnp.asarray(fitting[:, SEGMENT_TOKENS:]).astype(bf16)
    parts = fused_call(
        tokens, coeffs, cotangent, w_query, w_key, w_value, w_out, w_up, w_down.T, mu_weight, sigma_weight,
        present_flag, sticky_pos, gain_one, gain_two, fita, past,
    )

    def like(v):
        return jax.ShapeDtypeStruct(v.shape, f32)

    shapes = (
        jax.ShapeDtypeStruct(cotangent.shape, bf16), like(tokens), like(coeffs), like(gain_one), like(w_query),
        like(w_key), like(w_value), like(w_out), like(mu_weight), like(sigma_weight), like(gain_two), like(w_up),
        like(w_down.T),
    )
    vm = pl.BlockSpec(memory_space=pltpu.VMEM)
    done = pl.pallas_call(
        finish_kernel, out_shape=shapes, in_specs=[vm] * 5, out_specs=(vm,) * 13,
    )(*parts)
    return (*done[:12], done[12].T)


def solution(mesh):
    in_specs = (
        P("dp", "mp", None), P("dp", "mp", None), P("dp"), P("dp", None), P(), P("dp", "mp"), P("dp", "mp"),
        P("dp", "mp"), P("mp", "dp"), P("mp", None), P("mp", None), P(), P("dp", "mp"), P("mp", "dp"),
        P("dp", "mp", None),
    )
    out_specs = (
        P("dp", "mp", None), P("dp", "mp", None), P("dp", "mp", None), P(), P("dp", "mp"), P("dp", "mp"),
        P("dp", "mp"), P("mp", "dp"), P("mp", None), P("mp", None), P(), P("dp", "mp"), P("mp", "dp"),
    )
    whole = body
    if mesh.shape["dp"] == 8 and mesh.shape["mp"] == 4:
        whole = fused_body
    return jax.shard_map(whole, mesh=mesh, in_specs=in_specs, out_specs=out_specs, check_vma=False)
```

```python
import math

import jax
import jax.numpy as jnp
import numpy as np
from jax import lax
from jax.experimental import pallas as pl
from jax.experimental.pallas import tpu as pltpu
from jax.sharding import PartitionSpec as P

HD = 64
NB = 256
SEGMENT_TOKENS = 256
BOTH = ("dp", "mp")

highest = lax.Precision.HIGHEST
epsilon = 1e-05
ridge = 0.5
spread_scale = 1.0 / 64.0
gelu_coef = 0.7978845608028654


def basis_tables(basis_count, seg_len):
    centers = (np.arange(basis_count) + 0.5) / basis_count
    width = 1.0 / basis_count
    times = (np.arange(2 * seg_len) + 0.5) / (2 * seg_len)
    design = np.exp(-((times[:, None] - centers[None, :]) ** 2) / (2.0 * width * width))
    normal = design.T @ design + ridge * np.eye(basis_count)
    fitting = np.linalg.solve(normal, design.T)
    return centers.astype(np.float32), fitting.astype(np.float32)


def norm_rows(values):
    centered = values - jnp.mean(values, axis=-1, keepdims=True)
    inverse = lax.rsqrt(jnp.mean(centered * centered, axis=-1, keepdims=True) + epsilon)
    return (centered * inverse, inverse)


def gelu_tanh(values):
    return (
        0.5 * values * (1.0 + jnp.tanh(gelu_coef * (values + 0.044715 * values * values * values)))
    )


def memory_reach(mem_scores, mu_in, sigma_in, centers):
    rbf_width = 1.0 / centers.shape[0]
    mu_logit = jnp.einsum("...hn,hn->...h", mem_scores, mu_in, precision=highest)
    sigma_logit = jnp.einsum("...hn,hn->...h", mem_scores, sigma_in, precision=highest)
    mean_pos = jax.nn.sigmoid(mu_logit)
    spread = jax.nn.softplus(sigma_logit) * spread_scale + rbf_width * rbf_width
    distance = mean_pos[..., None] - centers
    return (
        rbf_width
        * lax.rsqrt(spread)[..., None]
        * jnp.exp(-distance * distance / (2.0 * spread[..., None]))
    )


def mm(pattern, left_in, right_in):
    return jnp.einsum(pattern, left_in, right_in, preferred_element_type=jnp.float32)


def norm_back(grad, flat_rows, inverse, gain_vec):
    scaled = grad * gain_vec
    return inverse * (
        scaled
        - jnp.mean(scaled, axis=-1, keepdims=True)
        - flat_rows * jnp.mean(scaled * flat_rows, axis=-1, keepdims=True)
    )


def low(v):
    return v.astype(jnp.bfloat16)


def whole_sequences(
    tokens, coeffs, present_flag, sticky_pos, gain_one, wq, wk, wv, wo, mu, sigma, gain_two, wu, wdt, cot
):
    count, length, width = tokens.shape
    cur = cot.shape[1]
    past = length - cur
    heads = width // HD
    root = math.sqrt(HD)
    centers, fitting = basis_tables(NB, SEGMENT_TOKENS)
    rbf_width = 1.0 / NB
    past_fit = jnp.asarray(fitting[:, SEGMENT_TOKENS:]).astype(jnp.bfloat16)
    centers = jnp.asarray(centers)
    g1 = gain_one.astype(jnp.float32)
    g2 = gain_two.astype(jnp.float32)
    mu = mu.astype(jnp.float32)
    sigma = sigma.astype(jnp.float32)
    causal = jnp.arange(length)[None, :] <= (past + jnp.arange(cur))[:, None]
    present = present_flag.astype(jnp.float32)[:, None, None]
    spots = (sticky_pos.astype(jnp.float32) + 0.5) / (2 * SEGMENT_TOKENS)
    samples = jnp.exp(-((spots[:, :, None] - centers) ** 2) / (2.0 * rbf_width * rbf_width))
    sticky = low(
        jnp.einsum("nm,bmk->bnk", jnp.asarray(fitting[:, :SEGMENT_TOKENS]), samples, precision=highest)
    )
    rows = tokens.astype(jnp.float32)
    flat_one, inv_one = norm_rows(rows)
    normed = low(flat_one * g1)
    q = low(mm("bld,de->ble", normed[:, past:], wq))
    k = low(mm("bld,de->ble", normed, wk))
    v = low(mm("bld,de->ble", normed, wv))
    ck = low(present * mm("bnd,de->bne", coeffs, wk))
    cv = low(present * mm("bnd,de->bne", coeffs, wv))
    mk = low(mm("bnm,bme->bne", sticky, ck) + mm("np,bpe->bne", past_fit, k[:, :past]))
    mv = low(mm("bnm,bme->bne", sticky, cv) + mm("np,bpe->bne", past_fit, v[:, :past]))
    qh = q.reshape(count, cur, heads, HD)
    kh = k.reshape(count, length, heads, HD)
    vh = v.reshape(count, length, heads, HD)
    mkh = mk.reshape(count, NB, heads, HD)
    mvh = mv.reshape(count, NB, heads, HD)
    scores = mm("bqhd,bkhd->bhqk", qh, kh) / root
    masked = jnp.where(causal, scores, -1e30)
    probs = jax.nn.softmax(masked, axis=-1)
    probs_low = low(probs)
    short = mm("bhqk,bkhd->bqhd", probs_low, vh)
    mem_scores = mm("bqhd,bnhd->bqhn", qh, mkh) / root

    def reach_of(s, m, g):
        return memory_reach(s, m, g, centers)

    reach, reach_pull = jax.vjp(reach_of, mem_scores, mu, sigma)
    reach_low = low(reach)
    long_part = mm("bqhn,bnhd->bqhd", reach_low, mvh)
    context = low((short + long_part).reshape(count, cur, width))
    hidden = rows[:, past:] + mm("bqd,de->bqe", context, wo)
    flat_two, inv_two = norm_rows(hidden)
    normed_two = low(flat_two * g2)
    up = mm("bqd,df->bqf", normed_two, wu)
    active_rows, gelu_pull = jax.vjp(gelu_tanh, up)
    active = low(active_rows)
    output = low(hidden + mm("bqf,df->bqd", active, wdt))
    wdt_grad = mm("bqd,bqf->df", cot, active)
    d_up = low(gelu_pull(mm("bqd,df->bqf", cot, wdt))[0])
    wu_grad = mm("bqd,bqf->df", normed_two, d_up)
    d_n2 = mm("bqf,df->bqd", d_up, wu)
    g2_grad = jnp.sum(d_n2 * flat_two, axis=(0, 1))
    d_hidden = cot.astype(jnp.float32) + norm_back(d_n2, flat_two, inv_two, g2)
    d_hidden_low = low(d_hidden)
    wo_grad = mm("bqd,bqe->de", context, d_hidden_low)
    d_context = low(mm("bqe,de->bqd", d_hidden_low, wo)).reshape(count, cur, heads, HD)
    d_probs = mm("bqhd,bkhd->bhqk", d_context, vh)
    d_scores = low(probs * (d_probs - jnp.sum(probs * d_probs, axis=-1, keepdims=True)))
    d_reach = mm("bqhd,bnhd->bqhn", d_context, mvh)
    d_mv = low(mm("bqhn,bqhd->bnhd", reach_low, d_context)).reshape(count, NB, width)
    d_ms, mu_grad, sigma_grad = reach_pull(d_reach)
    d_ms = low(d_ms)
    dq = low(
        (mm("bhqk,bkhd->bqhd", d_scores, kh) + mm("bqhn,bnhd->bqhd", d_ms, mkh)) / root
    ).reshape(count, cur, width)
    d_mk = low(mm("bqhn,bqhd->bnhd", d_ms, qh) / root).reshape(count, NB, width)
    keep = present_flag.astype(jnp.bfloat16)[:, None, None]
    d_ck = low(mm("bnm,bne->bme", sticky, d_mk)) * keep
    d_cv = low(mm("bnm,bne->bme", sticky, d_mv)) * keep
    dk = (mm("bhqk,bqhd->bkhd", d_scores, qh) / root).reshape(count, length, width)
    dv = mm("bhqk,bqhd->bkhd", probs_low, d_context).reshape(count, length, width)
    pad = ((0, 0), (0, cur), (0, 0))
    dk = low(dk + jnp.pad(mm("np,bne->bpe", past_fit, d_mk), pad))
    dv = low(dv + jnp.pad(mm("np,bne->bpe", past_fit, d_mv), pad))
    wq_grad = mm("bqd,bqe->de", normed[:, past:], dq)
    wk_grad = mm("bld,ble->de", normed, dk) + mm("bnd,bne->de", coeffs, d_ck)
    wv_grad = mm("bld,ble->de", normed, dv) + mm("bnd,bne->de", coeffs, d_cv)
    d_n1 = mm("ble,de->bld", dk, wk) + mm("ble,de->bld", dv, wv)
    d_n1 = d_n1 + jnp.pad(mm("bqe,de->bqd", dq, wq), ((0, 0), (past, 0), (0, 0)))
    coeff_grad = mm("bne,de->bnd", d_ck, wk) + mm("bne,de->bnd", d_cv, wv)
    g1_grad = jnp.sum(d_n1 * flat_one, axis=(0, 1))
    token_grad = norm_back(d_n1, flat_one, inv_one, g1) + jnp.pad(
        d_hidden, ((0, 0), (past, 0), (0, 0))
    )
    return (
        output, token_grad, coeff_grad, g1_grad, wq_grad, wk_grad, wv_grad, wo_grad,
        mu_grad, sigma_grad, g2_grad, wu_grad, wdt_grad,
    )


def to_sequences(rows):
    return lax.all_to_all(rows, "mp", 0, 1, tiled=True)


def to_rows(rows):
    return lax.all_to_all(rows, "mp", 1, 0, tiled=True)


def body(
    tokens, coeffs, present_flag, sticky_pos, gain_one, w_query, w_key, w_value, w_out, mu_weight,
    sigma_weight, gain_two, w_up, w_down, cotangent,
):
    dp, mp = lax.axis_size("dp"), lax.axis_size("mp")
    me = lax.axis_index("mp")
    count = tokens.shape[0] // mp
    depth, share = w_query.shape
    inner = w_up.shape[1]
    width = depth * dp
    seq_tokens = to_sequences(tokens)
    seq_coeffs = to_sequences(coeffs)
    seq_cot = to_sequences(cotangent)
    flags = lax.dynamic_slice_in_dim(present_flag, me * count, count, 0)
    spots = lax.dynamic_slice_in_dim(sticky_pos, me * count, count, 0)
    heads_local = mu_weight.shape[0]
    mu, sigma = lax.all_gather((mu_weight, sigma_weight), "mp", axis=0, tiled=True)
    square = jnp.concatenate([w_query, w_key, w_value, w_out.T], axis=1)
    packed = jnp.concatenate([square, w_up, w_down.T], axis=1)
    whole = lax.all_gather(packed, BOTH, axis=0, tiled=False)
    whole = whole.reshape(dp, mp, depth, packed.shape[1]).transpose(0, 2, 1, 3)
    whole = whole.reshape(width, mp, packed.shape[1])

    def columns(first, size):
        return whole[:, :, first : first + size].reshape(width, mp * size)

    wq, wk, wv, wot = (columns(i * share, share) for i in range(4))
    wu = columns(4 * share, inner)
    wdt = columns(4 * share + inner, inner)
    (
        output, token_grad, coeff_grad, g1_grad, wq_grad, wk_grad, wv_grad, wo_grad,
        mu_grad, sigma_grad, g2_grad, wu_grad, wdt_grad,
    ) = whole_sequences(
        seq_tokens, seq_coeffs, flags, spots, gain_one, wq, wk, wv, wot.T, mu, sigma, gain_two, wu, wdt, seq_cot
    )

    def blocks(grad):
        return low(grad).reshape(dp, depth, mp, grad.shape[1] // mp).transpose(0, 2, 1, 3)

    def scatter(grad):
        stacked = blocks(grad)
        stacked = stacked.reshape((dp * mp * depth, stacked.shape[3]))
        return lax.psum_scatter(stacked, BOTH, scatter_dimension=0, tiled=True).astype(jnp.float32)

    wdt_own = scatter(wdt_grad)
    wu_own = scatter(wu_grad)
    square_own = scatter(
        jnp.concatenate(
            [g.reshape(width, mp, share) for g in (wq_grad, wk_grad, wv_grad, wo_grad.T)], axis=2
        ).reshape(width, mp * 4 * share)
    )
    small = lax.psum((mu_grad, sigma_grad, g1_grad, g2_grad), BOTH)
    mu_own = lax.dynamic_slice_in_dim(small[0], me * heads_local, heads_local, 0)
    sigma_own = lax.dynamic_slice_in_dim(small[1], me * heads_local, heads_local, 0)
    return (
        to_rows(output),
        to_rows(low(token_grad)).astype(jnp.float32),
        to_rows(low(coeff_grad)).astype(jnp.float32),
        small[2],
        square_own[:, :share],
        square_own[:, share : 2 * share],
        square_own[:, 2 * share : 3 * share],
        square_own[:, 3 * share :].T,
        mu_own,
        sigma_own,
        small[3],
        wu_own,
        wdt_own.T,
    )


f32 = jnp.float32
bf16 = jnp.bfloat16
MESH = pl.DeviceIdType.MESH


def nn(a, b):
    return jnp.dot(a, b, preferred_element_type=f32)


def nt(a, b):
    return lax.dot_general(a, b, (((1,), (1,)), ((), ())), preferred_element_type=f32)


def tn(a, b):
    return lax.dot_general(a, b, (((0,), (0,)), ((), ())), preferred_element_type=f32)


class Sems:
    def __init__(self, send, recv, local):
        self.send, self.recv, self.local, self.names, self.locals = send, recv, local, {}, {}

    def pair(self, name):
        i = self.names.setdefault(name, len(self.names))
        return self.send.at[i], self.recv.at[i]

    def one(self, name):
        return self.local.at[self.locals.setdefault(name, len(self.locals))]


PAIRS = 371
LOCALS = 8
PIECES = ((0, 0, 512), (0, 512, 256), (1, 0, 512), (1, 512, 256), (2, 0, 512), (2, 512, 256))
SETS = (0, 0, 1, 1, 0, 0)
GATHER_PIECES = ((0, 0, 384), (0, 384, 384), (1, 0, 512), (1, 512, 256), (2, 0, 512), (2, 512, 256))
SIZE = {"y": 2, "z": 4, "x": 2}
GATHER = (
    ((0, 48, "zyx"), (48, 24, "zxy"), (72, 24, "yxz"),),
    ((0, 48, "zxy"), (48, 24, "yzx"), (72, 24, "zyx"),),
    ((0, 24, "zyx"), (24, 40, "zxy"), (64, 32, "yzx"),),
    ((0, 24, "zyx"), (24, 40, "zxy"), (64, 32, "yzx"),),
    ((0, 40, "xzy"), (40, 16, "zyx"), (56, 40, "yzx"),),
    ((0, 40, "xzy"), (40, 16, "zyx"), (56, 40, "yzx"),),
)
SCATTER = (
    ((0, 48, "yxz"), (48, 32, "xzy"), (80, 16, "xzy"),),
    ((0, 40, "xzy"), (40, 32, "xyz"), (72, 24, "zxy"),),
    ((0, 24, "zyx"), (24, 72, "xzy"),),
    ((0, 24, "zyx"), (24, 72, "xzy"),),
    ((0, 24, "zxy"), (24, 40, "yxz"), (64, 32, "xyz"),),
    ((0, 24, "zxy"), (24, 40, "yxz"), (64, 32, "xyz"),),
)
KIND_GATHER, KIND_PUSH, KIND_SCATTER, KIND_CORE, KIND_OWN, KIND_ROWS, KIND_SMALL = 1, 2, 3, 4, 5, 6, 7
KIND_GATHER_RELAY, KIND_SCATTER_RELAY = 8, 9
TOK, COEF, COT, OUT, CG, TG = 6000, 6001, 6002, 6003, 6004, 6005
PARAMS, SUM_C, SUM_X, SUM_Y, SUM_Z = 7000, 7001, 7002, 7003, 7004
PACK, PACKUD, STICKY, NORM1, X0_, X0T_, ATTNOUT, NORM2, COTT_, OUTS_, NORM2B, RB0, TOK1, TOK2 = range(14)
PJ1, PJ2, MEM1, MEM2, AT1, AT2, UP1, UP2, GD1, GD2, DN1, DN2, GU1, GU2, BU, AB1, AB2, GS1, GS2 = range(20, 39)
SCHEDULE = (
    TOK, PACK, 5000, 1000, 5100, PACKUD, 5200, 5300, 5400, 1400, 5500, 1500, STICKY, -5000, -5100, -5200, -5300,
    -5400, -5500, 1010, -1500, 2500, -1400, 1100, 2400, -2500, -2400, -1000, 2000, 1020, 1001, 1120, -2000, -1010,
    2010, 1011, 1200, -1020, 2020, 1021, -2010, -2020, COEF, 1210, -1021, 2021, -TOK, NORM1, -2021, -1011, -1120,
    -1100, 2011, 1022, 2120, 2100, 1101, -1200, 1012, -1001, 2001, -2011, 1002, -2120, -2100, -2001, -1210, 1110,
    1121, 8200, 8210, 1300, -COEF, X0_, 1220, -1101, 2101, 1102, 1310, -1110, 2110, 1111, -2101, -2110, -1300, -1012,
    2012, -8200, 2200, -1220, 2220, -1121, 2121, 1122, -1022, 2022, 8300, 1221, -2012, -2200, -2220, -8210, 2210,
    -1002, 2002, 1211, -2121, -1310, -2022, -2210, 1201, -8300, 2300, -2002, PJ1, PJ1, -2300, PJ1, -1111, 2111, 1112,
    8310, 1320, 1301, 1410, PJ1, 1401, MEM1, MEM1, 1420, MEM1, MEM1, -2111, -1122, 2122, AT1, -8310, -1320, COT,
    2310, 2320, -2122, AT1, -1102, -2320, -2310, -1410, 2102, 1311, AT1, -1201, -1211, -1221, -1301, -1420, 8221,
    2201, 2211, 1202, 1212, 2301, 1321, 2420, AT1, -2102, -1112, 2112, -2420, -2301, -2201, -2211, -1311, 2311, 8410,
    1421, 1302, -2112, PJ2, PJ2, PJ2, -2311, PJ2, MEM2, MEM2, MEM2, -COT, -1401, MEM2, AT2, -8221, -8410, 2221, 1222,
    2410, -1321, AT2, AT2, -2410, 8321, 1312, 8401, 1510, AT2, -2221, 1501, X0T_, -1202, -1302, 2202, 2302, ATTNOUT,
    -1510, 8510, 1411, NORM2, -2202, -8321, -1212, -2302, 2212, 2321, 1322, 1520, -1421, 8421, -8510, 2510, 1511,
    -2321, -1501, 8501, -2510, -2212, -1222, 2222, -8401, 2401, 1402, -1520, 2520, 1521, -1411, 2411, 1412, -2520,
    -1511, 2511, -1312, 2312, -2222, UP1, -1322, -8421, -2401, -2411, -8501, 2322, 2421, 1422, 2501, UP1, -2312,
    -2511, UP1, -1521, 8521, UP1, -2322, -2421, -2501, UP2, UP2, 1502, UP2, UP2, -8521, 2521, COTT_, -1412, 2412,
    GD1, GD1, -2521, GD1, -2412, GD1, 4400, GD2, 1512, GD2, GD2, GD2, 4500, -1402, 2402, 1522, -1502, 2502, -2402,
    -1512, 2512, -2502, -1422, 2422, -4500, 3500, 3510, 3520, -2512, -4400, 3400, -2422, DN1, 3420, DN1, -1522, 2522,
    3410, DN1, DN1, GU1, -2522, GU1, GU1, GU1, -3510, 4200, -3520, DN2, DN2, -3500, 9500, 3511, DN2, DN2, OUTS_, GU2,
    GU2, GU2, 3521, GU2, 4300, BU, BU, -9500, 3501, OUT, -4200, 3200, 3210, -3400, BU, BU, -3420, -3511, -4300,
    -3501, NORM2B, -3410, -3521, 9400, 3421, AB1, 3512, 3502, 3522, 3300, AB1, -9400, -3502, -3200, -OUT, 9200, AB1,
    -3421, -3522, -3512, 3422, 9522, 9512, 3411, AB1, -9522, -9200, -3210, -3300, 3401, 3201, 3211, 3310, -9512, GS1,
    -3422, GS1, GS1, -3201, GS1, -3411, 4000, AB2, -3401, 9422, 3402, AB2, 3412, 3202, AB2, -4000, -9422, -3402,
    3000, 3010, 9300, AB2, -3202, -3310, 3311, GS2, GS2, GS2, -9300, GS2, 4100, RB0, -3412, -3211, 3020, 9412, 9211,
    TOK1, -4100, -3010, 3100, 3120, CG, -3311, TOK2, -3000, -3020, -9412, SUM_C, 3110, TG, 3011, -3120, 9120, 3001,
    -9211, -SUM_C, -3100, -CG, 3101, 3021, -9120, SUM_X, 9311, -3110, 3121, -3011, 9011, 3111, -3121, 3122, -SUM_X,
    SUM_Y, -3001, 3002, -3101, 3212, -3021, 9101, -9311, -3122, 9021, 3312, 3301, -9011, 3012, -3111, 3112, -SUM_Y,
    SUM_Z, -TG, -3002, -3301, 9002, 3302, -9101, 3102, -3312, -9021, 3022, -3012, -3212, -3112, 9112, -3302, -3102,
    -3022, -SUM_Z, -9112, -9002,
)


def scatter_shape(piece, j, i):
    _, rows, order = SCATTER[piece][j]
    rest = [SIZE[d] for d in "yzx" if d in order[i + 1 :]]
    lead = [4] if order[i] == "z" else []
    return tuple(lead + rest + [rows, PIECES[piece][2]])


SCATTER_KEYS = [(p, j, i) for p in range(6) for j in range(len(SCATTER[p])) for i in range(3)]


def fused_kernel(
    tok_in, coef_in, cot_in, wq_ref, wk_ref, wv_ref, wo_ref, wu_ref, wd_ref, mu_ref, sigma_ref, flag_ref, spot_ref,
    gain1_ref, gain2_ref, fita_ref, past_ref,
    out_o, tg_o, cg_o, wg_o, small_o,
    W, G, RCA, RCB, RS, RZ,
    VTOK, VCOEF, VCOT, X0, X0T, COTT, N2, N2T, DHL, DHLT, PK, MEM, PR, CTX, HID, ACC, ACT, GP, SMP,
    TK, DQ, DM, SP, SPT, OUTS, ST1, ST2,
    *rest,
):
    bufs = dict(zip(SCATTER_KEYS, rest[: len(SCATTER_KEYS)]))
    send, recv, local = rest[len(SCATTER_KEYS) :]
    sems = Sems(send, recv, local)
    dp, mp = lax.axis_index("dp"), lax.axis_index("mp")
    z, x, y, c = dp // 2, dp % 2, mp // 2, mp % 2
    ox, oy, oc = 1 - x, 1 - y, 1 - c
    z_next = {k: (z + k) % 4 for k in (1, 2, 3)}
    z_prev = {k: (z - k + 4) % 4 for k in (1, 2, 3)}
    m_next = {k: (mp + k) % 4 for k in (1, 2, 3)}
    m_prev = {k: (mp - k + 4) % 4 for k in (1, 2, 3)}
    root = 0.125
    every = slice(None)
    to = {"c": (dp, y * 2 + oc), "y": (dp, oy * 2 + c), "x": (z * 2 + ox, mp)}
    to_mp = {k: (dp, m_next[k]) for k in (1, 2, 3)}
    to_z = {k: (z_next[k] * 2 + x, mp) for k in (1, 2, 3)}

    pending = {}

    def start(name, src, dst, dev):
        s, r = sems.pair(name)
        pltpu.make_async_remote_copy(
            src_ref=src, dst_ref=dst, send_sem=s, recv_sem=r, device_id=dev, device_id_type=MESH
        ).start()

    def wait_recv(name, region, dev):
        s, r = sems.pair(name)
        pltpu.make_async_remote_copy(
            src_ref=region, dst_ref=region, send_sem=s, recv_sem=r, device_id=dev, device_id_type=MESH
        ).wait_recv()

    def drain(group):
        for code in pending.pop(group, []):
            for k, src, dst, dev, _ in copies(code):
                s, r = sems.pair((code, k))
                at_z(senders(code, k), lambda: pltpu.make_async_remote_copy(
                    src_ref=src, dst_ref=dst, send_sem=s, recv_sem=r, device_id=dev, device_id_type=MESH
                ).wait_send())

    barrier = pltpu.get_barrier_semaphore()
    for dev in (to_mp[1], to_mp[2], to_mp[3], to["x"], to_z[1], to_z[2], to_z[3]):
        pl.semaphore_signal(barrier, inc=1, device_id=dev, device_id_type=MESH)
    pl.semaphore_wait(barrier, 7)

    GD, GU, GA = G.at[0], G.at[1], W.at[1]
    grads = {0: GA, 1: GU, 2: GD}

    def rows_in(src, dst, n):
        return [
            (k, src.at[m_next[k]], dst.at[pl.ds(mp * n, n)], to_mp[k], dst.at[pl.ds(m_prev[k] * n, n)])
            for k in (1, 2, 3)
        ], (src.at[mp], dst.at[pl.ds(mp * n, n)])

    def rows_out(src, dst, n):
        return [
            (k, src.at[pl.ds(m_next[k] * n, n)], dst.at[mp], to_mp[k], dst.at[m_prev[k]]) for k in (1, 2, 3)
        ], (src.at[pl.ds(mp * n, n)], dst.at[mp])

    def row_copies(code):
        if code == TOK:
            return rows_in(tok_in, VTOK, 128)
        if code == COEF:
            return rows_in(coef_in, VCOEF, 64)
        if code == COT:
            return rows_in(cot_in, VCOT, 64)
        if code == OUT:
            return rows_out(OUTS, out_o, 64)
        if code == CG:
            return rows_out(X0.at[pl.ds(0, 256)], cg_o, 64)
        return rows_out(X0.at[pl.ds(256, 512)], tg_o, 128)

    def parts_of(code):
        return code // 1000, code // 100 % 10, code // 10 % 10, code % 10

    def gather_part(code):
        _, piece, j, i = parts_of(code)
        a, col, wide = GATHER_PIECES[piece]
        lo, n, order = GATHER[piece][j]
        d = order[i]
        at = {ax: (every if ax in order[:i] else near) for ax, near in (("y", y), ("z", z), ("x", x))}

        def region(cc, axis=None, index=None):
            use = {**at, axis: index}
            return W.at[a, use["y"], cc, use["z"], use["x"], pl.ds(lo, n), pl.ds(col, wide)]

        def brings(cc):
            if d == "z":
                return [(k, region(cc, d, z_prev[k])) for k in (1, 2, 3)]
            return [(0, region(cc, d, oy if d == "y" else ox))]

        return d, region(c), brings, region

    def scatter_part(code):
        _, piece, j, i = parts_of(code)
        a, col, wide = PIECES[piece]
        lo, n, order = SCATTER[piece][j]
        rest_axes = [ax for ax in "yzx" if ax in order[i + 1 :]]
        return a, pl.ds(col, wide), lo, n, order[i], rest_axes, i, bufs[(piece, j, i)]

    def copies(code):
        kind, piece, _, _ = parts_of(code)
        if kind == KIND_ROWS:
            return row_copies(code)[0]
        if code == PARAMS:
            return [(k, SMP.at[mp], SMP.at[mp], to_mp[k], SMP.at[m_prev[k]]) for k in (1, 2, 3)]
        if code == SUM_Z:
            return [(k, RS.at[6], RZ.at[k - 1], to_z[k], RZ.at[k - 1]) for k in (1, 2, 3)]
        if kind == KIND_SMALL:
            i = code - SUM_C
            return [(0, RS.at[2 * i], RS.at[2 * i + 1], to["cxy"[i]], RS.at[2 * i + 1])]
        a, col, wide = (GATHER_PIECES if kind == KIND_OWN else PIECES)[piece]
        cols = pl.ds(col, wide)
        if kind == KIND_OWN:
            mine = W.at[a, y, c, z, x, every, cols]
            return [(0, mine, mine, to["c"], W.at[a, y, oc, z, x, every, cols])]
        if kind == KIND_GATHER:
            d, src, brings, _ = gather_part(code)
            return [(k, src, src, to_z[k] if k else to[d], region) for k, region in brings(c)]
        if kind == KIND_GATHER_RELAY:
            region = gather_part(code - 7000)[3]
            return [(k, region(c, "z", z_prev[2]), region(c, "z", z_prev[2]), to_z[k], region(c, "z", z_prev[4 - k])) for k in (1, 3)]
        if kind == KIND_PUSH:
            brings = gather_part(code)[2]
            return [(k, mine, mine, to["c"], theirs) for (k, mine), (_, theirs) in zip(brings(c), brings(oc))]
        if kind == KIND_CORE:
            buf = (RCA, RCB)[piece % 2].at[SETS[piece]]
            return [(0, grads[a].at[every, oc, every, every, every, cols], buf, to["c"], buf)]
        a, cols, lo, n, d, rest_axes, i, buf = scatter_part(code)
        at = {ax: (every if ax in rest_axes else near) for ax, near in (("y", y), ("z", z), ("x", x))}

        def send(index):
            use = {**at, d: index}
            return grads[a].at[use["y"], c, use["z"], use["x"], pl.ds(lo, n), cols]

        if kind == KIND_SCATTER_RELAY:
            return [(2, send(z_next[2]), buf.at[1], to_z[2], buf.at[1])]
        if d == "z":
            direct = [(k, send(z_next[k]), buf.at[k - 1], to_z[k], buf.at[k - 1]) for k in (1, 2, 3)]
            return direct + [(4, send(z_next[3]), buf.at[3], to_z[1], buf.at[3]), (5, send(z_next[1]), buf.at[3], to_z[3], buf.at[3])]
        return [(0, send(oy if d == "y" else ox), buf, to[d], buf)]

    def along_z(code):
        kind, piece, j, i = parts_of(code)
        if kind == KIND_GATHER:
            return piece > 1 and GATHER[piece][j][2][i] == "z"
        if kind == KIND_SCATTER:
            return SCATTER[piece][j][2][i] == "z"
        return kind in (KIND_GATHER_RELAY, KIND_SCATTER_RELAY)

    def senders(code, k):
        kind = code // 1000
        if not along_z(code):
            return None
        if kind == KIND_GATHER:
            return {1: (0, 1, 2), 2: (0, 1, 2, 3), 3: (1, 2, 3)}[k]
        if kind == KIND_GATHER_RELAY:
            return {1: (2,), 3: (1,)}[k]
        if kind == KIND_SCATTER:
            return {1: (0, 1, 2), 2: (0, 3), 3: (1, 2, 3), 4: (0,), 5: (3,)}[k]
        return (1, 2)

    def at_z(which, todo):
        if which is None or len(which) == 4:
            todo()
            return
        test = z == which[0]
        for one in which[1:]:
            test = test | (z == one)
        pl.when(test)(todo)

    def step_of(code, k):
        return {4: 1, 5: 3}.get(k, k)

    def receivers(code, k):
        which = senders(code, k)
        if which is None:
            return None
        return tuple(sorted((one + step_of(code, k)) % 4 for one in which))

    def go(code):
        kind, piece, _, _ = parts_of(code)
        if kind == KIND_SMALL and code != PARAMS:
            RS[2 * (code - SUM_C)] = small_o[...]
        gathers = kind in (KIND_GATHER, KIND_PUSH, KIND_OWN, KIND_GATHER_RELAY) and PIECES[piece][0] == 1
        pending.setdefault(gathers, []).append(code)
        for k, src, dst, dev, _ in copies(code):
            at_z(senders(code, k), lambda: start((code, k), src, dst, dev))
        if kind == KIND_ROWS:
            src, dst = row_copies(code)[1]
            pltpu.make_async_copy(src, dst, sems.one(code)).start()

    def got(code):
        kind, piece, _, _ = parts_of(code)
        for k, _, _, dev, region in copies(code):
            at_z(receivers(code, k), lambda: wait_recv((code, k), region, dev))
        if kind == KIND_ROWS:
            src, dst = row_copies(code)[1]
            pltpu.make_async_copy(src, dst, sems.one(code)).wait()
        if code == SUM_Z:
            small_o[...] = RS[6] + RZ[0] + RZ[1] + RZ[2]
        elif kind == KIND_SMALL and code != PARAMS:
            small_o[...] = small_o[...] + RS[2 * (code - SUM_C) + 1]
        elif kind == KIND_CORE:
            core_sum(piece)
        elif kind == KIND_SCATTER and along_z(code):
            at_z((1, 2), lambda: relay_sum(code))
        elif kind == KIND_SCATTER:
            stage_sum(code, ())
        elif kind == KIND_SCATTER_RELAY:
            at_z((1, 2), lambda: stage_sum(code, (0, 1, 2)))
            at_z((0,), lambda: stage_sum(code, (1, 2)))
            at_z((3,), lambda: stage_sum(code, (0, 1)))

    def core_sum(piece):
        a, col, wide = PIECES[piece]
        g, s, buf = grads[a], SETS[piece], (RCA, RCB)[piece % 2]

        def add(q, carry):
            at = (q // 8, c, (q // 2) % 4, q % 2, every, pl.ds(col, wide))
            g[at] = g[at] + buf[s, q // 8, (q // 2) % 4, q % 2]
            return carry

        lax.fori_loop(0, 16, add, 0)

    def over_rest(rest_axes, todo, **fixed):
        def one(q, carry):
            at = {"y": y, "z": z, "x": x, **fixed}
            left = q
            for ax in reversed(rest_axes):
                at[ax] = left % SIZE[ax]
                left = left // SIZE[ax]
            todo(at["y"], at["z"], at["x"], tuple(at[ax] for ax in rest_axes))
            return carry

        lax.fori_loop(0, math.prod(SIZE[ax] for ax in rest_axes), one, 0)

    def relay_sum(code):
        a, cols, lo, n, d, rest_axes, i, buf = scatter_part(code)
        g, rows = grads[a], pl.ds(lo, n)

        def todo(yy, zz, xx, inner):
            here = (yy, c, zz, xx, rows, cols)
            g[here] = g[here] + buf[(3,) + inner]

        over_rest(rest_axes, todo, z=z_next[2])

    def stage_sum(code, slots):
        a, cols, lo, n, d, rest_axes, i, buf = scatter_part(code)
        g, rows = grads[a], pl.ds(lo, n)

        def todo(yy, zz, xx, inner):
            here = (yy, c, zz, xx, rows, cols)
            parts = [buf[(k,) + inner] for k in slots] if d == "z" else [buf[inner] if inner else buf[...]]
            if i == 2:
                total = g[here].astype(f32)
                for part in parts:
                    total = total + part.astype(f32)
                wg_o[a, rows, cols] = total
            elif d == "z":
                total = g[here].astype(f32)
                for part in parts:
                    total = total + part.astype(f32)
                g[here] = total.astype(bf16)
            else:
                g[here] = g[here] + parts[0]

        if i == 2:
            todo(y, z, x, ())
        else:
            over_rest(rest_axes, todo)

    width_rbf = 1.0 / NB
    cen = (lax.broadcasted_iota(jnp.int32, (1, NB), 1).astype(f32) + 0.5) / NB
    present = flag_ref[mp].astype(f32)
    g1 = gain1_ref[...].astype(f32).reshape(1, 768)
    g2 = gain2_ref[...].astype(f32).reshape(1, 768)

    def weight(a, m, col=0, n=768):
        return W[a, m // 2, m % 2, :, :, :, col : col + n].reshape(768, n)

    def pack():
        wot = wo_ref[...].astype(f32).T
        for i, ref in enumerate((wq_ref, wk_ref, wv_ref)):
            W[0, y, c, z, x, :, i * 128 : i * 128 + 128] = ref[:, 0:128]
        W[0, y, c, z, x, :, 384:512] = wot[:, 0:128].astype(bf16)
        last = (wq_ref[:, 128:192], wk_ref[:, 128:192], wv_ref[:, 128:192])
        last = [v.astype(f32) for v in last] + [wot[:, 128:192]]
        for i in (0, 1):
            both = jnp.concatenate(last[2 * i : 2 * i + 2], axis=1)
            W[0, y, c, z, x, :, 512 + i * 128 : 640 + i * 128] = both.astype(bf16)

    def packud():
        W[1, y, c, z, x] = wu_ref[...]
        W[2, y, c, z, x] = wd_ref[...]
        SMP[mp, 0:3, :] = mu_ref[...].astype(f32)
        SMP[mp, 3:6, :] = sigma_ref[...].astype(f32)
        SMP[mp, 6:8, :] = jnp.zeros((2, 256), f32)
        go(PARAMS)

    def sticky():
        cen_down = (lax.broadcasted_iota(jnp.int32, (NB, 1), 0).astype(f32) + 0.5) / NB
        spots = (spot_ref[pl.ds(mp, 1), :].astype(f32) + 0.5) / (2 * SEGMENT_TOKENS)
        samples = jnp.exp(-((spots - cen_down) ** 2) / (2.0 * width_rbf * width_rbf))
        fit = lax.dot_general(
            fita_ref[...], samples, (((1,), (1,)), ((), ())), precision=highest, preferred_element_type=f32
        )
        SP[:, 0:256] = fit.astype(bf16)
        SP[:, 256:512] = past_ref[...]
        SPT[0:256, :] = fit.T.astype(bf16)
        SPT[256:512, :] = past_ref[...].astype(f32).T.astype(bf16)

    def norm1():
        def one(i, carry):
            rows = pl.ds(pl.multiple_of(i * 128, 128), 128)
            v = VTOK[rows, :].astype(f32)
            mean = jnp.mean(v, axis=-1, keepdims=True)
            centred = v - mean
            inv = lax.rsqrt(jnp.mean(centred * centred, axis=-1, keepdims=True) + epsilon)
            ST1[rows, 0:1] = mean
            ST1[rows, 1:2] = inv
            X0[pl.ds(pl.multiple_of(256 + i * 128, 128), 128), :] = (centred * inv * g1).astype(bf16)
            return carry

        lax.fori_loop(0, 4, one, 0)

    def x0():
        X0[0:256, :] = (VCOEF[...].astype(f32) * present).astype(bf16)
        got(PARAMS)

    def x0t():
        for r in range(3):
            X0T[:, r * 256 : (r + 1) * 256] = X0[r * 256 : (r + 1) * 256, :].astype(f32).T.astype(bf16)

    def project(m, col, wide):
        PK[m, :, col : col + wide] = nn(X0[...], weight(0, m, col, wide)).astype(bf16)

    def memory(m, first, col):
        MEM[m, :, col : col + 256] = nn(SP[...], PK[m, 0:512, first : first + 256]).astype(bf16)

    lane = lax.broadcasted_iota(jnp.int32, (256, 128), 1)
    row_i = lax.broadcasted_iota(jnp.int32, (256, 512), 0)
    col_i = lax.broadcasted_iota(jnp.int32, (256, 512), 1)
    upper = lane >= 64

    lower = jnp.logical_not(upper)
    HEADS = ((0, 1, 2, lower, lower, 0, 128), (0, 1, 2, upper, upper, 0, 128), (4, 4, 5, upper, lower, 256, 384))

    def head_query(m, h):
        qb, lanes = HEADS[h][0], HEADS[h][3]
        q = PK[m, 512:768, qb * 128 : qb * 128 + 128].astype(f32)
        if h == 2:
            q = pltpu.roll(q, 64, 1)
        return jnp.where(lanes, q * root, 0.0).astype(bf16)

    row8 = lax.broadcasted_iota(jnp.int32, (8, 128), 0)
    lane8 = lax.broadcasted_iota(jnp.int32, (8, 128), 1)
    low8, up8 = lane8 < 64, lane8 >= 64

    def split(v):
        top = v.astype(bf16)
        return top, (v - top.astype(f32)).astype(bf16)

    def memory_vectors(m, heads):
        first = HEADS[heads[0]][5]
        u = nn(SMP[m].astype(bf16), MEM[m, :, first : first + 128])
        if heads[0] == 0:
            keep = ((row8 % 2 == 0) & low8) | ((row8 % 2 == 1) & up8)
            rows = jnp.concatenate([u[0:2], u[3:5], jnp.zeros((4, 128), f32)], axis=0)
            return jnp.where(keep, rows, 0.0)
        rows = jnp.concatenate([u[2:3], u[7:8], u[5:6], u[7:8], jnp.zeros((4, 128), f32)], axis=0)
        return jnp.where(up8, rows, 0.0)

    def spread_of(m, heads, q8, vec):
        top, rest = split(vec)
        last = (vec - top.astype(f32) - rest.astype(f32)).astype(bf16)
        wide = jnp.concatenate([top, rest, last], axis=1)
        wide = jnp.concatenate([wide, jnp.zeros((120, 384), bf16)], axis=0)
        lg = nt(jnp.concatenate([q8, q8, q8], axis=1), wide)
        sil = pltpu.roll(lg, 126, 1)
        mean = 1.0 / (1.0 + jnp.exp(-lg))
        soft = jnp.maximum(sil, 0.0) + jnp.log1p(jnp.exp(-jnp.abs(sil)))
        spread = soft * spread_scale + width_rbf * width_rbf
        inv_s = 1.0 / spread
        return sil, mean, inv_s, width_rbf * lax.rsqrt(spread), -0.5 * inv_s

    def reach_of(i, mean, factor, rate):
        dist = mean[:, i : i + 1] - cen
        return dist, factor[:, i : i + 1] * jnp.exp(rate[:, i : i + 1] * (dist * dist))

    def attend(m, heads):
        parts = []
        qms = [head_query(m, h) for h in heads]
        q8 = qms[0] + qms[1] if heads[0] == 0 else qms[0]
        _, mean, _, factor, rate = spread_of(m, heads, q8, memory_vectors(m, heads))
        for i, h in enumerate(heads):
            qb, kb, vb, klanes, vlanes, mk0, mv0 = HEADS[h]
            s = nt(qms[i], PK[m, 256:768, kb * 128 : kb * 128 + 128])
            s = jnp.where(col_i - 256 <= row_i, s, -1e30)
            top = jnp.max(s, axis=-1, keepdims=True)
            e = jnp.exp(s - top)
            p = (e * (1.0 / jnp.sum(e, axis=-1, keepdims=True))).astype(bf16)
            PR[m, h] = p
            ctx = nn(p, PK[m, 256:768, vb * 128 : vb * 128 + 128])
            reach = reach_of(i, mean, factor, rate)[1]
            parts.append(ctx + nn(reach.astype(bf16), MEM[m, :, mv0 : mv0 + 128]))
        if heads[0] == 0:
            CTX[m, :, 0:128] = jnp.where(upper, parts[1], parts[0]).astype(bf16)
        else:
            CTX[m, :, 128:256] = jnp.where(upper, pltpu.roll(parts[0], 64, 1), 0.0).astype(bf16)

    def attnout():
        HID[...] = VTOK[256:512, :].astype(f32)

        def one(m, carry):
            wo = jnp.concatenate([weight(0, m, 384, 128), weight(0, m, 640, 128)], axis=1)
            HID[...] += nt(CTX[m], wo)
            return carry

        lax.fori_loop(0, 4, one, 0)

    def norm2():
        hid = HID[...]
        mean = jnp.mean(hid, axis=-1, keepdims=True)
        centred = hid - mean
        inv = lax.rsqrt(jnp.mean(centred * centred, axis=-1, keepdims=True) + epsilon)
        ST2[:, 0:1] = mean
        ST2[:, 1:2] = inv
        normed = centred * inv * g2
        N2[...] = normed.astype(bf16)
        N2T[...] = normed.T.astype(bf16)
        ACC[...] = hid

    def up(m, col, wide):
        cols = slice(col, col + wide)
        u = nn(N2[...], weight(1, m, col, wide))
        u2 = u * u
        th = jnp.tanh(gelu_coef * (u + 0.044715 * u2 * u))
        ACT[m, :, cols] = (0.5 * u * (1.0 + th)).astype(bf16)
        GP[m, :, cols] = 0.5 * (1.0 + th) + (0.5 * gelu_coef) * u * (1.0 - th * th) * (1.0 + 0.134145 * u2)

    def cott():
        COTT[...] = VCOT[...].astype(f32).T.astype(bf16)

    def put(g, m, col, wide, left, right):
        g[m // 2, m % 2, :, :, :, col : col + wide] = nn(left[...], right).reshape(4, 2, 96, wide).astype(bf16)

    def grad_down(m, col, wide):
        put(GD, m, col, wide, COTT, ACT[m, :, col : col + wide])

    def down(m, col, wide):
        cols = slice(col, col + wide)
        wd = weight(2, m, col, wide)
        ACC[...] += nt(ACT[m, :, cols], wd)
        d_act = nn(VCOT[...], wd)
        ACT[m, :, cols] = (d_act * GP[m, :, cols]).astype(bf16)

    def outs():
        OUTS[...] = ACC[...].astype(bf16)
        ACC[...] = jnp.zeros_like(ACC)

    def grad_up(m, col, wide):
        put(GU, m, col, wide, N2T, ACT[m, :, col : col + wide])

    def back_up(m):
        ACC[...] += nt(ACT[m], weight(1, m))

    def norm2b():
        d_n2 = ACC[...]
        flat = (HID[...] - ST2[:, 0:1]) * ST2[:, 1:2]
        g2_grad = jnp.sum(d_n2 * flat, axis=0, keepdims=True)
        e = d_n2 * g2
        d_hidden = VCOT[...].astype(f32) + ST2[:, 1:2] * (
            e - jnp.mean(e, axis=-1, keepdims=True) - flat * jnp.mean(e * flat, axis=-1, keepdims=True)
        )
        HID[...] = d_hidden
        DHL[...] = d_hidden.astype(bf16)
        DHLT[...] = d_hidden.T.astype(bf16)
        for i in range(3):
            small_o[27 + i : 28 + i, :] = g2_grad[:, i * 256 : (i + 1) * 256]

    lane_i = lax.broadcasted_iota(jnp.int32, (256, 128), 1)

    def attend_back(m, heads):
        pair = heads[0] == 0
        d_ctx = nn(DHL[...], weight(0, m, 384 if pair else 640, 128))
        if not pair:
            d_ctx = pltpu.roll(d_ctx, 64, 1)
        qms = [head_query(m, h) for h in heads]
        q8 = qms[0] + qms[1] if pair else qms[0]
        vec = memory_vectors(m, heads)
        sil, mean, inv_s, factor, rate = spread_of(m, heads, q8, vec)
        sums = []
        d_ks, d_vs, d_qs, d_mvs = [], [], [], []
        for i, h in enumerate(heads):
            qb, kb, vb, klanes, vlanes, mk0, mv0 = HEADS[h]
            dc = jnp.where(vlanes, d_ctx, 0.0).astype(bf16)
            p = PR[m, h]
            d_p = nt(dc, PK[m, 256:768, vb * 128 : vb * 128 + 128])
            pf = p.astype(f32)
            t = pf * d_p
            d_s = (t - pf * jnp.sum(t, axis=-1, keepdims=True)).astype(bf16)
            d_v = tn(p, dc)
            d_k = tn(d_s, qms[i])
            d_q = jnp.where(klanes, nn(d_s, PK[m, 256:768, kb * 128 : kb * 128 + 128]), 0.0)
            dist, reach = reach_of(i, mean, factor, rate)
            d_r = nt(dc, MEM[m, :, mv0 : mv0 + 128])
            d_mv = tn(reach.astype(bf16), dc)
            t = d_r * reach
            td = t * dist
            sums.append([jnp.sum(v, axis=-1, keepdims=True) for v in (t, td, td * dist)])
            if i == 0:
                TK[0] = d_k
                TK[1] = d_v
                DQ[...] = d_q
                DM[:, 128:256] = d_mv.astype(bf16)
            else:
                TK[0] += d_k
                TK[1] += d_v
                DQ[...] += d_q
                DM[:, 128:256] += d_mv.astype(bf16)
        s0, s1, s2 = (jnp.where(lane_i == 0, sums[0][k], sums[-1][k]) for k in range(3))
        g_mu = -s1 * inv_s * mean * (1.0 - mean)
        g_sg = (s2 * inv_s - s0) * (0.5 * inv_s) * spread_scale * (1.0 / (1.0 + jnp.exp(-sil)))
        used = 2 if pair else 1
        both = jnp.where(lane_i < used, g_mu, 0.0) + pltpu.roll(jnp.where(lane_i < used, g_sg, 0.0), 2, 1)
        grad = both.T[0:8]
        grad_top, grad_rest = split(grad)
        qg = nn(jnp.concatenate([grad_top, grad_rest], axis=1), jnp.concatenate([q8, q8], axis=0))
        own = (((row8 % 2 == 0) & low8) | ((row8 % 2 == 1) & up8)) if pair else up8
        qg_top, qg_rest = split(jnp.where(own, qg, 0.0))
        par = SMP[m].astype(bf16).astype(f32)
        if pair:
            par = jnp.concatenate([par[0:2], par[3:5], jnp.zeros((4, 256), f32)], axis=0)
        else:
            par = jnp.concatenate([par[2:3], par[7:8], par[5:6], par[7:8], jnp.zeros((4, 256), f32)], axis=0)
        par = par.astype(bf16)
        qg_all = jnp.concatenate([qg_top, qg_rest], axis=0)
        DM[:, 0:128] = tn(jnp.concatenate([par, par], axis=0), qg_all).astype(bf16)
        vec_top, vec_rest = split(vec)
        mem_q = tn(
            jnp.concatenate([grad_top, grad_top, grad_rest, jnp.zeros((8, 256), bf16)], axis=0),
            jnp.concatenate([vec_top, vec_rest, vec_top, jnp.zeros((8, 128), bf16)], axis=0),
        )
        mu_sg = nt(qg_all, MEM[m, :, HEADS[heads[0]][5] : HEADS[heads[0]][5] + 128])
        mu_sg = mu_sg[0:8] + mu_sg[8:16]
        for i, h in enumerate(heads):
            small_o[pl.ds(m * 3 + h, 1), :] = mu_sg[i : i + 1]
            small_o[pl.ds(12 + m * 3 + h, 1), :] = mu_sg[2 + i : 3 + i]
        d_q = (DQ[...] + mem_q) * root
        DQ[...] = d_q if pair else pltpu.roll(d_q, 64, 1)
        back = nn(SPT[...], DM[...])
        first = 128 if heads[0] == 0 else 512
        for i in range(2):
            b = back[:, 128 * i : 128 * i + 128]
            cols = slice(first + 128 * i, first + 128 * i + 128)
            PK[m, 0:256, cols] = (b[0:256] * present).astype(bf16)
            PK[m, 256:512, cols] = (TK[i, 0:256] + b[256:512]).astype(bf16)
            now = TK[i, 256:512]
            if heads[0] == 2 and i == 0:
                now = now + DQ[...]
            PK[m, 512:768, cols] = now.astype(bf16)
        if heads[0] == 0:
            PK[m, 0:512, 0:128] = jnp.zeros((512, 128), bf16)
            PK[m, 512:768, 0:128] = DQ[...].astype(bf16)
            PK[m, :, 384:512] = jnp.zeros((768, 128), bf16)

    def grad_square(m, col, wide):
        own = 0 if col == 0 else 128

        val = nn(X0T[...], PK[m, :, col : col + wide])
        out_part = nn(DHLT[...], CTX[m, :, own : own + 128])
        val = jnp.concatenate([val[:, : wide - 128], val[:, wide - 128 :] + out_part], axis=1)
        GA[m // 2, m % 2, :, :, :, col : col + wide] = val.reshape(4, 2, 96, wide).astype(bf16)

    def rows_back(r):
        ACC[...] = jnp.zeros_like(ACC)

        def one(m, carry):
            ACC[...] += nt(PK[m, r * 256 : (r + 1) * 256, :], weight(0, m))
            return carry

        lax.fori_loop(0, 4, one, 0)

    def token_rows(r, first, extra):
        rows_back(r)
        d_n1 = ACC[...]
        rows = slice(first, first + 256)
        inv_1 = ST1[rows, 1:2]
        flat_1 = (VTOK[rows, :].astype(f32) - ST1[rows, 0:1]) * inv_1
        part = jnp.sum(d_n1 * flat_1, axis=0, keepdims=True)
        e = d_n1 * g1
        grad = inv_1 * (
            e - jnp.mean(e, axis=-1, keepdims=True) - flat_1 * jnp.mean(e * flat_1, axis=-1, keepdims=True)
        )
        if extra:
            grad = grad + HID[...]
        X0[256 + first : 512 + first, :] = grad.astype(bf16)
        return part

    def rb0():
        rows_back(0)
        X0[0:256, :] = ACC[...].astype(bf16)

    def tok1():
        part = token_rows(1, 0, False)
        for i in range(3):
            small_o[24 + i : 25 + i, :] = part[:, i * 256 : (i + 1) * 256]

    def tok2():
        part = token_rows(2, 256, True)
        for i in range(3):
            small_o[24 + i : 25 + i, :] = small_o[24 + i : 25 + i, :] + part[:, i * 256 : (i + 1) * 256]
        small_o[30:32, :] = jnp.zeros((2, 256), f32)

    single = {
        PACK: pack, PACKUD: packud, STICKY: sticky, NORM1: norm1, X0_: x0, X0T_: x0t, ATTNOUT: attnout, NORM2: norm2,
        COTT_: cott, OUTS_: outs, NORM2B: norm2b, RB0: rb0, TOK1: tok1, TOK2: tok2,
    }
    looped = {
        PJ1: lambda m: project(m, 0, 384), PJ2: lambda m: project(m, 512, 256),
        MEM1: lambda m: memory(m, 128, 0), MEM2: lambda m: memory(m, 512, 256),
        AT1: lambda m: attend(m, (0, 1)), AT2: lambda m: attend(m, (2,)),
        UP1: lambda m: up(m, 0, 512), UP2: lambda m: up(m, 512, 256),
        GD1: lambda m: grad_down(m, 0, 512), GD2: lambda m: grad_down(m, 512, 256),
        DN1: lambda m: down(m, 0, 512), DN2: lambda m: down(m, 512, 256),
        GU1: lambda m: grad_up(m, 0, 512), GU2: lambda m: grad_up(m, 512, 256), BU: back_up,
        AB1: lambda m: attend_back(m, (0, 1)), AB2: lambda m: attend_back(m, (2,)),
        GS1: lambda m: grad_square(m, 0, 512), GS2: lambda m: grad_square(m, 512, 256),
    }

    def transfer(item):
        if item > 0:
            go(item)
        else:
            got(-item)

    at = 0
    while at < len(SCHEDULE):
        item = SCHEDULE[at]
        at += 1
        if abs(item) > 999:
            transfer(item)
        elif item in single:
            single[item]()
        else:
            if item == GS1:
                drain(True)
            between = {}
            done = 0
            while done < 3:
                if abs(SCHEDULE[at]) > 999:
                    between.setdefault(done, []).append(SCHEDULE[at])
                else:
                    done += 1
                at += 1

            def step(m, carry, item=item, between=between):
                looped[item](m)
                for i, items in between.items():

                    @pl.when(m == i)
                    def _(items=items):
                        for one in items:
                            transfer(one)

                return carry

            lax.fori_loop(0, 4, step, 0)
    for group in list(pending):
        drain(group)


def finish_kernel(
    out_b, tg_b, cg_b, wg, sums, out, tg, cg, g1, gq, gk, gv, go, gm, gs, g2, gu, gd,
):
    me = lax.axis_index("mp")
    out[...] = out_b[...]
    tg[...] = tg_b[...].astype(f32)
    cg[...] = cg_b[...].astype(f32)
    for i, ref in enumerate((gq, gk, gv)):
        ref[:, 0:128] = wg[0, :, 128 * i : 128 * i + 128]
        at = 512 + 128 * (i // 2)
        block = wg[0, :, at : at + 128]
        ref[:, 128:192] = block[:, 64 * (i % 2) : 64 * (i % 2) + 64]
    go[0:128, :] = wg[0, :, 384:512].T
    go[128:192, :] = wg[0, :, 640:768].T[64:128, :]
    gu[...] = wg[1]
    gd[...] = wg[2]
    for h in range(3):
        gm[h : h + 1, :] = sums[pl.ds(me * 3 + h, 1), :]
        gs[h : h + 1, :] = sums[pl.ds(12 + me * 3 + h, 1), :]
    for i in range(3):
        g1[pl.ds(i * 256, 256)] = sums[24 + i]
        g2[pl.ds(i * 256, 256)] = sums[27 + i]


def fused_call(*args):
    any_ = pl.BlockSpec(memory_space=pl.ANY)
    vm = pl.BlockSpec(memory_space=pltpu.VMEM)
    sm = pl.BlockSpec(memory_space=pltpu.SMEM)
    V = pltpu.VMEM
    return pl.pallas_call(
        fused_kernel,
        out_shape=(
            jax.ShapeDtypeStruct((4, 64, 768), bf16),
            jax.ShapeDtypeStruct((4, 128, 768), bf16),
            jax.ShapeDtypeStruct((4, 64, 768), bf16),
            jax.ShapeDtypeStruct((3, 96, 768), f32),
            jax.ShapeDtypeStruct((32, 256), f32),
        ),
        in_specs=[any_] * 3 + [vm] * 8 + [sm] + [vm] * 5,
        out_specs=(any_, any_, any_, vm, vm),
        scratch_shapes=[
            V((3, 2, 2, 4, 2, 96, 768), bf16),
            V((2, 2, 2, 4, 2, 96, 768), bf16),
            V((2, 2, 4, 2, 96, 512), bf16),
            V((2, 2, 4, 2, 96, 256), bf16),
            V((7, 32, 256), f32),
            V((3, 32, 256), f32),
            V((512, 768), bf16),
            V((256, 768), bf16),
            V((256, 768), bf16),
            V((768, 768), bf16),
            V((768, 768), bf16),
            V((768, 256), bf16),
            V((256, 768), bf16),
            V((768, 256), bf16),
            V((256, 768), bf16),
            V((768, 256), bf16),
            V((4, 768, 768), bf16),
            V((4, 256, 512), bf16),
            V((4, 3, 256, 512), bf16),
            V((4, 256, 256), bf16),
            V((256, 768), f32),
            V((256, 768), f32),
            V((4, 256, 768), bf16),
            V((4, 256, 768), f32),
            V((4, 8, 256), f32),
            V((2, 512, 128), f32),
            V((256, 128), f32),
            V((256, 256), bf16),
            V((256, 512), bf16),
            V((512, 256), bf16),
            V((256, 768), bf16),
            V((512, 128), f32),
            V((256, 128), f32),
            *(V(scatter_shape(p, j, i), bf16) for p, j, i in SCATTER_KEYS),
            pltpu.SemaphoreType.DMA((PAIRS,)),
            pltpu.SemaphoreType.DMA((PAIRS,)),
            pltpu.SemaphoreType.DMA((LOCALS,)),
        ],
        compiler_params=pltpu.CompilerParams(
            collective_id=0, has_side_effects=True, vmem_limit_bytes=63 * 1024 * 1024
        ),
    )(*args)


def fused_body(
    tokens, coeffs, present_flag, sticky_pos, gain_one, w_query, w_key, w_value, w_out, mu_weight,
    sigma_weight, gain_two, w_up, w_down, cotangent,
):
    _, fitting = basis_tables(NB, SEGMENT_TOKENS)
    fita = jnp.asarray(fitting[:, :SEGMENT_TOKENS])
    past = jnp.asarray(fitting[:, SEGMENT_TOKENS:]).astype(bf16)
    parts = fused_call(
        tokens, coeffs, cotangent, w_query, w_key, w_value, w_out, w_up, w_down.T, mu_weight, sigma_weight,
        present_flag, sticky_pos, gain_one, gain_two, fita, past,
    )

    def like(v):
        return jax.ShapeDtypeStruct(v.shape, f32)

    shapes = (
        jax.ShapeDtypeStruct(cotangent.shape, bf16), like(tokens), like(coeffs), like(gain_one), like(w_query),
        like(w_key), like(w_value), like(w_out), like(mu_weight), like(sigma_weight), like(gain_two), like(w_up),
        like(w_down.T),
    )
    vm = pl.BlockSpec(memory_space=pltpu.VMEM)
    done = pl.pallas_call(
        finish_kernel, out_shape=shapes, in_specs=[vm] * 5, out_specs=(vm,) * 13,
    )(*parts)
    return (*done[:12], done[12].T)


def solution(mesh):
    in_specs = (
        P("dp", "mp", None), P("dp", "mp", None), P("dp"), P("dp", None), P(), P("dp", "mp"), P("dp", "mp"),
        P("dp", "mp"), P("mp", "dp"), P("mp", None), P("mp", None), P(), P("dp", "mp"), P("mp", "dp"),
        P("dp", "mp", None),
    )
    out_specs = (
        P("dp", "mp", None), P("dp", "mp", None), P("dp", "mp", None), P(), P("dp", "mp"), P("dp", "mp"),
        P("dp", "mp"), P("mp", "dp"), P("mp", None), P("mp", None), P(), P("dp", "mp"), P("mp", "dp"),
    )
    whole = body
    if mesh.shape["dp"] == 8 and mesh.shape["mp"] == 4:
        whole = fused_body
    return jax.shard_map(whole, mesh=mesh, in_specs=in_specs, out_specs=out_specs, check_vma=False)
```

```python
import math

import jax
import jax.numpy as jnp
import numpy as np
from jax import lax
from jax.experimental import pallas as pl
from jax.experimental.pallas import tpu as pltpu
from jax.sharding import PartitionSpec as P

HD = 64
NB = 256
SEGMENT_TOKENS = 256
BOTH = ("dp", "mp")

highest = lax.Precision.HIGHEST
epsilon = 1e-05
ridge = 0.5
spread_scale = 1.0 / 64.0
gelu_coef = 0.7978845608028654


def basis_tables(basis_count, seg_len):
    centers = (np.arange(basis_count) + 0.5) / basis_count
    width = 1.0 / basis_count
    times = (np.arange(2 * seg_len) + 0.5) / (2 * seg_len)
    design = np.exp(-((times[:, None] - centers[None, :]) ** 2) / (2.0 * width * width))
    normal = design.T @ design + ridge * np.eye(basis_count)
    fitting = np.linalg.solve(normal, design.T)
    return centers.astype(np.float32), fitting.astype(np.float32)


def norm_rows(values):
    centered = values - jnp.mean(values, axis=-1, keepdims=True)
    inverse = lax.rsqrt(jnp.mean(centered * centered, axis=-1, keepdims=True) + epsilon)
    return (centered * inverse, inverse)


def gelu_tanh(values):
    return (
        0.5 * values * (1.0 + jnp.tanh(gelu_coef * (values + 0.044715 * values * values * values)))
    )


def memory_reach(mem_scores, mu_in, sigma_in, centers):
    rbf_width = 1.0 / centers.shape[0]
    mu_logit = jnp.einsum("...hn,hn->...h", mem_scores, mu_in, precision=highest)
    sigma_logit = jnp.einsum("...hn,hn->...h", mem_scores, sigma_in, precision=highest)
    mean_pos = jax.nn.sigmoid(mu_logit)
    spread = jax.nn.softplus(sigma_logit) * spread_scale + rbf_width * rbf_width
    distance = mean_pos[..., None] - centers
    return (
        rbf_width
        * lax.rsqrt(spread)[..., None]
        * jnp.exp(-distance * distance / (2.0 * spread[..., None]))
    )


def mm(pattern, left_in, right_in):
    return jnp.einsum(pattern, left_in, right_in, preferred_element_type=jnp.float32)


def norm_back(grad, flat_rows, inverse, gain_vec):
    scaled = grad * gain_vec
    return inverse * (
        scaled
        - jnp.mean(scaled, axis=-1, keepdims=True)
        - flat_rows * jnp.mean(scaled * flat_rows, axis=-1, keepdims=True)
    )


def low(v):
    return v.astype(jnp.bfloat16)


def whole_sequences(
    tokens, coeffs, present_flag, sticky_pos, gain_one, wq, wk, wv, wo, mu, sigma, gain_two, wu, wdt, cot
):
    count, length, width = tokens.shape
    cur = cot.shape[1]
    past = length - cur
    heads = width // HD
    root = math.sqrt(HD)
    centers, fitting = basis_tables(NB, SEGMENT_TOKENS)
    rbf_width = 1.0 / NB
    past_fit = jnp.asarray(fitting[:, SEGMENT_TOKENS:]).astype(jnp.bfloat16)
    centers = jnp.asarray(centers)
    g1 = gain_one.astype(jnp.float32)
    g2 = gain_two.astype(jnp.float32)
    mu = mu.astype(jnp.float32)
    sigma = sigma.astype(jnp.float32)
    causal = jnp.arange(length)[None, :] <= (past + jnp.arange(cur))[:, None]
    present = present_flag.astype(jnp.float32)[:, None, None]
    spots = (sticky_pos.astype(jnp.float32) + 0.5) / (2 * SEGMENT_TOKENS)
    samples = jnp.exp(-((spots[:, :, None] - centers) ** 2) / (2.0 * rbf_width * rbf_width))
    sticky = low(
        jnp.einsum("nm,bmk->bnk", jnp.asarray(fitting[:, :SEGMENT_TOKENS]), samples, precision=highest)
    )
    rows = tokens.astype(jnp.float32)
    flat_one, inv_one = norm_rows(rows)
    normed = low(flat_one * g1)
    q = low(mm("bld,de->ble", normed[:, past:], wq))
    k = low(mm("bld,de->ble", normed, wk))
    v = low(mm("bld,de->ble", normed, wv))
    ck = low(present * mm("bnd,de->bne", coeffs, wk))
    cv = low(present * mm("bnd,de->bne", coeffs, wv))
    mk = low(mm("bnm,bme->bne", sticky, ck) + mm("np,bpe->bne", past_fit, k[:, :past]))
    mv = low(mm("bnm,bme->bne", sticky, cv) + mm("np,bpe->bne", past_fit, v[:, :past]))
    qh = q.reshape(count, cur, heads, HD)
    kh = k.reshape(count, length, heads, HD)
    vh = v.reshape(count, length, heads, HD)
    mkh = mk.reshape(count, NB, heads, HD)
    mvh = mv.reshape(count, NB, heads, HD)
    scores = mm("bqhd,bkhd->bhqk", qh, kh) / root
    masked = jnp.where(causal, scores, -1e30)
    probs = jax.nn.softmax(masked, axis=-1)
    probs_low = low(probs)
    short = mm("bhqk,bkhd->bqhd", probs_low, vh)
    mem_scores = mm("bqhd,bnhd->bqhn", qh, mkh) / root

    def reach_of(s, m, g):
        return memory_reach(s, m, g, centers)

    reach, reach_pull = jax.vjp(reach_of, mem_scores, mu, sigma)
    reach_low = low(reach)
    long_part = mm("bqhn,bnhd->bqhd", reach_low, mvh)
    context = low((short + long_part).reshape(count, cur, width))
    hidden = rows[:, past:] + mm("bqd,de->bqe", context, wo)
    flat_two, inv_two = norm_rows(hidden)
    normed_two = low(flat_two * g2)
    up = mm("bqd,df->bqf", normed_two, wu)
    active_rows, gelu_pull = jax.vjp(gelu_tanh, up)
    active = low(active_rows)
    output = low(hidden + mm("bqf,df->bqd", active, wdt))
    wdt_grad = mm("bqd,bqf->df", cot, active)
    d_up = low(gelu_pull(mm("bqd,df->bqf", cot, wdt))[0])
    wu_grad = mm("bqd,bqf->df", normed_two, d_up)
    d_n2 = mm("bqf,df->bqd", d_up, wu)
    g2_grad = jnp.sum(d_n2 * flat_two, axis=(0, 1))
    d_hidden = cot.astype(jnp.float32) + norm_back(d_n2, flat_two, inv_two, g2)
    d_hidden_low = low(d_hidden)
    wo_grad = mm("bqd,bqe->de", context, d_hidden_low)
    d_context = low(mm("bqe,de->bqd", d_hidden_low, wo)).reshape(count, cur, heads, HD)
    d_probs = mm("bqhd,bkhd->bhqk", d_context, vh)
    d_scores = low(probs * (d_probs - jnp.sum(probs * d_probs, axis=-1, keepdims=True)))
    d_reach = mm("bqhd,bnhd->bqhn", d_context, mvh)
    d_mv = low(mm("bqhn,bqhd->bnhd", reach_low, d_context)).reshape(count, NB, width)
    d_ms, mu_grad, sigma_grad = reach_pull(d_reach)
    d_ms = low(d_ms)
    dq = low(
        (mm("bhqk,bkhd->bqhd", d_scores, kh) + mm("bqhn,bnhd->bqhd", d_ms, mkh)) / root
    ).reshape(count, cur, width)
    d_mk = low(mm("bqhn,bqhd->bnhd", d_ms, qh) / root).reshape(count, NB, width)
    keep = present_flag.astype(jnp.bfloat16)[:, None, None]
    d_ck = low(mm("bnm,bne->bme", sticky, d_mk)) * keep
    d_cv = low(mm("bnm,bne->bme", sticky, d_mv)) * keep
    dk = (mm("bhqk,bqhd->bkhd", d_scores, qh) / root).reshape(count, length, width)
    dv = mm("bhqk,bqhd->bkhd", probs_low, d_context).reshape(count, length, width)
    pad = ((0, 0), (0, cur), (0, 0))
    dk = low(dk + jnp.pad(mm("np,bne->bpe", past_fit, d_mk), pad))
    dv = low(dv + jnp.pad(mm("np,bne->bpe", past_fit, d_mv), pad))
    wq_grad = mm("bqd,bqe->de", normed[:, past:], dq)
    wk_grad = mm("bld,ble->de", normed, dk) + mm("bnd,bne->de", coeffs, d_ck)
    wv_grad = mm("bld,ble->de", normed, dv) + mm("bnd,bne->de", coeffs, d_cv)
    d_n1 = mm("ble,de->bld", dk, wk) + mm("ble,de->bld", dv, wv)
    d_n1 = d_n1 + jnp.pad(mm("bqe,de->bqd", dq, wq), ((0, 0), (past, 0), (0, 0)))
    coeff_grad = mm("bne,de->bnd", d_ck, wk) + mm("bne,de->bnd", d_cv, wv)
    g1_grad = jnp.sum(d_n1 * flat_one, axis=(0, 1))
    token_grad = norm_back(d_n1, flat_one, inv_one, g1) + jnp.pad(
        d_hidden, ((0, 0), (past, 0), (0, 0))
    )
    return (
        output, token_grad, coeff_grad, g1_grad, wq_grad, wk_grad, wv_grad, wo_grad,
        mu_grad, sigma_grad, g2_grad, wu_grad, wdt_grad,
    )


def to_sequences(rows):
    return lax.all_to_all(rows, "mp", 0, 1, tiled=True)


def to_rows(rows):
    return lax.all_to_all(rows, "mp", 1, 0, tiled=True)


def body(
    tokens, coeffs, present_flag, sticky_pos, gain_one, w_query, w_key, w_value, w_out, mu_weight,
    sigma_weight, gain_two, w_up, w_down, cotangent,
):
    dp, mp = lax.axis_size("dp"), lax.axis_size("mp")
    me = lax.axis_index("mp")
    count = tokens.shape[0] // mp
    depth, share = w_query.shape
    inner = w_up.shape[1]
    width = depth * dp
    seq_tokens = to_sequences(tokens)
    seq_coeffs = to_sequences(coeffs)
    seq_cot = to_sequences(cotangent)
    flags = lax.dynamic_slice_in_dim(present_flag, me * count, count, 0)
    spots = lax.dynamic_slice_in_dim(sticky_pos, me * count, count, 0)
    heads_local = mu_weight.shape[0]
    mu, sigma = lax.all_gather((mu_weight, sigma_weight), "mp", axis=0, tiled=True)
    square = jnp.concatenate([w_query, w_key, w_value, w_out.T], axis=1)
    packed = jnp.concatenate([square, w_up, w_down.T], axis=1)
    whole = lax.all_gather(packed, BOTH, axis=0, tiled=False)
    whole = whole.reshape(dp, mp, depth, packed.shape[1]).transpose(0, 2, 1, 3)
    whole = whole.reshape(width, mp, packed.shape[1])

    def columns(first, size):
        return whole[:, :, first : first + size].reshape(width, mp * size)

    wq, wk, wv, wot = (columns(i * share, share) for i in range(4))
    wu = columns(4 * share, inner)
    wdt = columns(4 * share + inner, inner)
    (
        output, token_grad, coeff_grad, g1_grad, wq_grad, wk_grad, wv_grad, wo_grad,
        mu_grad, sigma_grad, g2_grad, wu_grad, wdt_grad,
    ) = whole_sequences(
        seq_tokens, seq_coeffs, flags, spots, gain_one, wq, wk, wv, wot.T, mu, sigma, gain_two, wu, wdt, seq_cot
    )

    def blocks(grad):
        return low(grad).reshape(dp, depth, mp, grad.shape[1] // mp).transpose(0, 2, 1, 3)

    def scatter(grad):
        stacked = blocks(grad)
        stacked = stacked.reshape((dp * mp * depth, stacked.shape[3]))
        return lax.psum_scatter(stacked, BOTH, scatter_dimension=0, tiled=True).astype(jnp.float32)

    wdt_own = scatter(wdt_grad)
    wu_own = scatter(wu_grad)
    square_own = scatter(
        jnp.concatenate(
            [g.reshape(width, mp, share) for g in (wq_grad, wk_grad, wv_grad, wo_grad.T)], axis=2
        ).reshape(width, mp * 4 * share)
    )
    small = lax.psum((mu_grad, sigma_grad, g1_grad, g2_grad), BOTH)
    mu_own = lax.dynamic_slice_in_dim(small[0], me * heads_local, heads_local, 0)
    sigma_own = lax.dynamic_slice_in_dim(small[1], me * heads_local, heads_local, 0)
    return (
        to_rows(output),
        to_rows(low(token_grad)).astype(jnp.float32),
        to_rows(low(coeff_grad)).astype(jnp.float32),
        small[2],
        square_own[:, :share],
        square_own[:, share : 2 * share],
        square_own[:, 2 * share : 3 * share],
        square_own[:, 3 * share :].T,
        mu_own,
        sigma_own,
        small[3],
        wu_own,
        wdt_own.T,
    )


f32 = jnp.float32
bf16 = jnp.bfloat16
MESH = pl.DeviceIdType.MESH


def nn(a, b):
    return jnp.dot(a, b, preferred_element_type=f32)


def nt(a, b):
    return lax.dot_general(a, b, (((1,), (1,)), ((), ())), preferred_element_type=f32)


def tn(a, b):
    return lax.dot_general(a, b, (((0,), (0,)), ((), ())), preferred_element_type=f32)


class Sems:
    def __init__(self, send, recv, local):
        self.send, self.recv, self.local, self.names, self.locals = send, recv, local, {}, {}

    def pair(self, name):
        i = self.names.setdefault(name, len(self.names))
        return self.send.at[i], self.recv.at[i]

    def one(self, name):
        return self.local.at[self.locals.setdefault(name, len(self.locals))]


PAIRS = 339
LOCALS = 8
PIECES = ((0, 0, 512), (0, 512, 256), (1, 0, 512), (1, 512, 256), (2, 0, 512), (2, 512, 256))
SETS = (0, 0, 1, 1, 0, 0)
GATHER_PIECES = ((0, 0, 384), (0, 384, 384), (1, 0, 512), (1, 512, 256), (2, 0, 512), (2, 512, 256))
SIZE = {"y": 2, "z": 4, "x": 2}
GATHER = (
    ((0, 32, "zyx"), (32, 16, "zyx"), (48, 48, "zxy"),),
    ((0, 40, "zyx"), (40, 24, "yzx"), (64, 32, "yzx"),),
    ((0, 40, "zxy"), (40, 56, "zyx"),),
    ((0, 48, "yxz"), (48, 24, "xyz"), (72, 24, "zxy"),),
    ((0, 48, "xzy"), (48, 16, "zyx"), (64, 32, "xyz"),),
    ((0, 48, "yzx"), (48, 48, "zxy"),),
)
SCATTER = (
    ((0, 48, "yxz"), (48, 8, "zyx"), (56, 40, "xzy"),),
    ((0, 16, "zxy"), (16, 40, "yxz"), (56, 40, "xyz"),),
    ((0, 32, "xyz"), (32, 16, "zxy"), (48, 48, "yxz"),),
    ((0, 8, "xzy"), (8, 88, "zxy"),),
    ((0, 40, "xyz"), (40, 32, "yxz"), (72, 24, "zyx"),),
    ((0, 96, "xyz"),),
)
KIND_GATHER, KIND_PUSH, KIND_SCATTER, KIND_CORE, KIND_OWN, KIND_ROWS, KIND_SMALL = 1, 2, 3, 4, 5, 6, 7
KIND_GATHER_RELAY, KIND_SCATTER_RELAY = 8, 9
TOK, COEF, COT, OUT, CG, TG = 6000, 6001, 6002, 6003, 6004, 6005
PARAMS, SUM_C, SUM_X, SUM_Y, SUM_Z = 7000, 7001, 7002, 7003, 7004
PACK, PACKUD, STICKY, NORM1, X0_, X0T_, ATTNOUT, NORM2, COTT_, OUTS_, NORM2B, RB0, TOK1, TOK2 = range(14)
PJ1, PJ2, MEM1, MEM2, AT1, AT2, UP1, UP2, GD1, GD2, DN1, DN2, GU1, GU2, BU, AB1, AB2, GS1, GS2 = range(20, 39)
SCHEDULE = (
    PACK, 5000, 1000, 1010, TOK, 5100, PACKUD, 5300, 1310, 5200, 5400, 1400, 1420, 5500, STICKY, -5000, -5100, -5300,
    -5200, -5400, -5500, 1020, -1310, 2310, -2310, 1100, -1010, 2010, -1420, 2420, -1400, 2400, -2010, -2420, -2400,
    -1000, 2000, -2000, 1011, 1320, 1001, 1200, -1020, 2020, 1021, COEF, 1210, -2020, -1320, 8320, -1011, 2011, 1012,
    -1100, 2100, -2011, -TOK, NORM1, -1001, -2100, -8320, 2001, 1002, 1110, 1120, 1101, 2320, 1410, 1401, -1200,
    8200, -2001, -2320, -COEF, 1300, 1311, X0_, -1210, 1321, 8210, 1421, -1021, 2021, 1022, -1012, 2012, -1110, 2110,
    1111, -1120, 2120, -2110, -2012, -2021, -1410, -2120, -8200, 1121, 2200, 1201, -1300, -2200, 2300, -1311, 2311,
    -1321, 2321, 1301, -2300, -2311, -1002, 2002, -2321, -1101, 2101, 1102, -2002, -1421, 2421, -2101, -2421, 1322,
    -8210, 1312, 2210, 1211, -1301, 2301, -1111, 2111, -2301, -2210, 1112, -1201, 2201, -2111, -2201, -1022, 2022,
    1302, -1401, 1202, -1322, 2322, -2022, PJ1, -1121, -2322, 2121, 1122, PJ1, PJ1, -2121, -1102, 2102, PJ1, -1112,
    -1312, 2112, MEM1, MEM1, MEM1, -2102, MEM1, COT, 8312, 8410, 8401, 1422, AT1, -2112, -1211, 2211, 1212, AT1,
    -2211, AT1, -1122, -8410, 2122, 2410, AT1, -2122, -2410, 1411, PJ2, -1302, 8302, PJ2, PJ2, PJ2, -8312, 2312,
    1500, MEM2, MEM2, MEM2, 1510, MEM2, AT2, -2312, AT2, AT2, AT2, -8401, 2401, 1402, X0T_, -COT, -1202, -1500, 2202,
    2500, 1501, -1411, 2411, 1412, -2401, ATTNOUT, -2202, -1212, -2411, -1510, -2500, 2212, 8510, NORM2, -1422, 8422,
    -8302, 2302, -2212, UP1, UP1, -2302, UP1, -1412, -8510, 2412, 2510, 1511, -1501, 8501, UP1, UP2, -2412, -2510,
    UP2, UP2, UP2, COTT_, GD1, -8422, 2422, GD1, -8501, 2501, 1502, GD1, -1402, 2402, -1511, 2511, 1512, GD1, -2422,
    -2501, 4400, GD2, GD2, -2511, GD2, GD2, -2402, 4500, DN1, DN1, DN1, DN1, GU1, -4500, 3500, -4400, 3410, 3420,
    -1502, 2502, GU1, -1512, 2512, GU1, -2502, GU1, -2512, 4200, DN2, DN2, DN2, DN2, OUTS_, OUT, GU2, GU2, GU2, GU2,
    4300, BU, BU, -4200, 3200, 3210, BU, -4300, 3310, BU, 3220, NORM2B, -3420, 9420, -3410, AB1, -3500, 3501, 3411,
    AB1, -OUT, 3400, AB1, -3200, -3210, -9420, -3411, 9210, 3412, AB1, 3201, 3300, GS1, 3421, GS1, -3501, 3502, GS1,
    -9210, 3211, -3220, 3221, GS1, -3412, -3300, 4000, 9412, 3301, -3400, 3401, AB2, -3421, -3310, 3422, 9310, AB2,
    -3201, -3211, 3202, 3212, -3301, -4000, 3000, 3010, 3020, -3502, -9412, 9502, AB2, -3422, AB2, -3212, -3221,
    -3401, 3222, GS2, GS2, 3402, GS2, GS2, -3202, 9202, 4100, RB0, -3010, -4100, 9010, CG, 3100, 3120, TOK1, -9502,
    -3020, -3000, 3021, 3001, 3110, TOK2, -9202, -3222, -9010, -3402, -3120, -3100, -9310, SUM_C, 9222, 3011, 9402,
    3121, 3311, -CG, -SUM_C, SUM_X, 9100, TG, -3001, 3002, -3110, 3111, 9301, -3011, 3012, -3021, 9021, -SUM_X,
    SUM_Y, -9402, -3311, -9100, 3101, -9222, -3121, 3122, -3012, -9301, -3111, 3112, -3101, 3102, -SUM_Y, SUM_Z,
    -3002, -3122, 9002, 3312, -9021, 3022, 9122, -3102, -3112, 9112, 3302, -SUM_Z, -9122, -3302, -3312, -3022, -9112,
    -9002, -TG,
)


def scatter_shape(piece, j, i):
    _, rows, order = SCATTER[piece][j]
    rest = [SIZE[d] for d in "yzx" if d in order[i + 1 :]]
    lead = [4] if order[i] == "z" else []
    return tuple(lead + rest + [rows, PIECES[piece][2]])


SCATTER_KEYS = [(p, j, i) for p in range(6) for j in range(len(SCATTER[p])) for i in range(3)]


def fused_kernel(
    tok_in, coef_in, cot_in, wq_ref, wk_ref, wv_ref, wo_ref, wu_ref, wd_ref, mu_ref, sigma_ref, flag_ref, spot_ref,
    gain1_ref, gain2_ref, fita_ref, past_ref,
    out_o, tg_o, cg_o, wg_o, small_o,
    W, G, RCA, RCB, RS, RZ,
    VTOK, VCOEF, VCOT, X0, X0T, COTT, N2, N2T, DHL, DHLT, PK, MEM, PR, CTX, HID, ACC, ACT, GP, SMP,
    TK, DQ, DM, SP, SPT, OUTS, ST1, ST2,
    *rest,
):
    bufs = dict(zip(SCATTER_KEYS, rest[: len(SCATTER_KEYS)]))
    send, recv, local = rest[len(SCATTER_KEYS) :]
    sems = Sems(send, recv, local)
    dp, mp = lax.axis_index("dp"), lax.axis_index("mp")
    z, x, y, c = dp // 2, dp % 2, mp // 2, mp % 2
    ox, oy, oc = 1 - x, 1 - y, 1 - c
    z_next = {k: (z + k) % 4 for k in (1, 2, 3)}
    z_prev = {k: (z - k + 4) % 4 for k in (1, 2, 3)}
    m_next = {k: (mp + k) % 4 for k in (1, 2, 3)}
    m_prev = {k: (mp - k + 4) % 4 for k in (1, 2, 3)}
    root = 0.125
    every = slice(None)
    to = {"c": (dp, y * 2 + oc), "y": (dp, oy * 2 + c), "x": (z * 2 + ox, mp)}
    to_mp = {k: (dp, m_next[k]) for k in (1, 2, 3)}
    to_z = {k: (z_next[k] * 2 + x, mp) for k in (1, 2, 3)}

    pending = {}

    def start(name, src, dst, dev):
        s, r = sems.pair(name)
        pltpu.make_async_remote_copy(
            src_ref=src, dst_ref=dst, send_sem=s, recv_sem=r, device_id=dev, device_id_type=MESH
        ).start()

    def wait_recv(name, region, dev):
        s, r = sems.pair(name)
        pltpu.make_async_remote_copy(
            src_ref=region, dst_ref=region, send_sem=s, recv_sem=r, device_id=dev, device_id_type=MESH
        ).wait_recv()

    def drain(group):
        for code in pending.pop(group, []):
            for k, src, dst, dev, _ in copies(code):
                s, r = sems.pair((code, k))
                at_z(senders(code, k), lambda: pltpu.make_async_remote_copy(
                    src_ref=src, dst_ref=dst, send_sem=s, recv_sem=r, device_id=dev, device_id_type=MESH
                ).wait_send())

    barrier = pltpu.get_barrier_semaphore()
    for dev in (to_mp[1], to_mp[2], to_mp[3], to["x"], to_z[1], to_z[2], to_z[3]):
        pl.semaphore_signal(barrier, inc=1, device_id=dev, device_id_type=MESH)
    pl.semaphore_wait(barrier, 7)

    GD, GU, GA = G.at[0], G.at[1], W.at[1]
    grads = {0: GA, 1: GU, 2: GD}

    def rows_in(src, dst, n):
        return [
            (k, src.at[m_next[k]], dst.at[pl.ds(mp * n, n)], to_mp[k], dst.at[pl.ds(m_prev[k] * n, n)])
            for k in (1, 2, 3)
        ], (src.at[mp], dst.at[pl.ds(mp * n, n)])

    def rows_out(src, dst, n):
        return [
            (k, src.at[pl.ds(m_next[k] * n, n)], dst.at[mp], to_mp[k], dst.at[m_prev[k]]) for k in (1, 2, 3)
        ], (src.at[pl.ds(mp * n, n)], dst.at[mp])

    def row_copies(code):
        if code == TOK:
            return rows_in(tok_in, VTOK, 128)
        if code == COEF:
            return rows_in(coef_in, VCOEF, 64)
        if code == COT:
            return rows_in(cot_in, VCOT, 64)
        if code == OUT:
            return rows_out(OUTS, out_o, 64)
        if code == CG:
            return rows_out(X0.at[pl.ds(0, 256)], cg_o, 64)
        return rows_out(X0.at[pl.ds(256, 512)], tg_o, 128)

    def parts_of(code):
        return code // 1000, code // 100 % 10, code // 10 % 10, code % 10

    def gather_part(code):
        _, piece, j, i = parts_of(code)
        a, col, wide = GATHER_PIECES[piece]
        lo, n, order = GATHER[piece][j]
        d = order[i]
        at = {ax: (every if ax in order[:i] else near) for ax, near in (("y", y), ("z", z), ("x", x))}

        def region(cc, axis=None, index=None):
            use = {**at, axis: index}
            return W.at[a, use["y"], cc, use["z"], use["x"], pl.ds(lo, n), pl.ds(col, wide)]

        def brings(cc):
            if d == "z":
                return [(k, region(cc, d, z_prev[k])) for k in (1, 2, 3)]
            return [(0, region(cc, d, oy if d == "y" else ox))]

        return d, region(c), brings, region

    def scatter_part(code):
        _, piece, j, i = parts_of(code)
        a, col, wide = PIECES[piece]
        lo, n, order = SCATTER[piece][j]
        rest_axes = [ax for ax in "yzx" if ax in order[i + 1 :]]
        return a, pl.ds(col, wide), lo, n, order[i], rest_axes, i, bufs[(piece, j, i)]

    def copies(code):
        kind, piece, _, _ = parts_of(code)
        if kind == KIND_ROWS:
            return row_copies(code)[0]
        if code == PARAMS:
            return [(k, SMP.at[mp], SMP.at[mp], to_mp[k], SMP.at[m_prev[k]]) for k in (1, 2, 3)]
        if code == SUM_Z:
            return [(k, RS.at[6], RZ.at[k - 1], to_z[k], RZ.at[k - 1]) for k in (1, 2, 3)]
        if kind == KIND_SMALL:
            i = code - SUM_C
            return [(0, RS.at[2 * i], RS.at[2 * i + 1], to["cxy"[i]], RS.at[2 * i + 1])]
        a, col, wide = (GATHER_PIECES if kind == KIND_OWN else PIECES)[piece]
        cols = pl.ds(col, wide)
        if kind == KIND_OWN:
            mine = W.at[a, y, c, z, x, every, cols]
            return [(0, mine, mine, to["c"], W.at[a, y, oc, z, x, every, cols])]
        if kind == KIND_GATHER:
            d, src, brings, _ = gather_part(code)
            return [(k, src, src, to_z[k] if k else to[d], region) for k, region in brings(c)]
        if kind == KIND_GATHER_RELAY:
            region = gather_part(code - 7000)[3]
            return [(k, region(c, "z", z_prev[2]), region(c, "z", z_prev[2]), to_z[k], region(c, "z", z_prev[4 - k])) for k in (1, 3)]
        if kind == KIND_PUSH:
            brings = gather_part(code)[2]
            return [(k, mine, mine, to["c"], theirs) for (k, mine), (_, theirs) in zip(brings(c), brings(oc))]
        if kind == KIND_CORE:
            buf = (RCA, RCB)[piece % 2].at[SETS[piece]]
            return [(0, grads[a].at[every, oc, every, every, every, cols], buf, to["c"], buf)]
        a, cols, lo, n, d, rest_axes, i, buf = scatter_part(code)
        at = {ax: (every if ax in rest_axes else near) for ax, near in (("y", y), ("z", z), ("x", x))}

        def send(index):
            use = {**at, d: index}
            return grads[a].at[use["y"], c, use["z"], use["x"], pl.ds(lo, n), cols]

        if kind == KIND_SCATTER_RELAY:
            return [(2, send(z_next[2]), buf.at[1], to_z[2], buf.at[1])]
        if d == "z":
            direct = [(k, send(z_next[k]), buf.at[k - 1], to_z[k], buf.at[k - 1]) for k in (1, 2, 3)]
            return direct + [(4, send(z_next[3]), buf.at[3], to_z[1], buf.at[3]), (5, send(z_next[1]), buf.at[3], to_z[3], buf.at[3])]
        return [(0, send(oy if d == "y" else ox), buf, to[d], buf)]

    def along_z(code):
        kind, piece, j, i = parts_of(code)
        if kind == KIND_GATHER:
            return piece > 1 and GATHER[piece][j][2][i] == "z"
        if kind == KIND_SCATTER:
            return SCATTER[piece][j][2][i] == "z"
        return kind in (KIND_GATHER_RELAY, KIND_SCATTER_RELAY)

    def senders(code, k):
        kind = code // 1000
        if not along_z(code):
            return None
        if kind == KIND_GATHER:
            return {1: (0, 1, 2), 2: (0, 1, 2, 3), 3: (1, 2, 3)}[k]
        if kind == KIND_GATHER_RELAY:
            return {1: (2,), 3: (1,)}[k]
        if kind == KIND_SCATTER:
            return {1: (0, 1, 2), 2: (0, 3), 3: (1, 2, 3), 4: (0,), 5: (3,)}[k]
        return (1, 2)

    def at_z(which, todo):
        if which is None or len(which) == 4:
            todo()
            return
        test = z == which[0]
        for one in which[1:]:
            test = test | (z == one)
        pl.when(test)(todo)

    def step_of(code, k):
        return {4: 1, 5: 3}.get(k, k)

    def receivers(code, k):
        which = senders(code, k)
        if which is None:
            return None
        return tuple(sorted((one + step_of(code, k)) % 4 for one in which))

    def go(code):
        kind, piece, _, _ = parts_of(code)
        if kind == KIND_SMALL and code != PARAMS:
            RS[2 * (code - SUM_C)] = small_o[...]
        gathers = kind in (KIND_GATHER, KIND_PUSH, KIND_OWN, KIND_GATHER_RELAY) and PIECES[piece][0] == 1
        pending.setdefault(gathers, []).append(code)
        for k, src, dst, dev, _ in copies(code):
            at_z(senders(code, k), lambda: start((code, k), src, dst, dev))
        if kind == KIND_ROWS:
            src, dst = row_copies(code)[1]
            pltpu.make_async_copy(src, dst, sems.one(code)).start()

    def got(code):
        kind, piece, _, _ = parts_of(code)
        for k, _, _, dev, region in copies(code):
            at_z(receivers(code, k), lambda: wait_recv((code, k), region, dev))
        if kind == KIND_ROWS:
            src, dst = row_copies(code)[1]
            pltpu.make_async_copy(src, dst, sems.one(code)).wait()
        if code == SUM_Z:
            small_o[...] = RS[6] + RZ[0] + RZ[1] + RZ[2]
        elif kind == KIND_SMALL and code != PARAMS:
            small_o[...] = small_o[...] + RS[2 * (code - SUM_C) + 1]
        elif kind == KIND_CORE:
            core_sum(piece)
        elif kind == KIND_SCATTER and along_z(code):
            at_z((1, 2), lambda: relay_sum(code))
        elif kind == KIND_SCATTER:
            stage_sum(code, ())
        elif kind == KIND_SCATTER_RELAY:
            at_z((1, 2), lambda: stage_sum(code, (0, 1, 2)))
            at_z((0,), lambda: stage_sum(code, (1, 2)))
            at_z((3,), lambda: stage_sum(code, (0, 1)))

    def core_sum(piece):
        a, col, wide = PIECES[piece]
        g, s, buf = grads[a], SETS[piece], (RCA, RCB)[piece % 2]

        def add(q, carry):
            at = (q // 8, c, (q // 2) % 4, q % 2, every, pl.ds(col, wide))
            g[at] = g[at] + buf[s, q // 8, (q // 2) % 4, q % 2]
            return carry

        lax.fori_loop(0, 16, add, 0)

    def over_rest(rest_axes, todo, **fixed):
        def one(q, carry):
            at = {"y": y, "z": z, "x": x, **fixed}
            left = q
            for ax in reversed(rest_axes):
                at[ax] = left % SIZE[ax]
                left = left // SIZE[ax]
            todo(at["y"], at["z"], at["x"], tuple(at[ax] for ax in rest_axes))
            return carry

        lax.fori_loop(0, math.prod(SIZE[ax] for ax in rest_axes), one, 0)

    def relay_sum(code):
        a, cols, lo, n, d, rest_axes, i, buf = scatter_part(code)
        g, rows = grads[a], pl.ds(lo, n)

        def todo(yy, zz, xx, inner):
            here = (yy, c, zz, xx, rows, cols)
            g[here] = g[here] + buf[(3,) + inner]

        over_rest(rest_axes, todo, z=z_next[2])

    def stage_sum(code, slots):
        a, cols, lo, n, d, rest_axes, i, buf = scatter_part(code)
        g, rows = grads[a], pl.ds(lo, n)

        def todo(yy, zz, xx, inner):
            here = (yy, c, zz, xx, rows, cols)
            parts = [buf[(k,) + inner] for k in slots] if d == "z" else [buf[inner] if inner else buf[...]]
            if i == 2:
                total = g[here].astype(f32)
                for part in parts:
                    total = total + part.astype(f32)
                wg_o[a, rows, cols] = total
            elif d == "z":
                total = g[here].astype(f32)
                for part in parts:
                    total = total + part.astype(f32)
                g[here] = total.astype(bf16)
            else:
                g[here] = g[here] + parts[0]

        if i == 2:
            todo(y, z, x, ())
        else:
            over_rest(rest_axes, todo)

    width_rbf = 1.0 / NB
    cen = (lax.broadcasted_iota(jnp.int32, (1, NB), 1).astype(f32) + 0.5) / NB
    present = flag_ref[mp].astype(f32)
    g1 = gain1_ref[...].astype(f32).reshape(1, 768)
    g2 = gain2_ref[...].astype(f32).reshape(1, 768)

    def weight(a, m, col=0, n=768):
        return W[a, m // 2, m % 2, :, :, :, col : col + n].reshape(768, n)

    def pack():
        wot = wo_ref[...].astype(f32).T
        for i, ref in enumerate((wq_ref, wk_ref, wv_ref)):
            W[0, y, c, z, x, :, i * 128 : i * 128 + 128] = ref[:, 0:128]
        W[0, y, c, z, x, :, 384:512] = wot[:, 0:128].astype(bf16)
        last = (wq_ref[:, 128:192], wk_ref[:, 128:192], wv_ref[:, 128:192])
        last = [v.astype(f32) for v in last] + [wot[:, 128:192]]
        for i in (0, 1):
            both = jnp.concatenate(last[2 * i : 2 * i + 2], axis=1)
            W[0, y, c, z, x, :, 512 + i * 128 : 640 + i * 128] = both.astype(bf16)

    def packud():
        W[1, y, c, z, x] = wu_ref[...]
        W[2, y, c, z, x] = wd_ref[...]
        SMP[mp, 0:3, :] = mu_ref[...].astype(f32)
        SMP[mp, 3:6, :] = sigma_ref[...].astype(f32)
        SMP[mp, 6:8, :] = jnp.zeros((2, 256), f32)
        go(PARAMS)

    def sticky():
        cen_down = (lax.broadcasted_iota(jnp.int32, (NB, 1), 0).astype(f32) + 0.5) / NB
        spots = (spot_ref[pl.ds(mp, 1), :].astype(f32) + 0.5) / (2 * SEGMENT_TOKENS)
        samples = jnp.exp(-((spots - cen_down) ** 2) / (2.0 * width_rbf * width_rbf))
        fit = lax.dot_general(
            fita_ref[...], samples, (((1,), (1,)), ((), ())), precision=highest, preferred_element_type=f32
        )
        SP[:, 0:256] = fit.astype(bf16)
        SP[:, 256:512] = past_ref[...]
        SPT[0:256, :] = fit.T.astype(bf16)
        SPT[256:512, :] = past_ref[...].astype(f32).T.astype(bf16)

    def norm1():
        def one(i, carry):
            rows = pl.ds(pl.multiple_of(i * 128, 128), 128)
            v = VTOK[rows, :].astype(f32)
            mean = jnp.mean(v, axis=-1, keepdims=True)
            centred = v - mean
            inv = lax.rsqrt(jnp.mean(centred * centred, axis=-1, keepdims=True) + epsilon)
            ST1[rows, 0:1] = mean
            ST1[rows, 1:2] = inv
            X0[pl.ds(pl.multiple_of(256 + i * 128, 128), 128), :] = (centred * inv * g1).astype(bf16)
            return carry

        lax.fori_loop(0, 4, one, 0)

    def x0():
        X0[0:256, :] = (VCOEF[...].astype(f32) * present).astype(bf16)
        got(PARAMS)

    def x0t():
        for r in range(3):
            X0T[:, r * 256 : (r + 1) * 256] = X0[r * 256 : (r + 1) * 256, :].astype(f32).T.astype(bf16)

    def project(m, col, wide):
        PK[m, :, col : col + wide] = nn(X0[...], weight(0, m, col, wide)).astype(bf16)

    def memory(m, first, col):
        MEM[m, :, col : col + 256] = nn(SP[...], PK[m, 0:512, first : first + 256]).astype(bf16)

    lane = lax.broadcasted_iota(jnp.int32, (256, 128), 1)
    row_i = lax.broadcasted_iota(jnp.int32, (256, 512), 0)
    col_i = lax.broadcasted_iota(jnp.int32, (256, 512), 1)
    upper = lane >= 64

    lower = jnp.logical_not(upper)
    HEADS = ((0, 1, 2, lower, lower, 0, 128), (0, 1, 2, upper, upper, 0, 128), (4, 4, 5, upper, lower, 256, 384))

    def head_query(m, h):
        qb, lanes = HEADS[h][0], HEADS[h][3]
        q = PK[m, 512:768, qb * 128 : qb * 128 + 128].astype(f32)
        if h == 2:
            q = pltpu.roll(q, 64, 1)
        return jnp.where(lanes, q * root, 0.0).astype(bf16)

    row8 = lax.broadcasted_iota(jnp.int32, (8, 128), 0)
    lane8 = lax.broadcasted_iota(jnp.int32, (8, 128), 1)
    low8, up8 = lane8 < 64, lane8 >= 64

    def split(v):
        top = v.astype(bf16)
        return top, (v - top.astype(f32)).astype(bf16)

    def memory_vectors(m, heads):
        first = HEADS[heads[0]][5]
        u = nn(SMP[m].astype(bf16), MEM[m, :, first : first + 128])
        if heads[0] == 0:
            keep = ((row8 % 2 == 0) & low8) | ((row8 % 2 == 1) & up8)
            rows = jnp.concatenate([u[0:2], u[3:5], jnp.zeros((4, 128), f32)], axis=0)
            return jnp.where(keep, rows, 0.0)
        rows = jnp.concatenate([u[2:3], u[7:8], u[5:6], u[7:8], jnp.zeros((4, 128), f32)], axis=0)
        return jnp.where(up8, rows, 0.0)

    def spread_of(m, heads, q8, vec):
        top, rest = split(vec)
        last = (vec - top.astype(f32) - rest.astype(f32)).astype(bf16)
        wide = jnp.concatenate([top, rest, last], axis=1)
        wide = jnp.concatenate([wide, jnp.zeros((120, 384), bf16)], axis=0)
        lg = nt(jnp.concatenate([q8, q8, q8], axis=1), wide)
        sil = pltpu.roll(lg, 126, 1)
        mean = 1.0 / (1.0 + jnp.exp(-lg))
        soft = jnp.maximum(sil, 0.0) + jnp.log1p(jnp.exp(-jnp.abs(sil)))
        spread = soft * spread_scale + width_rbf * width_rbf
        inv_s = 1.0 / spread
        return sil, mean, inv_s, width_rbf * lax.rsqrt(spread), -0.5 * inv_s

    def reach_of(i, mean, factor, rate):
        dist = mean[:, i : i + 1] - cen
        return dist, factor[:, i : i + 1] * jnp.exp(rate[:, i : i + 1] * (dist * dist))

    def attend(m, heads):
        parts = []
        qms = [head_query(m, h) for h in heads]
        q8 = qms[0] + qms[1] if heads[0] == 0 else qms[0]
        _, mean, _, factor, rate = spread_of(m, heads, q8, memory_vectors(m, heads))
        for i, h in enumerate(heads):
            qb, kb, vb, klanes, vlanes, mk0, mv0 = HEADS[h]
            s = nt(qms[i], PK[m, 256:768, kb * 128 : kb * 128 + 128])
            s = jnp.where(col_i - 256 <= row_i, s, -1e30)
            top = jnp.max(s, axis=-1, keepdims=True)
            e = jnp.exp(s - top)
            p = (e * (1.0 / jnp.sum(e, axis=-1, keepdims=True))).astype(bf16)
            PR[m, h] = p
            ctx = nn(p, PK[m, 256:768, vb * 128 : vb * 128 + 128])
            reach = reach_of(i, mean, factor, rate)[1]
            parts.append(ctx + nn(reach.astype(bf16), MEM[m, :, mv0 : mv0 + 128]))
        if heads[0] == 0:
            CTX[m, :, 0:128] = jnp.where(upper, parts[1], parts[0]).astype(bf16)
        else:
            CTX[m, :, 128:256] = jnp.where(upper, pltpu.roll(parts[0], 64, 1), 0.0).astype(bf16)

    def attnout():
        HID[...] = VTOK[256:512, :].astype(f32)

        def one(m, carry):
            wo = jnp.concatenate([weight(0, m, 384, 128), weight(0, m, 640, 128)], axis=1)
            HID[...] += nt(CTX[m], wo)
            return carry

        lax.fori_loop(0, 4, one, 0)

    def norm2():
        hid = HID[...]
        mean = jnp.mean(hid, axis=-1, keepdims=True)
        centred = hid - mean
        inv = lax.rsqrt(jnp.mean(centred * centred, axis=-1, keepdims=True) + epsilon)
        ST2[:, 0:1] = mean
        ST2[:, 1:2] = inv
        normed = centred * inv * g2
        N2[...] = normed.astype(bf16)
        N2T[...] = normed.T.astype(bf16)
        ACC[...] = hid

    def up(m, col, wide):
        cols = slice(col, col + wide)
        u = nn(N2[...], weight(1, m, col, wide))
        u2 = u * u
        th = jnp.tanh(gelu_coef * (u + 0.044715 * u2 * u))
        ACT[m, :, cols] = (0.5 * u * (1.0 + th)).astype(bf16)
        GP[m, :, cols] = 0.5 * (1.0 + th) + (0.5 * gelu_coef) * u * (1.0 - th * th) * (1.0 + 0.134145 * u2)

    def cott():
        COTT[...] = VCOT[...].astype(f32).T.astype(bf16)

    def put(g, m, col, wide, left, right):
        g[m // 2, m % 2, :, :, :, col : col + wide] = nn(left[...], right).reshape(4, 2, 96, wide).astype(bf16)

    def grad_down(m, col, wide):
        put(GD, m, col, wide, COTT, ACT[m, :, col : col + wide])

    def down(m, col, wide):
        cols = slice(col, col + wide)
        wd = weight(2, m, col, wide)
        ACC[...] += nt(ACT[m, :, cols], wd)
        d_act = nn(VCOT[...], wd)
        ACT[m, :, cols] = (d_act * GP[m, :, cols]).astype(bf16)

    def outs():
        OUTS[...] = ACC[...].astype(bf16)
        ACC[...] = jnp.zeros_like(ACC)

    def grad_up(m, col, wide):
        put(GU, m, col, wide, N2T, ACT[m, :, col : col + wide])

    def back_up(m):
        ACC[...] += nt(ACT[m], weight(1, m))

    def norm2b():
        d_n2 = ACC[...]
        flat = (HID[...] - ST2[:, 0:1]) * ST2[:, 1:2]
        g2_grad = jnp.sum(d_n2 * flat, axis=0, keepdims=True)
        e = d_n2 * g2
        d_hidden = VCOT[...].astype(f32) + ST2[:, 1:2] * (
            e - jnp.mean(e, axis=-1, keepdims=True) - flat * jnp.mean(e * flat, axis=-1, keepdims=True)
        )
        HID[...] = d_hidden
        DHL[...] = d_hidden.astype(bf16)
        DHLT[...] = d_hidden.T.astype(bf16)
        for i in range(3):
            small_o[27 + i : 28 + i, :] = g2_grad[:, i * 256 : (i + 1) * 256]

    lane_i = lax.broadcasted_iota(jnp.int32, (256, 128), 1)

    def attend_back(m, heads):
        pair = heads[0] == 0
        d_ctx = nn(DHL[...], weight(0, m, 384 if pair else 640, 128))
        if not pair:
            d_ctx = pltpu.roll(d_ctx, 64, 1)
        qms = [head_query(m, h) for h in heads]
        q8 = qms[0] + qms[1] if pair else qms[0]
        vec = memory_vectors(m, heads)
        sil, mean, inv_s, factor, rate = spread_of(m, heads, q8, vec)
        sums = []
        d_ks, d_vs, d_qs, d_mvs = [], [], [], []
        for i, h in enumerate(heads):
            qb, kb, vb, klanes, vlanes, mk0, mv0 = HEADS[h]
            dc = jnp.where(vlanes, d_ctx, 0.0).astype(bf16)
            p = PR[m, h]
            d_p = nt(dc, PK[m, 256:768, vb * 128 : vb * 128 + 128])
            pf = p.astype(f32)
            t = pf * d_p
            d_s = (t - pf * jnp.sum(t, axis=-1, keepdims=True)).astype(bf16)
            d_v = tn(p, dc)
            d_k = tn(d_s, qms[i])
            d_q = jnp.where(klanes, nn(d_s, PK[m, 256:768, kb * 128 : kb * 128 + 128]), 0.0)
            dist, reach = reach_of(i, mean, factor, rate)
            d_r = nt(dc, MEM[m, :, mv0 : mv0 + 128])
            d_mv = tn(reach.astype(bf16), dc)
            t = d_r * reach
            td = t * dist
            sums.append([jnp.sum(v, axis=-1, keepdims=True) for v in (t, td, td * dist)])
            if i == 0:
                TK[0] = d_k
                TK[1] = d_v
                DQ[...] = d_q
                DM[:, 128:256] = d_mv.astype(bf16)
            else:
                TK[0] += d_k
                TK[1] += d_v
                DQ[...] += d_q
                DM[:, 128:256] += d_mv.astype(bf16)
        s0, s1, s2 = (jnp.where(lane_i == 0, sums[0][k], sums[-1][k]) for k in range(3))
        g_mu = -s1 * inv_s * mean * (1.0 - mean)
        g_sg = (s2 * inv_s - s0) * (0.5 * inv_s) * spread_scale * (1.0 / (1.0 + jnp.exp(-sil)))
        used = 2 if pair else 1
        both = jnp.where(lane_i < used, g_mu, 0.0) + pltpu.roll(jnp.where(lane_i < used, g_sg, 0.0), 2, 1)
        grad = both.T[0:8]
        grad_top, grad_rest = split(grad)
        qg = nn(jnp.concatenate([grad_top, grad_rest], axis=1), jnp.concatenate([q8, q8], axis=0))
        own = (((row8 % 2 == 0) & low8) | ((row8 % 2 == 1) & up8)) if pair else up8
        qg_top, qg_rest = split(jnp.where(own, qg, 0.0))
        par = SMP[m].astype(bf16).astype(f32)
        if pair:
            par = jnp.concatenate([par[0:2], par[3:5], jnp.zeros((4, 256), f32)], axis=0)
        else:
            par = jnp.concatenate([par[2:3], par[7:8], par[5:6], par[7:8], jnp.zeros((4, 256), f32)], axis=0)
        par = par.astype(bf16)
        qg_all = jnp.concatenate([qg_top, qg_rest], axis=0)
        DM[:, 0:128] = tn(jnp.concatenate([par, par], axis=0), qg_all).astype(bf16)
        vec_top, vec_rest = split(vec)
        mem_q = tn(
            jnp.concatenate([grad_top, grad_top, grad_rest, jnp.zeros((8, 256), bf16)], axis=0),
            jnp.concatenate([vec_top, vec_rest, vec_top, jnp.zeros((8, 128), bf16)], axis=0),
        )
        mu_sg = nt(qg_all, MEM[m, :, HEADS[heads[0]][5] : HEADS[heads[0]][5] + 128])
        mu_sg = mu_sg[0:8] + mu_sg[8:16]
        for i, h in enumerate(heads):
            small_o[pl.ds(m * 3 + h, 1), :] = mu_sg[i : i + 1]
            small_o[pl.ds(12 + m * 3 + h, 1), :] = mu_sg[2 + i : 3 + i]
        d_q = (DQ[...] + mem_q) * root
        DQ[...] = d_q if pair else pltpu.roll(d_q, 64, 1)
        back = nn(SPT[...], DM[...])
        first = 128 if heads[0] == 0 else 512
        for i in range(2):
            b = back[:, 128 * i : 128 * i + 128]
            cols = slice(first + 128 * i, first + 128 * i + 128)
            PK[m, 0:256, cols] = (b[0:256] * present).astype(bf16)
            PK[m, 256:512, cols] = (TK[i, 0:256] + b[256:512]).astype(bf16)
            now = TK[i, 256:512]
            if heads[0] == 2 and i == 0:
                now = now + DQ[...]
            PK[m, 512:768, cols] = now.astype(bf16)
        if heads[0] == 0:
            PK[m, 0:512, 0:128] = jnp.zeros((512, 128), bf16)
            PK[m, 512:768, 0:128] = DQ[...].astype(bf16)
            PK[m, :, 384:512] = jnp.zeros((768, 128), bf16)

    def grad_square(m, col, wide):
        own = 0 if col == 0 else 128

        val = nn(X0T[...], PK[m, :, col : col + wide])
        out_part = nn(DHLT[...], CTX[m, :, own : own + 128])
        val = jnp.concatenate([val[:, : wide - 128], val[:, wide - 128 :] + out_part], axis=1)
        GA[m // 2, m % 2, :, :, :, col : col + wide] = val.reshape(4, 2, 96, wide).astype(bf16)

    def rows_back(r):
        ACC[...] = jnp.zeros_like(ACC)

        def one(m, carry):
            ACC[...] += nt(PK[m, r * 256 : (r + 1) * 256, :], weight(0, m))
            return carry

        lax.fori_loop(0, 4, one, 0)

    def token_rows(r, first, extra):
        rows_back(r)
        d_n1 = ACC[...]
        rows = slice(first, first + 256)
        inv_1 = ST1[rows, 1:2]
        flat_1 = (VTOK[rows, :].astype(f32) - ST1[rows, 0:1]) * inv_1
        part = jnp.sum(d_n1 * flat_1, axis=0, keepdims=True)
        e = d_n1 * g1
        grad = inv_1 * (
            e - jnp.mean(e, axis=-1, keepdims=True) - flat_1 * jnp.mean(e * flat_1, axis=-1, keepdims=True)
        )
        if extra:
            grad = grad + HID[...]
        X0[256 + first : 512 + first, :] = grad.astype(bf16)
        return part

    def rb0():
        rows_back(0)
        X0[0:256, :] = ACC[...].astype(bf16)

    def tok1():
        part = token_rows(1, 0, False)
        for i in range(3):
            small_o[24 + i : 25 + i, :] = part[:, i * 256 : (i + 1) * 256]

    def tok2():
        part = token_rows(2, 256, True)
        for i in range(3):
            small_o[24 + i : 25 + i, :] = small_o[24 + i : 25 + i, :] + part[:, i * 256 : (i + 1) * 256]
        small_o[30:32, :] = jnp.zeros((2, 256), f32)

    single = {
        PACK: pack, PACKUD: packud, STICKY: sticky, NORM1: norm1, X0_: x0, X0T_: x0t, ATTNOUT: attnout, NORM2: norm2,
        COTT_: cott, OUTS_: outs, NORM2B: norm2b, RB0: rb0, TOK1: tok1, TOK2: tok2,
    }
    looped = {
        PJ1: lambda m: project(m, 0, 384), PJ2: lambda m: project(m, 512, 256),
        MEM1: lambda m: memory(m, 128, 0), MEM2: lambda m: memory(m, 512, 256),
        AT1: lambda m: attend(m, (0, 1)), AT2: lambda m: attend(m, (2,)),
        UP1: lambda m: up(m, 0, 512), UP2: lambda m: up(m, 512, 256),
        GD1: lambda m: grad_down(m, 0, 512), GD2: lambda m: grad_down(m, 512, 256),
        DN1: lambda m: down(m, 0, 512), DN2: lambda m: down(m, 512, 256),
        GU1: lambda m: grad_up(m, 0, 512), GU2: lambda m: grad_up(m, 512, 256), BU: back_up,
        AB1: lambda m: attend_back(m, (0, 1)), AB2: lambda m: attend_back(m, (2,)),
        GS1: lambda m: grad_square(m, 0, 512), GS2: lambda m: grad_square(m, 512, 256),
    }

    def transfer(item):
        if item > 0:
            go(item)
        else:
            got(-item)

    at = 0
    while at < len(SCHEDULE):
        item = SCHEDULE[at]
        at += 1
        if abs(item) > 999:
            transfer(item)
        elif item in single:
            single[item]()
        else:
            if item in (GS1, GS2):
                drain(True)
            between = {}
            done = 0
            while done < 3:
                if abs(SCHEDULE[at]) > 999:
                    between.setdefault(done, []).append(SCHEDULE[at])
                else:
                    done += 1
                at += 1

            def step(m, carry, item=item, between=between):
                looped[item](m)
                for i, items in between.items():

                    @pl.when(m == i)
                    def _(items=items):
                        for one in items:
                            transfer(one)

                return carry

            lax.fori_loop(0, 4, step, 0)
    for group in list(pending):
        drain(group)


def finish_kernel(
    out_b, tg_b, cg_b, wg, sums, out, tg, cg, g1, gq, gk, gv, go, gm, gs, g2, gu, gd,
):
    me = lax.axis_index("mp")
    out[...] = out_b[...]
    tg[...] = tg_b[...].astype(f32)
    cg[...] = cg_b[...].astype(f32)
    for i, ref in enumerate((gq, gk, gv)):
        ref[:, 0:128] = wg[0, :, 128 * i : 128 * i + 128]
        at = 512 + 128 * (i // 2)
        block = wg[0, :, at : at + 128]
        ref[:, 128:192] = block[:, 64 * (i % 2) : 64 * (i % 2) + 64]
    go[0:128, :] = wg[0, :, 384:512].T
    go[128:192, :] = wg[0, :, 640:768].T[64:128, :]
    gu[...] = wg[1]
    gd[...] = wg[2]
    for h in range(3):
        gm[h : h + 1, :] = sums[pl.ds(me * 3 + h, 1), :]
        gs[h : h + 1, :] = sums[pl.ds(12 + me * 3 + h, 1), :]
    for i in range(3):
        g1[pl.ds(i * 256, 256)] = sums[24 + i]
        g2[pl.ds(i * 256, 256)] = sums[27 + i]


def fused_call(*args):
    any_ = pl.BlockSpec(memory_space=pl.ANY)
    vm = pl.BlockSpec(memory_space=pltpu.VMEM)
    sm = pl.BlockSpec(memory_space=pltpu.SMEM)
    V = pltpu.VMEM
    return pl.pallas_call(
        fused_kernel,
        out_shape=(
            jax.ShapeDtypeStruct((4, 64, 768), bf16),
            jax.ShapeDtypeStruct((4, 128, 768), bf16),
            jax.ShapeDtypeStruct((4, 64, 768), bf16),
            jax.ShapeDtypeStruct((3, 96, 768), f32),
            jax.ShapeDtypeStruct((32, 256), f32),
        ),
        in_specs=[any_] * 3 + [vm] * 8 + [sm] + [vm] * 5,
        out_specs=(any_, any_, any_, vm, vm),
        scratch_shapes=[
            V((3, 2, 2, 4, 2, 96, 768), bf16),
            V((2, 2, 2, 4, 2, 96, 768), bf16),
            V((2, 2, 4, 2, 96, 512), bf16),
            V((2, 2, 4, 2, 96, 256), bf16),
            V((7, 32, 256), f32),
            V((3, 32, 256), f32),
            V((512, 768), bf16),
            V((256, 768), bf16),
            V((256, 768), bf16),
            V((768, 768), bf16),
            V((768, 768), bf16),
            V((768, 256), bf16),
            V((256, 768), bf16),
            V((768, 256), bf16),
            V((256, 768), bf16),
            V((768, 256), bf16),
            V((4, 768, 768), bf16),
            V((4, 256, 512), bf16),
            V((4, 3, 256, 512), bf16),
            V((4, 256, 256), bf16),
            V((256, 768), f32),
            V((256, 768), f32),
            V((4, 256, 768), bf16),
            V((4, 256, 768), f32),
            V((4, 8, 256), f32),
            V((2, 512, 128), f32),
            V((256, 128), f32),
            V((256, 256), bf16),
            V((256, 512), bf16),
            V((512, 256), bf16),
            V((256, 768), bf16),
            V((512, 128), f32),
            V((256, 128), f32),
            *(V(scatter_shape(p, j, i), bf16) for p, j, i in SCATTER_KEYS),
            pltpu.SemaphoreType.DMA((PAIRS,)),
            pltpu.SemaphoreType.DMA((PAIRS,)),
            pltpu.SemaphoreType.DMA((LOCALS,)),
        ],
        compiler_params=pltpu.CompilerParams(
            collective_id=0, has_side_effects=True, vmem_limit_bytes=63 * 1024 * 1024
        ),
    )(*args)


def fused_body(
    tokens, coeffs, present_flag, sticky_pos, gain_one, w_query, w_key, w_value, w_out, mu_weight,
    sigma_weight, gain_two, w_up, w_down, cotangent,
):
    _, fitting = basis_tables(NB, SEGMENT_TOKENS)
    fita = jnp.asarray(fitting[:, :SEGMENT_TOKENS])
    past = jnp.asarray(fitting[:, SEGMENT_TOKENS:]).astype(bf16)
    parts = fused_call(
        tokens, coeffs, cotangent, w_query, w_key, w_value, w_out, w_up, w_down.T, mu_weight, sigma_weight,
        present_flag, sticky_pos, gain_one, gain_two, fita, past,
    )

    def like(v):
        return jax.ShapeDtypeStruct(v.shape, f32)

    shapes = (
        jax.ShapeDtypeStruct(cotangent.shape, bf16), like(tokens), like(coeffs), like(gain_one), like(w_query),
        like(w_key), like(w_value), like(w_out), like(mu_weight), like(sigma_weight), like(gain_two), like(w_up),
        like(w_down.T),
    )
    vm = pl.BlockSpec(memory_space=pltpu.VMEM)
    done = pl.pallas_call(
        finish_kernel, out_shape=shapes, in_specs=[vm] * 5, out_specs=(vm,) * 13,
    )(*parts)
    return (*done[:12], done[12].T)


def solution(mesh):
    in_specs = (
        P("dp", "mp", None), P("dp", "mp", None), P("dp"), P("dp", None), P(), P("dp", "mp"), P("dp", "mp"),
        P("dp", "mp"), P("mp", "dp"), P("mp", None), P("mp", None), P(), P("dp", "mp"), P("mp", "dp"),
        P("dp", "mp", None),
    )
    out_specs = (
        P("dp", "mp", None), P("dp", "mp", None), P("dp", "mp", None), P(), P("dp", "mp"), P("dp", "mp"),
        P("dp", "mp"), P("mp", "dp"), P("mp", None), P("mp", None), P(), P("dp", "mp"), P("mp", "dp"),
    )
    whole = body
    if mesh.shape["dp"] == 8 and mesh.shape["mp"] == 4:
        whole = fused_body
    return jax.shard_map(whole, mesh=mesh, in_specs=in_specs, out_specs=out_specs, check_vma=False)
```

```python
import math

import jax
import jax.numpy as jnp
import numpy as np
from jax import lax
from jax.experimental import pallas as pl
from jax.experimental.pallas import tpu as pltpu
from jax.sharding import PartitionSpec as P

HD = 64
NB = 256
SEGMENT_TOKENS = 256
BOTH = ("dp", "mp")

highest = lax.Precision.HIGHEST
epsilon = 1e-05
ridge = 0.5
spread_scale = 1.0 / 64.0
gelu_coef = 0.7978845608028654


def basis_tables(basis_count, seg_len):
    centers = (np.arange(basis_count) + 0.5) / basis_count
    width = 1.0 / basis_count
    times = (np.arange(2 * seg_len) + 0.5) / (2 * seg_len)
    design = np.exp(-((times[:, None] - centers[None, :]) ** 2) / (2.0 * width * width))
    normal = design.T @ design + ridge * np.eye(basis_count)
    fitting = np.linalg.solve(normal, design.T)
    return centers.astype(np.float32), fitting.astype(np.float32)


def norm_rows(values):
    centered = values - jnp.mean(values, axis=-1, keepdims=True)
    inverse = lax.rsqrt(jnp.mean(centered * centered, axis=-1, keepdims=True) + epsilon)
    return (centered * inverse, inverse)


def gelu_tanh(values):
    return (
        0.5 * values * (1.0 + jnp.tanh(gelu_coef * (values + 0.044715 * values * values * values)))
    )


def memory_reach(mem_scores, mu_in, sigma_in, centers):
    rbf_width = 1.0 / centers.shape[0]
    mu_logit = jnp.einsum("...hn,hn->...h", mem_scores, mu_in, precision=highest)
    sigma_logit = jnp.einsum("...hn,hn->...h", mem_scores, sigma_in, precision=highest)
    mean_pos = jax.nn.sigmoid(mu_logit)
    spread = jax.nn.softplus(sigma_logit) * spread_scale + rbf_width * rbf_width
    distance = mean_pos[..., None] - centers
    return (
        rbf_width
        * lax.rsqrt(spread)[..., None]
        * jnp.exp(-distance * distance / (2.0 * spread[..., None]))
    )


def mm(pattern, left_in, right_in):
    return jnp.einsum(pattern, left_in, right_in, preferred_element_type=jnp.float32)


def norm_back(grad, flat_rows, inverse, gain_vec):
    scaled = grad * gain_vec
    return inverse * (
        scaled
        - jnp.mean(scaled, axis=-1, keepdims=True)
        - flat_rows * jnp.mean(scaled * flat_rows, axis=-1, keepdims=True)
    )


def low(v):
    return v.astype(jnp.bfloat16)


def whole_sequences(
    tokens, coeffs, present_flag, sticky_pos, gain_one, wq, wk, wv, wo, mu, sigma, gain_two, wu, wdt, cot
):
    count, length, width = tokens.shape
    cur = cot.shape[1]
    past = length - cur
    heads = width // HD
    root = math.sqrt(HD)
    centers, fitting = basis_tables(NB, SEGMENT_TOKENS)
    rbf_width = 1.0 / NB
    past_fit = jnp.asarray(fitting[:, SEGMENT_TOKENS:]).astype(jnp.bfloat16)
    centers = jnp.asarray(centers)
    g1 = gain_one.astype(jnp.float32)
    g2 = gain_two.astype(jnp.float32)
    mu = mu.astype(jnp.float32)
    sigma = sigma.astype(jnp.float32)
    causal = jnp.arange(length)[None, :] <= (past + jnp.arange(cur))[:, None]
    present = present_flag.astype(jnp.float32)[:, None, None]
    spots = (sticky_pos.astype(jnp.float32) + 0.5) / (2 * SEGMENT_TOKENS)
    samples = jnp.exp(-((spots[:, :, None] - centers) ** 2) / (2.0 * rbf_width * rbf_width))
    sticky = low(
        jnp.einsum("nm,bmk->bnk", jnp.asarray(fitting[:, :SEGMENT_TOKENS]), samples, precision=highest)
    )
    rows = tokens.astype(jnp.float32)
    flat_one, inv_one = norm_rows(rows)
    normed = low(flat_one * g1)
    q = low(mm("bld,de->ble", normed[:, past:], wq))
    k = low(mm("bld,de->ble", normed, wk))
    v = low(mm("bld,de->ble", normed, wv))
    ck = low(present * mm("bnd,de->bne", coeffs, wk))
    cv = low(present * mm("bnd,de->bne", coeffs, wv))
    mk = low(mm("bnm,bme->bne", sticky, ck) + mm("np,bpe->bne", past_fit, k[:, :past]))
    mv = low(mm("bnm,bme->bne", sticky, cv) + mm("np,bpe->bne", past_fit, v[:, :past]))
    qh = q.reshape(count, cur, heads, HD)
    kh = k.reshape(count, length, heads, HD)
    vh = v.reshape(count, length, heads, HD)
    mkh = mk.reshape(count, NB, heads, HD)
    mvh = mv.reshape(count, NB, heads, HD)
    scores = mm("bqhd,bkhd->bhqk", qh, kh) / root
    masked = jnp.where(causal, scores, -1e30)
    probs = jax.nn.softmax(masked, axis=-1)
    probs_low = low(probs)
    short = mm("bhqk,bkhd->bqhd", probs_low, vh)
    mem_scores = mm("bqhd,bnhd->bqhn", qh, mkh) / root

    def reach_of(s, m, g):
        return memory_reach(s, m, g, centers)

    reach, reach_pull = jax.vjp(reach_of, mem_scores, mu, sigma)
    reach_low = low(reach)
    long_part = mm("bqhn,bnhd->bqhd", reach_low, mvh)
    context = low((short + long_part).reshape(count, cur, width))
    hidden = rows[:, past:] + mm("bqd,de->bqe", context, wo)
    flat_two, inv_two = norm_rows(hidden)
    normed_two = low(flat_two * g2)
    up = mm("bqd,df->bqf", normed_two, wu)
    active_rows, gelu_pull = jax.vjp(gelu_tanh, up)
    active = low(active_rows)
    output = low(hidden + mm("bqf,df->bqd", active, wdt))
    wdt_grad = mm("bqd,bqf->df", cot, active)
    d_up = low(gelu_pull(mm("bqd,df->bqf", cot, wdt))[0])
    wu_grad = mm("bqd,bqf->df", normed_two, d_up)
    d_n2 = mm("bqf,df->bqd", d_up, wu)
    g2_grad = jnp.sum(d_n2 * flat_two, axis=(0, 1))
    d_hidden = cot.astype(jnp.float32) + norm_back(d_n2, flat_two, inv_two, g2)
    d_hidden_low = low(d_hidden)
    wo_grad = mm("bqd,bqe->de", context, d_hidden_low)
    d_context = low(mm("bqe,de->bqd", d_hidden_low, wo)).reshape(count, cur, heads, HD)
    d_probs = mm("bqhd,bkhd->bhqk", d_context, vh)
    d_scores = low(probs * (d_probs - jnp.sum(probs * d_probs, axis=-1, keepdims=True)))
    d_reach = mm("bqhd,bnhd->bqhn", d_context, mvh)
    d_mv = low(mm("bqhn,bqhd->bnhd", reach_low, d_context)).reshape(count, NB, width)
    d_ms, mu_grad, sigma_grad = reach_pull(d_reach)
    d_ms = low(d_ms)
    dq = low(
        (mm("bhqk,bkhd->bqhd", d_scores, kh) + mm("bqhn,bnhd->bqhd", d_ms, mkh)) / root
    ).reshape(count, cur, width)
    d_mk = low(mm("bqhn,bqhd->bnhd", d_ms, qh) / root).reshape(count, NB, width)
    keep = present_flag.astype(jnp.bfloat16)[:, None, None]
    d_ck = low(mm("bnm,bne->bme", sticky, d_mk)) * keep
    d_cv = low(mm("bnm,bne->bme", sticky, d_mv)) * keep
    dk = (mm("bhqk,bqhd->bkhd", d_scores, qh) / root).reshape(count, length, width)
    dv = mm("bhqk,bqhd->bkhd", probs_low, d_context).reshape(count, length, width)
    pad = ((0, 0), (0, cur), (0, 0))
    dk = low(dk + jnp.pad(mm("np,bne->bpe", past_fit, d_mk), pad))
    dv = low(dv + jnp.pad(mm("np,bne->bpe", past_fit, d_mv), pad))
    wq_grad = mm("bqd,bqe->de", normed[:, past:], dq)
    wk_grad = mm("bld,ble->de", normed, dk) + mm("bnd,bne->de", coeffs, d_ck)
    wv_grad = mm("bld,ble->de", normed, dv) + mm("bnd,bne->de", coeffs, d_cv)
    d_n1 = mm("ble,de->bld", dk, wk) + mm("ble,de->bld", dv, wv)
    d_n1 = d_n1 + jnp.pad(mm("bqe,de->bqd", dq, wq), ((0, 0), (past, 0), (0, 0)))
    coeff_grad = mm("bne,de->bnd", d_ck, wk) + mm("bne,de->bnd", d_cv, wv)
    g1_grad = jnp.sum(d_n1 * flat_one, axis=(0, 1))
    token_grad = norm_back(d_n1, flat_one, inv_one, g1) + jnp.pad(
        d_hidden, ((0, 0), (past, 0), (0, 0))
    )
    return (
        output, token_grad, coeff_grad, g1_grad, wq_grad, wk_grad, wv_grad, wo_grad,
        mu_grad, sigma_grad, g2_grad, wu_grad, wdt_grad,
    )


def to_sequences(rows):
    return lax.all_to_all(rows, "mp", 0, 1, tiled=True)


def to_rows(rows):
    return lax.all_to_all(rows, "mp", 1, 0, tiled=True)


def body(
    tokens, coeffs, present_flag, sticky_pos, gain_one, w_query, w_key, w_value, w_out, mu_weight,
    sigma_weight, gain_two, w_up, w_down, cotangent,
):
    dp, mp = lax.axis_size("dp"), lax.axis_size("mp")
    me = lax.axis_index("mp")
    count = tokens.shape[0] // mp
    depth, share = w_query.shape
    inner = w_up.shape[1]
    width = depth * dp
    seq_tokens = to_sequences(tokens)
    seq_coeffs = to_sequences(coeffs)
    seq_cot = to_sequences(cotangent)
    flags = lax.dynamic_slice_in_dim(present_flag, me * count, count, 0)
    spots = lax.dynamic_slice_in_dim(sticky_pos, me * count, count, 0)
    heads_local = mu_weight.shape[0]
    mu, sigma = lax.all_gather((mu_weight, sigma_weight), "mp", axis=0, tiled=True)
    square = jnp.concatenate([w_query, w_key, w_value, w_out.T], axis=1)
    packed = jnp.concatenate([square, w_up, w_down.T], axis=1)
    whole = lax.all_gather(packed, BOTH, axis=0, tiled=False)
    whole = whole.reshape(dp, mp, depth, packed.shape[1]).transpose(0, 2, 1, 3)
    whole = whole.reshape(width, mp, packed.shape[1])

    def columns(first, size):
        return whole[:, :, first : first + size].reshape(width, mp * size)

    wq, wk, wv, wot = (columns(i * share, share) for i in range(4))
    wu = columns(4 * share, inner)
    wdt = columns(4 * share + inner, inner)
    (
        output, token_grad, coeff_grad, g1_grad, wq_grad, wk_grad, wv_grad, wo_grad,
        mu_grad, sigma_grad, g2_grad, wu_grad, wdt_grad,
    ) = whole_sequences(
        seq_tokens, seq_coeffs, flags, spots, gain_one, wq, wk, wv, wot.T, mu, sigma, gain_two, wu, wdt, seq_cot
    )

    def blocks(grad):
        return low(grad).reshape(dp, depth, mp, grad.shape[1] // mp).transpose(0, 2, 1, 3)

    def scatter(grad):
        stacked = blocks(grad)
        stacked = stacked.reshape((dp * mp * depth, stacked.shape[3]))
        return lax.psum_scatter(stacked, BOTH, scatter_dimension=0, tiled=True).astype(jnp.float32)

    wdt_own = scatter(wdt_grad)
    wu_own = scatter(wu_grad)
    square_own = scatter(
        jnp.concatenate(
            [g.reshape(width, mp, share) for g in (wq_grad, wk_grad, wv_grad, wo_grad.T)], axis=2
        ).reshape(width, mp * 4 * share)
    )
    small = lax.psum((mu_grad, sigma_grad, g1_grad, g2_grad), BOTH)
    mu_own = lax.dynamic_slice_in_dim(small[0], me * heads_local, heads_local, 0)
    sigma_own = lax.dynamic_slice_in_dim(small[1], me * heads_local, heads_local, 0)
    return (
        to_rows(output),
        to_rows(low(token_grad)).astype(jnp.float32),
        to_rows(low(coeff_grad)).astype(jnp.float32),
        small[2],
        square_own[:, :share],
        square_own[:, share : 2 * share],
        square_own[:, 2 * share : 3 * share],
        square_own[:, 3 * share :].T,
        mu_own,
        sigma_own,
        small[3],
        wu_own,
        wdt_own.T,
    )


f32 = jnp.float32
bf16 = jnp.bfloat16
MESH = pl.DeviceIdType.MESH


def nn(a, b):
    return jnp.dot(a, b, preferred_element_type=f32)


def nt(a, b):
    return lax.dot_general(a, b, (((1,), (1,)), ((), ())), preferred_element_type=f32)


def tn(a, b):
    return lax.dot_general(a, b, (((0,), (0,)), ((), ())), preferred_element_type=f32)


class Sems:
    def __init__(self, send, recv, local):
        self.send, self.recv, self.local, self.names, self.locals = send, recv, local, {}, {}

    def pair(self, name):
        i = self.names.setdefault(name, len(self.names))
        return self.send.at[i], self.recv.at[i]

    def one(self, name):
        return self.local.at[self.locals.setdefault(name, len(self.locals))]


PAIRS = 281
LOCALS = 8
PIECES = ((0, 0, 512), (0, 512, 256), (1, 0, 512), (1, 512, 256), (2, 0, 512), (2, 512, 256))
SETS = (0, 0, 1, 1, 0, 0)
GATHER_PIECES = ((0, 0, 384), (0, 384, 384), (1, 0, 512), (1, 512, 256), (2, 0, 512), (2, 512, 256))
SIZE = {"y": 2, "z": 4, "x": 2}
GATHER = (
    ((0, 32, "yzx"), (32, 24, "zyx"), (56, 40, "zxy"),),
    ((0, 72, "zyx"), (72, 24, "zxy"),),
    ((0, 64, "zyx"), (64, 32, "xzy"),),
    ((0, 56, "yxz"), (56, 40, "yzx"),),
    ((0, 32, "xzy"), (32, 40, "zyx"), (72, 24, "xzy"),),
    ((0, 96, "xzy"),),
)
SCATTER = (
    ((0, 40, "yxz"), (40, 16, "xyz"), (56, 40, "xzy"),),
    ((0, 16, "xzy"), (16, 32, "xyz"), (48, 48, "yxz"),),
    ((0, 48, "xyz"), (48, 48, "yzx"),),
    ((0, 96, "xyz"),),
    ((0, 48, "yxz"), (48, 48, "zxy"),),
    ((0, 96, "xyz"),),
)
KIND_GATHER, KIND_PUSH, KIND_SCATTER, KIND_CORE, KIND_OWN, KIND_ROWS, KIND_SMALL = 1, 2, 3, 4, 5, 6, 7
KIND_GATHER_RELAY, KIND_SCATTER_RELAY = 8, 9
TOK, COEF, COT, OUT, CG, TG = 6000, 6001, 6002, 6003, 6004, 6005
PARAMS, SUM_C, SUM_X, SUM_Y, SUM_Z = 7000, 7001, 7002, 7003, 7004
PACK, PACKUD, STICKY, NORM1, X0_, X0T_, ATTNOUT, NORM2, COTT_, OUTS_, NORM2B, RB0, TOK1, TOK2 = range(14)
PJ1, PJ2, MEM1, MEM2, AT1, AT2, UP1, UP2, GD1, GD2, DN1, DN2, GU1, GU2, BU, AB1, AB2, GS1, GS2 = range(20, 39)
SCHEDULE = (
    PACK, 5000, 1000, 1010, 1020, TOK, 5100, PACKUD, -5000, 5200, 1210, 5400, 1400, 1420, 5300, 5500, 1500, -5100,
    STICKY, -1000, -5200, -5400, -5300, -5500, 2000, 1001, -2000, -1010, 2010, -1210, -1420, 2210, 2420, -1400, 2400,
    -2010, 1100, -2210, -2420, -1500, 1011, 2500, -1020, -2400, 2020, 1021, -2500, -2020, COEF, -1001, 2001, 1002,
    1110, 1200, 1300, 1310, -1021, -1011, 2021, 2011, 1022, -2001, -TOK, NORM1, -2011, -2021, -1100, 1012, 2100,
    1211, -1310, 2310, -1300, 2300, -2100, -1110, 2110, 1111, -2310, -2300, -COEF, 1101, X0_, -2110, 1301, -1002,
    2002, -2002, 1410, -1200, 8200, -1022, 2022, 1421, -1012, -1111, 2012, 2111, 1112, -1301, 2301, -2022, -2111,
    -2301, -2012, 1401, PJ1, -1211, 8211, -1101, -8200, 2101, 1102, 2200, 1201, -1410, PJ1, PJ1, -2101, -2200, PJ1,
    8410, 1311, MEM1, -1112, 2112, MEM1, MEM1, MEM1, AT1, -2112, -8211, -1421, 2211, 1212, 8421, 1302, AT1, -2211,
    -8410, 2410, -1201, 2201, 1202, AT1, -2201, -2410, -1401, 1411, AT1, -8421, -1311, 2421, -1102, 2102, 8401, 8311,
    1501, COT, 1422, -2421, -2102, PJ2, PJ2, PJ2, -1212, 2212, PJ2, MEM2, MEM2, MEM2, MEM2, AT2, -2212, AT2, AT2,
    -1302, 8302, AT2, -8311, 2311, 1312, X0T_, -8401, -1411, -2311, 2401, 2411, 1402, ATTNOUT, -1202, -2401, -2411,
    -1501, 2202, 1412, 8501, NORM2, -8302, 2302, -2202, UP1, UP1, -1422, -2302, -1312, -COT, 2422, 2312, UP1, UP1,
    -2422, -2312, -8501, 2501, 1502, UP2, UP2, UP2, -2501, UP2, COTT_, -1402, 2402, GD1, GD1, -2402, GD1, -1412,
    2412, GD1, 4400, GD2, GD2, GD2, -2412, GD2, 4500, DN1, DN1, DN1, DN1, GU1, -4500, 3500, -4400, 3400, 3410, -1502,
    2502, GU1, GU1, GU1, -2502, 4200, DN2, DN2, DN2, DN2, OUTS_, OUT, GU2, GU2, GU2, GU2, 4300, BU, BU, -4200, 3200,
    BU, -4300, BU, 3210, NORM2B, AB1, -3500, AB1, -3410, 3300, 9410, AB1, -OUT, -3200, -3400, 3201, AB1, GS1, -9410,
    3501, 3401, GS1, -3210, 3211, GS1, GS1, 4000, 3411, AB2, -3201, -3300, 3202, 3301, AB2, -4000, 3010, AB2, -3501,
    3502, 3000, 3020, -3401, 3402, -3411, AB2, GS2, GS2, -3301, 3302, -3211, 9211, GS2, -3010, GS2, 4100, RB0, -3202,
    -4100, 9202, 3011, 3100, 3110, 3120, TOK1, -9211, -3000, -3020, 3212, 3001, 3021, 3412, -9202, -3502, -3402,
    9502, CG, -3302, -3011, -3100, 9302, TOK2, -3212, -3110, SUM_C, 3012, 3101, 3111, 9402, TG, -SUM_C, -3120, -3412,
    SUM_X, 3121, -3001, 3002, -9502, -9302, -3021, 9021, -3012, 9012, -CG, -3101, 9101, -SUM_X, SUM_Y, -9402, -3111,
    3112, -3121, 3122, -3002, 9002, -9012, -9101, 3102, -SUM_Y, SUM_Z, -9021, 3022, -3112, 9112, -3102, -3122, 9122,
    -9002, -3022, -SUM_Z, -9112, -TG, -9122,
)


def scatter_shape(piece, j, i):
    _, rows, order = SCATTER[piece][j]
    rest = [SIZE[d] for d in "yzx" if d in order[i + 1 :]]
    lead = [4] if order[i] == "z" else []
    return tuple(lead + rest + [rows, PIECES[piece][2]])


SCATTER_KEYS = [(p, j, i) for p in range(6) for j in range(len(SCATTER[p])) for i in range(3)]


def fused_kernel(
    tok_in, coef_in, cot_in, wq_ref, wk_ref, wv_ref, wo_ref, wu_ref, wd_ref, mu_ref, sigma_ref, flag_ref, spot_ref,
    gain1_ref, gain2_ref, fita_ref, past_ref,
    out_o, tg_o, cg_o, wg_o, small_o,
    W, G, RCA, RCB, RS, RZ,
    VTOK, VCOEF, VCOT, X0, X0T, COTT, N2, N2T, DHL, DHLT, PK, MEM, PR, CTX, HID, ACC, ACT, GP, SMP,
    TK, DQ, DM, SP, SPT, OUTS, ST1, ST2,
    *rest,
):
    bufs = dict(zip(SCATTER_KEYS, rest[: len(SCATTER_KEYS)]))
    send, recv, local = rest[len(SCATTER_KEYS) :]
    sems = Sems(send, recv, local)
    dp, mp = lax.axis_index("dp"), lax.axis_index("mp")
    z, x, y, c = dp // 2, dp % 2, mp // 2, mp % 2
    ox, oy, oc = 1 - x, 1 - y, 1 - c
    z_next = {k: (z + k) % 4 for k in (1, 2, 3)}
    z_prev = {k: (z - k + 4) % 4 for k in (1, 2, 3)}
    m_next = {k: (mp + k) % 4 for k in (1, 2, 3)}
    m_prev = {k: (mp - k + 4) % 4 for k in (1, 2, 3)}
    root = 0.125
    every = slice(None)
    to = {"c": (dp, y * 2 + oc), "y": (dp, oy * 2 + c), "x": (z * 2 + ox, mp)}
    to_mp = {k: (dp, m_next[k]) for k in (1, 2, 3)}
    to_z = {k: (z_next[k] * 2 + x, mp) for k in (1, 2, 3)}

    pending = {}

    def start(name, src, dst, dev):
        s, r = sems.pair(name)
        pltpu.make_async_remote_copy(
            src_ref=src, dst_ref=dst, send_sem=s, recv_sem=r, device_id=dev, device_id_type=MESH
        ).start()

    def wait_recv(name, region, dev):
        s, r = sems.pair(name)
        pltpu.make_async_remote_copy(
            src_ref=region, dst_ref=region, send_sem=s, recv_sem=r, device_id=dev, device_id_type=MESH
        ).wait_recv()

    def drain(group):
        for code in pending.pop(group, []):
            for k, src, dst, dev, _ in copies(code):
                s, r = sems.pair((code, k))
                at_z(senders(code, k), lambda: pltpu.make_async_remote_copy(
                    src_ref=src, dst_ref=dst, send_sem=s, recv_sem=r, device_id=dev, device_id_type=MESH
                ).wait_send())

    barrier = pltpu.get_barrier_semaphore()
    for dev in (to_mp[1], to_mp[2], to_mp[3], to["x"], to_z[1], to_z[2], to_z[3]):
        pl.semaphore_signal(barrier, inc=1, device_id=dev, device_id_type=MESH)
    pl.semaphore_wait(barrier, 7)

    GD, GU, GA = G.at[0], G.at[1], W.at[1]
    grads = {0: GA, 1: GU, 2: GD}

    def rows_in(src, dst, n):
        return [
            (k, src.at[m_next[k]], dst.at[pl.ds(mp * n, n)], to_mp[k], dst.at[pl.ds(m_prev[k] * n, n)])
            for k in (1, 2, 3)
        ], (src.at[mp], dst.at[pl.ds(mp * n, n)])

    def rows_out(src, dst, n):
        return [
            (k, src.at[pl.ds(m_next[k] * n, n)], dst.at[mp], to_mp[k], dst.at[m_prev[k]]) for k in (1, 2, 3)
        ], (src.at[pl.ds(mp * n, n)], dst.at[mp])

    def row_copies(code):
        if code == TOK:
            return rows_in(tok_in, VTOK, 128)
        if code == COEF:
            return rows_in(coef_in, VCOEF, 64)
        if code == COT:
            return rows_in(cot_in, VCOT, 64)
        if code == OUT:
            return rows_out(OUTS, out_o, 64)
        if code == CG:
            return rows_out(X0.at[pl.ds(0, 256)], cg_o, 64)
        return rows_out(X0.at[pl.ds(256, 512)], tg_o, 128)

    def parts_of(code):
        return code // 1000, code // 100 % 10, code // 10 % 10, code % 10

    def gather_part(code):
        _, piece, j, i = parts_of(code)
        a, col, wide = GATHER_PIECES[piece]
        lo, n, order = GATHER[piece][j]
        d = order[i]
        at = {ax: (every if ax in order[:i] else near) for ax, near in (("y", y), ("z", z), ("x", x))}

        def region(cc, axis=None, index=None):
            use = {**at, axis: index}
            return W.at[a, use["y"], cc, use["z"], use["x"], pl.ds(lo, n), pl.ds(col, wide)]

        def brings(cc):
            if d == "z":
                return [(k, region(cc, d, z_prev[k])) for k in (1, 2, 3)]
            return [(0, region(cc, d, oy if d == "y" else ox))]

        return d, region(c), brings, region

    def scatter_part(code):
        _, piece, j, i = parts_of(code)
        a, col, wide = PIECES[piece]
        lo, n, order = SCATTER[piece][j]
        rest_axes = [ax for ax in "yzx" if ax in order[i + 1 :]]
        return a, pl.ds(col, wide), lo, n, order[i], rest_axes, i, bufs[(piece, j, i)]

    def copies(code):
        kind, piece, _, _ = parts_of(code)
        if kind == KIND_ROWS:
            return row_copies(code)[0]
        if code == PARAMS:
            return [(k, SMP.at[mp], SMP.at[mp], to_mp[k], SMP.at[m_prev[k]]) for k in (1, 2, 3)]
        if code == SUM_Z:
            return [(k, RS.at[6], RZ.at[k - 1], to_z[k], RZ.at[k - 1]) for k in (1, 2, 3)]
        if kind == KIND_SMALL:
            i = code - SUM_C
            return [(0, RS.at[2 * i], RS.at[2 * i + 1], to["cxy"[i]], RS.at[2 * i + 1])]
        a, col, wide = (GATHER_PIECES if kind == KIND_OWN else PIECES)[piece]
        cols = pl.ds(col, wide)
        if kind == KIND_OWN:
            mine = W.at[a, y, c, z, x, every, cols]
            return [(0, mine, mine, to["c"], W.at[a, y, oc, z, x, every, cols])]
        if kind == KIND_GATHER:
            d, src, brings, _ = gather_part(code)
            return [(k, src, src, to_z[k] if k else to[d], region) for k, region in brings(c)]
        if kind == KIND_GATHER_RELAY:
            region = gather_part(code - 7000)[3]
            return [(k, region(c, "z", z_prev[2]), region(c, "z", z_prev[2]), to_z[k], region(c, "z", z_prev[4 - k])) for k in (1, 3)]
        if kind == KIND_PUSH:
            brings = gather_part(code)[2]
            return [(k, mine, mine, to["c"], theirs) for (k, mine), (_, theirs) in zip(brings(c), brings(oc))]
        if kind == KIND_CORE:
            buf = (RCA, RCB)[piece % 2].at[SETS[piece]]
            return [(0, grads[a].at[every, oc, every, every, every, cols], buf, to["c"], buf)]
        a, cols, lo, n, d, rest_axes, i, buf = scatter_part(code)
        at = {ax: (every if ax in rest_axes else near) for ax, near in (("y", y), ("z", z), ("x", x))}

        def send(index):
            use = {**at, d: index}
            return grads[a].at[use["y"], c, use["z"], use["x"], pl.ds(lo, n), cols]

        if kind == KIND_SCATTER_RELAY:
            return [(2, send(z_next[2]), buf.at[1], to_z[2], buf.at[1])]
        if d == "z":
            direct = [(k, send(z_next[k]), buf.at[k - 1], to_z[k], buf.at[k - 1]) for k in (1, 2, 3)]
            return direct + [(4, send(z_next[3]), buf.at[3], to_z[1], buf.at[3]), (5, send(z_next[1]), buf.at[3], to_z[3], buf.at[3])]
        return [(0, send(oy if d == "y" else ox), buf, to[d], buf)]

    def along_z(code):
        kind, piece, j, i = parts_of(code)
        if kind == KIND_GATHER:
            return piece > 1 and GATHER[piece][j][2][i] == "z"
        if kind == KIND_SCATTER:
            return SCATTER[piece][j][2][i] == "z"
        return kind in (KIND_GATHER_RELAY, KIND_SCATTER_RELAY)

    def senders(code, k):
        kind = code // 1000
        if not along_z(code):
            return None
        if kind == KIND_GATHER:
            return {1: (0, 1, 2), 2: (0, 1, 2, 3), 3: (1, 2, 3)}[k]
        if kind == KIND_GATHER_RELAY:
            return {1: (2,), 3: (1,)}[k]
        if kind == KIND_SCATTER:
            return {1: (0, 1, 2), 2: (0, 3), 3: (1, 2, 3), 4: (0,), 5: (3,)}[k]
        return (1, 2)

    def at_z(which, todo):
        if which is None or len(which) == 4:
            todo()
            return
        test = z == which[0]
        for one in which[1:]:
            test = test | (z == one)
        pl.when(test)(todo)

    def step_of(code, k):
        return {4: 1, 5: 3}.get(k, k)

    def receivers(code, k):
        which = senders(code, k)
        if which is None:
            return None
        return tuple(sorted((one + step_of(code, k)) % 4 for one in which))

    def go(code):
        kind, piece, _, _ = parts_of(code)
        if kind == KIND_SMALL and code != PARAMS:
            RS[2 * (code - SUM_C)] = small_o[...]
        gathers = kind in (KIND_GATHER, KIND_PUSH, KIND_OWN, KIND_GATHER_RELAY) and PIECES[piece][0] == 1
        pending.setdefault(gathers, []).append(code)
        for k, src, dst, dev, _ in copies(code):
            at_z(senders(code, k), lambda: start((code, k), src, dst, dev))
        if kind == KIND_ROWS:
            src, dst = row_copies(code)[1]
            pltpu.make_async_copy(src, dst, sems.one(code)).start()

    def got(code):
        kind, piece, _, _ = parts_of(code)
        for k, _, _, dev, region in copies(code):
            at_z(receivers(code, k), lambda: wait_recv((code, k), region, dev))
        if kind == KIND_ROWS:
            src, dst = row_copies(code)[1]
            pltpu.make_async_copy(src, dst, sems.one(code)).wait()
        if code == SUM_Z:
            small_o[...] = RS[6] + RZ[0] + RZ[1] + RZ[2]
        elif kind == KIND_SMALL and code != PARAMS:
            small_o[...] = small_o[...] + RS[2 * (code - SUM_C) + 1]
        elif kind == KIND_CORE:
            core_sum(piece)
        elif kind == KIND_SCATTER and along_z(code):
            at_z((1, 2), lambda: relay_sum(code))
        elif kind == KIND_SCATTER:
            stage_sum(code, ())
        elif kind == KIND_SCATTER_RELAY:
            at_z((1, 2), lambda: stage_sum(code, (0, 1, 2)))
            at_z((0,), lambda: stage_sum(code, (1, 2)))
            at_z((3,), lambda: stage_sum(code, (0, 1)))

    def core_sum(piece):
        a, col, wide = PIECES[piece]
        g, s, buf = grads[a], SETS[piece], (RCA, RCB)[piece % 2]

        def add(q, carry):
            at = (q // 8, c, (q // 2) % 4, q % 2, every, pl.ds(col, wide))
            g[at] = g[at] + buf[s, q // 8, (q // 2) % 4, q % 2]
            return carry

        lax.fori_loop(0, 16, add, 0)

    def over_rest(rest_axes, todo, **fixed):
        def one(q, carry):
            at = {"y": y, "z": z, "x": x, **fixed}
            left = q
            for ax in reversed(rest_axes):
                at[ax] = left % SIZE[ax]
                left = left // SIZE[ax]
            todo(at["y"], at["z"], at["x"], tuple(at[ax] for ax in rest_axes))
            return carry

        lax.fori_loop(0, math.prod(SIZE[ax] for ax in rest_axes), one, 0)

    def relay_sum(code):
        a, cols, lo, n, d, rest_axes, i, buf = scatter_part(code)
        g, rows = grads[a], pl.ds(lo, n)

        def todo(yy, zz, xx, inner):
            here = (yy, c, zz, xx, rows, cols)
            g[here] = g[here] + buf[(3,) + inner]

        over_rest(rest_axes, todo, z=z_next[2])

    def stage_sum(code, slots):
        a, cols, lo, n, d, rest_axes, i, buf = scatter_part(code)
        g, rows = grads[a], pl.ds(lo, n)

        def todo(yy, zz, xx, inner):
            here = (yy, c, zz, xx, rows, cols)
            parts = [buf[(k,) + inner] for k in slots] if d == "z" else [buf[inner] if inner else buf[...]]
            if i == 2:
                total = g[here].astype(f32)
                for part in parts:
                    total = total + part.astype(f32)
                wg_o[a, rows, cols] = total
            elif d == "z":
                total = g[here].astype(f32)
                for part in parts:
                    total = total + part.astype(f32)
                g[here] = total.astype(bf16)
            else:
                g[here] = g[here] + parts[0]

        if i == 2:
            todo(y, z, x, ())
        else:
            over_rest(rest_axes, todo)

    width_rbf = 1.0 / NB
    cen = (lax.broadcasted_iota(jnp.int32, (1, NB), 1).astype(f32) + 0.5) / NB
    present = flag_ref[mp].astype(f32)
    g1 = gain1_ref[...].astype(f32).reshape(1, 768)
    g2 = gain2_ref[...].astype(f32).reshape(1, 768)

    def weight(a, m, col=0, n=768):
        return W[a, m // 2, m % 2, :, :, :, col : col + n].reshape(768, n)

    def pack():
        wot = wo_ref[...].astype(f32).T
        for i, ref in enumerate((wq_ref, wk_ref, wv_ref)):
            W[0, y, c, z, x, :, i * 128 : i * 128 + 128] = ref[:, 0:128]
        W[0, y, c, z, x, :, 384:512] = wot[:, 0:128].astype(bf16)
        last = (wq_ref[:, 128:192], wk_ref[:, 128:192], wv_ref[:, 128:192])
        last = [v.astype(f32) for v in last] + [wot[:, 128:192]]
        for i in (0, 1):
            both = jnp.concatenate(last[2 * i : 2 * i + 2], axis=1)
            W[0, y, c, z, x, :, 512 + i * 128 : 640 + i * 128] = both.astype(bf16)

    def packud():
        W[1, y, c, z, x] = wu_ref[...]
        W[2, y, c, z, x] = wd_ref[...]
        SMP[mp, 0:3, :] = mu_ref[...].astype(f32)
        SMP[mp, 3:6, :] = sigma_ref[...].astype(f32)
        SMP[mp, 6:8, :] = jnp.zeros((2, 256), f32)
        go(PARAMS)

    def sticky():
        cen_down = (lax.broadcasted_iota(jnp.int32, (NB, 1), 0).astype(f32) + 0.5) / NB
        spots = (spot_ref[pl.ds(mp, 1), :].astype(f32) + 0.5) / (2 * SEGMENT_TOKENS)
        samples = jnp.exp(-((spots - cen_down) ** 2) / (2.0 * width_rbf * width_rbf))
        fit = lax.dot_general(
            fita_ref[...], samples, (((1,), (1,)), ((), ())), precision=highest, preferred_element_type=f32
        )
        SP[:, 0:256] = fit.astype(bf16)
        SP[:, 256:512] = past_ref[...]
        SPT[0:256, :] = fit.T.astype(bf16)
        SPT[256:512, :] = past_ref[...].astype(f32).T.astype(bf16)

    def norm1():
        def one(i, carry):
            rows = pl.ds(pl.multiple_of(i * 128, 128), 128)
            v = VTOK[rows, :].astype(f32)
            mean = jnp.mean(v, axis=-1, keepdims=True)
            centred = v - mean
            inv = lax.rsqrt(jnp.mean(centred * centred, axis=-1, keepdims=True) + epsilon)
            ST1[rows, 0:1] = mean
            ST1[rows, 1:2] = inv
            X0[pl.ds(pl.multiple_of(256 + i * 128, 128), 128), :] = (centred * inv * g1).astype(bf16)
            return carry

        lax.fori_loop(0, 4, one, 0)

    def x0():
        X0[0:256, :] = (VCOEF[...].astype(f32) * present).astype(bf16)
        got(PARAMS)

    def x0t():
        for r in range(3):
            X0T[:, r * 256 : (r + 1) * 256] = X0[r * 256 : (r + 1) * 256, :].astype(f32).T.astype(bf16)

    def project(m, col, wide):
        PK[m, :, col : col + wide] = nn(X0[...], weight(0, m, col, wide)).astype(bf16)

    def memory(m, first, col):
        MEM[m, :, col : col + 256] = nn(SP[...], PK[m, 0:512, first : first + 256]).astype(bf16)

    lane = lax.broadcasted_iota(jnp.int32, (256, 128), 1)
    row_i = lax.broadcasted_iota(jnp.int32, (256, 512), 0)
    col_i = lax.broadcasted_iota(jnp.int32, (256, 512), 1)
    upper = lane >= 64

    lower = jnp.logical_not(upper)
    HEADS = ((0, 1, 2, lower, lower, 0, 128), (0, 1, 2, upper, upper, 0, 128), (4, 4, 5, upper, lower, 256, 384))

    def head_query(m, h):
        qb, lanes = HEADS[h][0], HEADS[h][3]
        q = PK[m, 512:768, qb * 128 : qb * 128 + 128].astype(f32)
        if h == 2:
            q = pltpu.roll(q, 64, 1)
        return jnp.where(lanes, q * root, 0.0).astype(bf16)

    row8 = lax.broadcasted_iota(jnp.int32, (8, 128), 0)
    lane8 = lax.broadcasted_iota(jnp.int32, (8, 128), 1)
    low8, up8 = lane8 < 64, lane8 >= 64

    def split(v):
        top = v.astype(bf16)
        return top, (v - top.astype(f32)).astype(bf16)

    def memory_vectors(m, heads):
        first = HEADS[heads[0]][5]
        u = nn(SMP[m].astype(bf16), MEM[m, :, first : first + 128])
        if heads[0] == 0:
            keep = ((row8 % 2 == 0) & low8) | ((row8 % 2 == 1) & up8)
            rows = jnp.concatenate([u[0:2], u[3:5], jnp.zeros((4, 128), f32)], axis=0)
            return jnp.where(keep, rows, 0.0)
        rows = jnp.concatenate([u[2:3], u[7:8], u[5:6], u[7:8], jnp.zeros((4, 128), f32)], axis=0)
        return jnp.where(up8, rows, 0.0)

    def spread_of(m, heads, q8, vec):
        top, rest = split(vec)
        last = (vec - top.astype(f32) - rest.astype(f32)).astype(bf16)
        wide = jnp.concatenate([top, rest, last], axis=1)
        wide = jnp.concatenate([wide, jnp.zeros((120, 384), bf16)], axis=0)
        lg = nt(jnp.concatenate([q8, q8, q8], axis=1), wide)
        sil = pltpu.roll(lg, 126, 1)
        mean = 1.0 / (1.0 + jnp.exp(-lg))
        soft = jnp.maximum(sil, 0.0) + jnp.log1p(jnp.exp(-jnp.abs(sil)))
        spread = soft * spread_scale + width_rbf * width_rbf
        inv_s = 1.0 / spread
        return sil, mean, inv_s, width_rbf * lax.rsqrt(spread), -0.5 * inv_s

    def reach_of(i, mean, factor, rate):
        dist = mean[:, i : i + 1] - cen
        return dist, factor[:, i : i + 1] * jnp.exp(rate[:, i : i + 1] * (dist * dist))

    def attend(m, heads):
        parts = []
        qms = [head_query(m, h) for h in heads]
        q8 = qms[0] + qms[1] if heads[0] == 0 else qms[0]
        _, mean, _, factor, rate = spread_of(m, heads, q8, memory_vectors(m, heads))
        for i, h in enumerate(heads):
            qb, kb, vb, klanes, vlanes, mk0, mv0 = HEADS[h]
            s = nt(qms[i], PK[m, 256:768, kb * 128 : kb * 128 + 128])
            s = jnp.where(col_i - 256 <= row_i, s, -1e30)
            top = jnp.max(s, axis=-1, keepdims=True)
            e = jnp.exp(s - top)
            p = (e * (1.0 / jnp.sum(e, axis=-1, keepdims=True))).astype(bf16)
            PR[m, h] = p
            ctx = nn(p, PK[m, 256:768, vb * 128 : vb * 128 + 128])
            reach = reach_of(i, mean, factor, rate)[1]
            parts.append(ctx + nn(reach.astype(bf16), MEM[m, :, mv0 : mv0 + 128]))
        if heads[0] == 0:
            CTX[m, :, 0:128] = jnp.where(upper, parts[1], parts[0]).astype(bf16)
        else:
            CTX[m, :, 128:256] = jnp.where(upper, pltpu.roll(parts[0], 64, 1), 0.0).astype(bf16)

    def attnout():
        HID[...] = VTOK[256:512, :].astype(f32)

        def one(m, carry):
            wo = jnp.concatenate([weight(0, m, 384, 128), weight(0, m, 640, 128)], axis=1)
            HID[...] += nt(CTX[m], wo)
            return carry

        lax.fori_loop(0, 4, one, 0)

    def norm2():
        hid = HID[...]
        mean = jnp.mean(hid, axis=-1, keepdims=True)
        centred = hid - mean
        inv = lax.rsqrt(jnp.mean(centred * centred, axis=-1, keepdims=True) + epsilon)
        ST2[:, 0:1] = mean
        ST2[:, 1:2] = inv
        normed = centred * inv * g2
        N2[...] = normed.astype(bf16)
        N2T[...] = normed.T.astype(bf16)
        ACC[...] = hid

    def up(m, col, wide):
        cols = slice(col, col + wide)
        u = nn(N2[...], weight(1, m, col, wide))
        u2 = u * u
        th = jnp.tanh(gelu_coef * (u + 0.044715 * u2 * u))
        ACT[m, :, cols] = (0.5 * u * (1.0 + th)).astype(bf16)
        GP[m, :, cols] = 0.5 * (1.0 + th) + (0.5 * gelu_coef) * u * (1.0 - th * th) * (1.0 + 0.134145 * u2)

    def cott():
        COTT[...] = VCOT[...].astype(f32).T.astype(bf16)

    def put(g, m, col, wide, left, right):
        g[m // 2, m % 2, :, :, :, col : col + wide] = nn(left[...], right).reshape(4, 2, 96, wide).astype(bf16)

    def grad_down(m, col, wide):
        put(GD, m, col, wide, COTT, ACT[m, :, col : col + wide])

    def down(m, col, wide):
        cols = slice(col, col + wide)
        wd = weight(2, m, col, wide)
        ACC[...] += nt(ACT[m, :, cols], wd)
        d_act = nn(VCOT[...], wd)
        ACT[m, :, cols] = (d_act * GP[m, :, cols]).astype(bf16)

    def outs():
        OUTS[...] = ACC[...].astype(bf16)
        ACC[...] = jnp.zeros_like(ACC)

    def grad_up(m, col, wide):
        put(GU, m, col, wide, N2T, ACT[m, :, col : col + wide])

    def back_up(m):
        ACC[...] += nt(ACT[m], weight(1, m))

    def norm2b():
        d_n2 = ACC[...]
        flat = (HID[...] - ST2[:, 0:1]) * ST2[:, 1:2]
        g2_grad = jnp.sum(d_n2 * flat, axis=0, keepdims=True)
        e = d_n2 * g2
        d_hidden = VCOT[...].astype(f32) + ST2[:, 1:2] * (
            e - jnp.mean(e, axis=-1, keepdims=True) - flat * jnp.mean(e * flat, axis=-1, keepdims=True)
        )
        HID[...] = d_hidden
        DHL[...] = d_hidden.astype(bf16)
        DHLT[...] = d_hidden.T.astype(bf16)
        for i in range(3):
            small_o[27 + i : 28 + i, :] = g2_grad[:, i * 256 : (i + 1) * 256]

    lane_i = lax.broadcasted_iota(jnp.int32, (256, 128), 1)

    def attend_back(m, heads):
        pair = heads[0] == 0
        d_ctx = nn(DHL[...], weight(0, m, 384 if pair else 640, 128))
        if not pair:
            d_ctx = pltpu.roll(d_ctx, 64, 1)
        qms = [head_query(m, h) for h in heads]
        q8 = qms[0] + qms[1] if pair else qms[0]
        vec = memory_vectors(m, heads)
        sil, mean, inv_s, factor, rate = spread_of(m, heads, q8, vec)
        sums = []
        d_ks, d_vs, d_qs, d_mvs = [], [], [], []
        for i, h in enumerate(heads):
            qb, kb, vb, klanes, vlanes, mk0, mv0 = HEADS[h]
            dc = jnp.where(vlanes, d_ctx, 0.0).astype(bf16)
            p = PR[m, h]
            d_p = nt(dc, PK[m, 256:768, vb * 128 : vb * 128 + 128])
            pf = p.astype(f32)
            t = pf * d_p
            d_s = (t - pf * jnp.sum(t, axis=-1, keepdims=True)).astype(bf16)
            d_v = tn(p, dc)
            d_k = tn(d_s, qms[i])
            d_q = jnp.where(klanes, nn(d_s, PK[m, 256:768, kb * 128 : kb * 128 + 128]), 0.0)
            dist, reach = reach_of(i, mean, factor, rate)
            d_r = nt(dc, MEM[m, :, mv0 : mv0 + 128])
            d_mv = tn(reach.astype(bf16), dc)
            t = d_r * reach
            td = t * dist
            sums.append([jnp.sum(v, axis=-1, keepdims=True) for v in (t, td, td * dist)])
            if i == 0:
                TK[0] = d_k
                TK[1] = d_v
                DQ[...] = d_q
                DM[:, 128:256] = d_mv.astype(bf16)
            else:
                TK[0] += d_k
                TK[1] += d_v
                DQ[...] += d_q
                DM[:, 128:256] += d_mv.astype(bf16)
        s0, s1, s2 = (jnp.where(lane_i == 0, sums[0][k], sums[-1][k]) for k in range(3))
        g_mu = -s1 * inv_s * mean * (1.0 - mean)
        g_sg = (s2 * inv_s - s0) * (0.5 * inv_s) * spread_scale * (1.0 / (1.0 + jnp.exp(-sil)))
        used = 2 if pair else 1
        both = jnp.where(lane_i < used, g_mu, 0.0) + pltpu.roll(jnp.where(lane_i < used, g_sg, 0.0), 2, 1)
        grad = both.T[0:8]
        grad_top, grad_rest = split(grad)
        qg = nn(jnp.concatenate([grad_top, grad_rest], axis=1), jnp.concatenate([q8, q8], axis=0))
        own = (((row8 % 2 == 0) & low8) | ((row8 % 2 == 1) & up8)) if pair else up8
        qg_top, qg_rest = split(jnp.where(own, qg, 0.0))
        par = SMP[m].astype(bf16).astype(f32)
        if pair:
            par = jnp.concatenate([par[0:2], par[3:5], jnp.zeros((4, 256), f32)], axis=0)
        else:
            par = jnp.concatenate([par[2:3], par[7:8], par[5:6], par[7:8], jnp.zeros((4, 256), f32)], axis=0)
        par = par.astype(bf16)
        qg_all = jnp.concatenate([qg_top, qg_rest], axis=0)
        DM[:, 0:128] = tn(jnp.concatenate([par, par], axis=0), qg_all).astype(bf16)
        vec_top, vec_rest = split(vec)
        mem_q = tn(
            jnp.concatenate([grad_top, grad_top, grad_rest, jnp.zeros((8, 256), bf16)], axis=0),
            jnp.concatenate([vec_top, vec_rest, vec_top, jnp.zeros((8, 128), bf16)], axis=0),
        )
        mu_sg = nt(qg_all, MEM[m, :, HEADS[heads[0]][5] : HEADS[heads[0]][5] + 128])
        mu_sg = mu_sg[0:8] + mu_sg[8:16]
        for i, h in enumerate(heads):
            small_o[pl.ds(m * 3 + h, 1), :] = mu_sg[i : i + 1]
            small_o[pl.ds(12 + m * 3 + h, 1), :] = mu_sg[2 + i : 3 + i]
        d_q = (DQ[...] + mem_q) * root
        DQ[...] = d_q if pair else pltpu.roll(d_q, 64, 1)
        back = nn(SPT[...], DM[...])
        first = 128 if heads[0] == 0 else 512
        for i in range(2):
            b = back[:, 128 * i : 128 * i + 128]
            cols = slice(first + 128 * i, first + 128 * i + 128)
            PK[m, 0:256, cols] = (b[0:256] * present).astype(bf16)
            PK[m, 256:512, cols] = (TK[i, 0:256] + b[256:512]).astype(bf16)
            now = TK[i, 256:512]
            if heads[0] == 2 and i == 0:
                now = now + DQ[...]
            PK[m, 512:768, cols] = now.astype(bf16)
        if heads[0] == 0:
            PK[m, 0:512, 0:128] = jnp.zeros((512, 128), bf16)
            PK[m, 512:768, 0:128] = DQ[...].astype(bf16)
            PK[m, :, 384:512] = jnp.zeros((768, 128), bf16)

    def grad_square(m, col, wide):
        own = 0 if col == 0 else 128

        val = nn(X0T[...], PK[m, :, col : col + wide])
        out_part = nn(DHLT[...], CTX[m, :, own : own + 128])
        val = jnp.concatenate([val[:, : wide - 128], val[:, wide - 128 :] + out_part], axis=1)
        GA[m // 2, m % 2, :, :, :, col : col + wide] = val.reshape(4, 2, 96, wide).astype(bf16)

    def rows_back(r):
        ACC[...] = jnp.zeros_like(ACC)

        def one(m, carry):
            ACC[...] += nt(PK[m, r * 256 : (r + 1) * 256, :], weight(0, m))
            return carry

        lax.fori_loop(0, 4, one, 0)

    def token_rows(r, first, extra):
        rows_back(r)
        d_n1 = ACC[...]
        rows = slice(first, first + 256)
        inv_1 = ST1[rows, 1:2]
        flat_1 = (VTOK[rows, :].astype(f32) - ST1[rows, 0:1]) * inv_1
        part = jnp.sum(d_n1 * flat_1, axis=0, keepdims=True)
        e = d_n1 * g1
        grad = inv_1 * (
            e - jnp.mean(e, axis=-1, keepdims=True) - flat_1 * jnp.mean(e * flat_1, axis=-1, keepdims=True)
        )
        if extra:
            grad = grad + HID[...]
        X0[256 + first : 512 + first, :] = grad.astype(bf16)
        return part

    def rb0():
        rows_back(0)
        X0[0:256, :] = ACC[...].astype(bf16)

    def tok1():
        part = token_rows(1, 0, False)
        for i in range(3):
            small_o[24 + i : 25 + i, :] = part[:, i * 256 : (i + 1) * 256]

    def tok2():
        part = token_rows(2, 256, True)
        for i in range(3):
            small_o[24 + i : 25 + i, :] = small_o[24 + i : 25 + i, :] + part[:, i * 256 : (i + 1) * 256]
        small_o[30:32, :] = jnp.zeros((2, 256), f32)

    single = {
        PACK: pack, PACKUD: packud, STICKY: sticky, NORM1: norm1, X0_: x0, X0T_: x0t, ATTNOUT: attnout, NORM2: norm2,
        COTT_: cott, OUTS_: outs, NORM2B: norm2b, RB0: rb0, TOK1: tok1, TOK2: tok2,
    }
    looped = {
        PJ1: lambda m: project(m, 0, 384), PJ2: lambda m: project(m, 512, 256),
        MEM1: lambda m: memory(m, 128, 0), MEM2: lambda m: memory(m, 512, 256),
        AT1: lambda m: attend(m, (0, 1)), AT2: lambda m: attend(m, (2,)),
        UP1: lambda m: up(m, 0, 512), UP2: lambda m: up(m, 512, 256),
        GD1: lambda m: grad_down(m, 0, 512), GD2: lambda m: grad_down(m, 512, 256),
        DN1: lambda m: down(m, 0, 512), DN2: lambda m: down(m, 512, 256),
        GU1: lambda m: grad_up(m, 0, 512), GU2: lambda m: grad_up(m, 512, 256), BU: back_up,
        AB1: lambda m: attend_back(m, (0, 1)), AB2: lambda m: attend_back(m, (2,)),
        GS1: lambda m: grad_square(m, 0, 512), GS2: lambda m: grad_square(m, 512, 256),
    }

    def transfer(item):
        if item > 0:
            go(item)
        else:
            got(-item)

    at = 0
    while at < len(SCHEDULE):
        item = SCHEDULE[at]
        at += 1
        if abs(item) > 999:
            transfer(item)
        elif item in single:
            single[item]()
        else:
            if item in (GS1, GS2):
                drain(True)
            between = {}
            done = 0
            while done < 3:
                if abs(SCHEDULE[at]) > 999:
                    between.setdefault(done, []).append(SCHEDULE[at])
                else:
                    done += 1
                at += 1

            def step(m, carry, item=item, between=between):
                looped[item](m)
                for i, items in between.items():

                    @pl.when(m == i)
                    def _(items=items):
                        for one in items:
                            transfer(one)

                return carry

            lax.fori_loop(0, 4, step, 0)
    for group in list(pending):
        drain(group)


def finish_kernel(
    out_b, tg_b, cg_b, wg, sums, out, tg, cg, g1, gq, gk, gv, go, gm, gs, g2, gu, gd,
):
    me = lax.axis_index("mp")
    out[...] = out_b[...]
    tg[...] = tg_b[...].astype(f32)
    cg[...] = cg_b[...].astype(f32)
    for i, ref in enumerate((gq, gk, gv)):
        ref[:, 0:128] = wg[0, :, 128 * i : 128 * i + 128]
        at = 512 + 128 * (i // 2)
        block = wg[0, :, at : at + 128]
        ref[:, 128:192] = block[:, 64 * (i % 2) : 64 * (i % 2) + 64]
    go[0:128, :] = wg[0, :, 384:512].T
    go[128:192, :] = wg[0, :, 640:768].T[64:128, :]
    gu[...] = wg[1]
    gd[...] = wg[2]
    for h in range(3):
        gm[h : h + 1, :] = sums[pl.ds(me * 3 + h, 1), :]
        gs[h : h + 1, :] = sums[pl.ds(12 + me * 3 + h, 1), :]
    for i in range(3):
        g1[pl.ds(i * 256, 256)] = sums[24 + i]
        g2[pl.ds(i * 256, 256)] = sums[27 + i]


def fused_call(*args):
    any_ = pl.BlockSpec(memory_space=pl.ANY)
    vm = pl.BlockSpec(memory_space=pltpu.VMEM)
    sm = pl.BlockSpec(memory_space=pltpu.SMEM)
    V = pltpu.VMEM
    return pl.pallas_call(
        fused_kernel,
        out_shape=(
            jax.ShapeDtypeStruct((4, 64, 768), bf16),
            jax.ShapeDtypeStruct((4, 128, 768), bf16),
            jax.ShapeDtypeStruct((4, 64, 768), bf16),
            jax.ShapeDtypeStruct((3, 96, 768), f32),
            jax.ShapeDtypeStruct((32, 256), f32),
        ),
        in_specs=[any_] * 3 + [vm] * 8 + [sm] + [vm] * 5,
        out_specs=(any_, any_, any_, vm, vm),
        scratch_shapes=[
            V((3, 2, 2, 4, 2, 96, 768), bf16),
            V((2, 2, 2, 4, 2, 96, 768), bf16),
            V((2, 2, 4, 2, 96, 512), bf16),
            V((2, 2, 4, 2, 96, 256), bf16),
            V((7, 32, 256), f32),
            V((3, 32, 256), f32),
            V((512, 768), bf16),
            V((256, 768), bf16),
            V((256, 768), bf16),
            V((768, 768), bf16),
            V((768, 768), bf16),
            V((768, 256), bf16),
            V((256, 768), bf16),
            V((768, 256), bf16),
            V((256, 768), bf16),
            V((768, 256), bf16),
            V((4, 768, 768), bf16),
            V((4, 256, 512), bf16),
            V((4, 3, 256, 512), bf16),
            V((4, 256, 256), bf16),
            V((256, 768), f32),
            V((256, 768), f32),
            V((4, 256, 768), bf16),
            V((4, 256, 768), f32),
            V((4, 8, 256), f32),
            V((2, 512, 128), f32),
            V((256, 128), f32),
            V((256, 256), bf16),
            V((256, 512), bf16),
            V((512, 256), bf16),
            V((256, 768), bf16),
            V((512, 128), f32),
            V((256, 128), f32),
            *(V(scatter_shape(p, j, i), bf16) for p, j, i in SCATTER_KEYS),
            pltpu.SemaphoreType.DMA((PAIRS,)),
            pltpu.SemaphoreType.DMA((PAIRS,)),
            pltpu.SemaphoreType.DMA((LOCALS,)),
        ],
        compiler_params=pltpu.CompilerParams(
            collective_id=0, has_side_effects=True, vmem_limit_bytes=63 * 1024 * 1024
        ),
    )(*args)


def fused_body(
    tokens, coeffs, present_flag, sticky_pos, gain_one, w_query, w_key, w_value, w_out, mu_weight,
    sigma_weight, gain_two, w_up, w_down, cotangent,
):
    _, fitting = basis_tables(NB, SEGMENT_TOKENS)
    fita = jnp.asarray(fitting[:, :SEGMENT_TOKENS])
    past = jnp.asarray(fitting[:, SEGMENT_TOKENS:]).astype(bf16)
    parts = fused_call(
        tokens, coeffs, cotangent, w_query, w_key, w_value, w_out, w_up, w_down.T, mu_weight, sigma_weight,
        present_flag, sticky_pos, gain_one, gain_two, fita, past,
    )

    def like(v):
        return jax.ShapeDtypeStruct(v.shape, f32)

    shapes = (
        jax.ShapeDtypeStruct(cotangent.shape, bf16), like(tokens), like(coeffs), like(gain_one), like(w_query),
        like(w_key), like(w_value), like(w_out), like(mu_weight), like(sigma_weight), like(gain_two), like(w_up),
        like(w_down.T),
    )
    vm = pl.BlockSpec(memory_space=pltpu.VMEM)
    done = pl.pallas_call(
        finish_kernel, out_shape=shapes, in_specs=[vm] * 5, out_specs=(vm,) * 13,
    )(*parts)
    return (*done[:12], done[12].T)


def solution(mesh):
    in_specs = (
        P("dp", "mp", None), P("dp", "mp", None), P("dp"), P("dp", None), P(), P("dp", "mp"), P("dp", "mp"),
        P("dp", "mp"), P("mp", "dp"), P("mp", None), P("mp", None), P(), P("dp", "mp"), P("mp", "dp"),
        P("dp", "mp", None),
    )
    out_specs = (
        P("dp", "mp", None), P("dp", "mp", None), P("dp", "mp", None), P(), P("dp", "mp"), P("dp", "mp"),
        P("dp", "mp"), P("mp", "dp"), P("mp", None), P("mp", None), P(), P("dp", "mp"), P("mp", "dp"),
    )
    whole = body
    if mesh.shape["dp"] == 8 and mesh.shape["mp"] == 4:
        whole = fused_body
    return jax.shard_map(whole, mesh=mesh, in_specs=in_specs, out_specs=out_specs, check_vma=False)
```
